512 devices in a mesh: row: 32 (over z, x_lo), col: 16 (over x_hi, y, core).
Axes of the slice: x: 4 (x_hi: 2, x_lo: 2; x = x_hi * 2 + x_lo), y: 4, z: 16, core: 2. Of those that a mesh axis runs over, the one named last changes fastest.
Arguments:
- stereo_neuron_outputs: bfloat16 [2, 256, 64, 2048], P(None, 'row', None, 'col'), may hold values from -6 to 6
- filter_tap_coefficients: bfloat16 [3, 3, 3, 64, 64], replicated, may hold values from -0.25 to 0.25
- filter_stack_intercepts: float32 [3, 64], replicated, may hold values from -3 to 3
- reference_picture_present: int32 [256, 2048], P('row', 'col'), may hold values 0 or 1
- tile_shift_amounts: int32 [32, 16], P('row', 'col'), may hold values from 0 to 256, as said below
- smoothness_charges: int32 [2], replicated, may hold values from 4 to 96, as said below
Outputs:
- aggregated: float32 [256, 2048, 128], P('row', 'col')
The draws below stay inside these ranges and needn't reach their ends.
Inputs may be any that keep to these rules, and one draw needn't show every extreme that they name: `tile_shift_amounts`: every tile's offset is a whole number of 0 to 256; some tile has exactly 256. smoothness_charges[0] lies in 4 to 16; smoothness_charges[1] is 96.
All inputs are finite; a program needn't handle non-finite values. No bound on the sum of `reference_picture_present` on one device may be relied on, other than what follows from the above.
Results may differ from the reference program's by a relative error of at most 0.006.
Values may be sent and summed in bfloat16 or wider, within the bound.
A program may use at most 64 MiB of HBM per device.

```python
import jax
import jax.numpy as jnp
from jax import lax

CHANNELS = 64
DISPARITIES = 128
LAYERS = 3
TILE_ROWS = 8
TILE_COLS = 128
OFF_MOST = 256
TILES_DOWN = 32
TILES_ACROSS = 16
ROWS = 256
COLS = 2048


def draw_tile_shift_amounts(key, part):
    first_key, second_key = jax.random.split(key)
    values = jax.random.randint(first_key, (TILES_DOWN, TILES_ACROSS), 0, OFF_MOST + 1)
    chosen = jax.random.randint(second_key, (), 0, TILES_DOWN * TILES_ACROSS)
    places = jnp.arange(TILES_DOWN * TILES_ACROSS).reshape(TILES_DOWN, TILES_ACROSS)
    return jnp.where(places == chosen, OFF_MOST, values).astype(jnp.int32)


def draw_smoothness_charges(key, part):
    first_key = jax.random.fold_in(key, 11)
    small_pen = jax.random.randint(first_key, (), 4, 17)
    large_pen = jnp.full((), 96, jnp.int32)
    return jnp.stack([small_pen.astype(jnp.int32), large_pen]).astype(jnp.int32)


def place_ends(array, rng, low, high):
    spot = [jax.random.randint(jax.random.fold_in(rng, axis), (), 0, length) for axis, length in enumerate(array.shape)]
    longest = array.shape.index(max(array.shape))
    next_to = spot[:longest] + [(spot[longest] + 1) % array.shape[longest]] + spot[longest + 1:]
    return array.at[tuple(spot)].set(low).at[tuple(next_to)].set(high)


def block_scale(own_key, dims, cuts, smallest, largest):
    def one(dim, blocks):
        heights = jax.random.uniform(jax.random.fold_in(jax.random.fold_in(own_key, 6), dim), (blocks,), jnp.float32, smallest / len(cuts), largest / len(cuts))
        return jnp.repeat(jnp.exp(heights), dims[dim] // blocks).reshape((-1,) + (1,) * (len(dims) - dim - 1))

    factor_of = one(*cuts[0])
    for cut in cuts[1:]:
        factor_of = factor_of * one(*cut)
    return factor_of


def centred(key, dims, deviation, most, cuts=(), kind=jnp.bfloat16):
    factor_of = block_scale(key, dims, cuts, -0.22, 0.18) if cuts else 1.0
    entries = jax.random.normal(key, dims, jnp.float32) * deviation * factor_of
    return jnp.minimum(jnp.maximum(entries, -most), most).astype(kind)


def setup_inputs(seed: int = 0) -> dict:
    key_list = jax.random.split(jax.random.key(seed), 7)
    stereo_neuron_outputs = centred(key_list[0], (2, ROWS, CHANNELS, COLS), 1.0, 6.0, ((1, 32), (3, 16)))
    filter_tap_coefficients = centred(key_list[1], (LAYERS, 3, 3, CHANNELS, CHANNELS), (9 * CHANNELS) ** -0.5, 0.25)
    filter_stack_intercepts = centred(key_list[2], (LAYERS, CHANNELS), 0.5, 3.0, (), jnp.float32)
    reference_picture_present = place_ends((jax.random.randint(key_list[3], (ROWS, COLS), 0, 8) < 7).astype(jnp.int32), jax.random.fold_in(key_list[3], 1), 0, 1)
    tile_shift_amounts = draw_tile_shift_amounts(jax.random.fold_in(key_list[6], 71), 0)
    smoothness_charges = draw_smoothness_charges(jax.random.fold_in(key_list[6], 71), 0)
    return dict(stereo_neuron_outputs=stereo_neuron_outputs, filter_tap_coefficients=filter_tap_coefficients, filter_stack_intercepts=filter_stack_intercepts, reference_picture_present=reference_picture_present, tile_shift_amounts=tile_shift_amounts, smoothness_charges=smoothness_charges)


def advance(state, cost_row, gentle_change_charge, steep_change_charge):
    least = lax.optimization_barrier(jnp.min(state, axis=-1, keepdims=True))
    barrier = jnp.full(state.shape[:-1] + (1,), jnp.inf, state.dtype)
    lower = jnp.concatenate([barrier, state[..., :-1]], axis=-1)
    upper = jnp.concatenate([state[..., 1:], barrier], axis=-1)
    best = jnp.minimum(jnp.minimum(state, jnp.minimum(lower, upper) + gentle_change_charge), least + steep_change_charge)
    return cost_row + best - least

def sweep(costs, incoming, gentle_change_charge, steep_change_charge, backward):

    def stepper(state, cost_row):
        fresh = advance(state, cost_row, gentle_change_charge, steep_change_charge)
        return (fresh, fresh)
    return lax.scan(stepper, incoming, costs, reverse=backward)

def one_image(image, filter_tap_coefficients, filter_stack_intercepts):
    hidden = image[None]
    features = None
    for layer_number in range(LAYERS):
        summed = lax.conv_general_dilated(hidden.astype(jnp.float32), filter_tap_coefficients[layer_number].astype(jnp.float32), (1, 1), 'SAME', dimension_numbers=('NHCW', 'HWOI', 'NHCW'), precision=lax.Precision.HIGHEST)
        summed = summed + filter_stack_intercepts[layer_number][None, None, :, None]
        if layer_number < LAYERS - 1:
            hidden = jnp.maximum(summed, 0.0).astype(jnp.bfloat16)
        else:
            features = summed
    features = features[0]
    scale = lax.rsqrt(lax.optimization_barrier(jnp.sum(features * features, axis=1, keepdims=True)) + 1e-06)
    return (features * scale).astype(jnp.bfloat16)

def reference(stereo_neuron_outputs, filter_tap_coefficients, filter_stack_intercepts, reference_picture_present, tile_shift_amounts, smoothness_charges):
    unit = lax.map(lambda image: one_image(image, filter_tap_coefficients, filter_stack_intercepts), stereo_neuron_outputs)
    shift_map = jnp.repeat(jnp.repeat(tile_shift_amounts, TILE_ROWS, axis=0), TILE_COLS, axis=1).astype(jnp.int32)
    columns = jnp.arange(COLS, dtype=jnp.int32)
    levels = jnp.arange(DISPARITIES, dtype=jnp.int32)

    def row_cost(items):
        left_row, right_row, disparity_offset_row, valid_row = items
        source = columns[:, None] - disparity_offset_row[:, None] - levels[None, :]
        inside = source >= 0
        taken = right_row.astype(jnp.float32)[:, jnp.maximum(source, 0)]
        taken = jnp.where(inside[None], taken, 0.0)
        similar = lax.optimization_barrier(jnp.sum(left_row.astype(jnp.float32)[:, :, None] * taken, axis=0))
        return jnp.where(valid_row[:, None] == 1, 1.0 - similar, 1.0)
    cost = lax.map(row_cost, (unit[0], unit[1], shift_map, reference_picture_present))
    gentle_change_charge = smoothness_charges[0].astype(jnp.float32) / 64.0
    steep_change_charge = smoothness_charges[1].astype(jnp.float32) / 64.0
    start_cols = jnp.zeros((COLS, DISPARITIES), jnp.float32)
    final_down, down_layers = sweep(cost, start_cols, gentle_change_charge, steep_change_charge, False)
    final_up, up_layers = sweep(cost, start_cols, gentle_change_charge, steep_change_charge, True)
    vertical = down_layers + up_layers
    across = jnp.swapaxes(cost, 0, 1)
    start_rows = jnp.zeros((ROWS, DISPARITIES), jnp.float32)
    final_right, right_layers = sweep(across, start_rows, gentle_change_charge, steep_change_charge, False)
    final_left, left_layers = sweep(across, start_rows, gentle_change_charge, steep_change_charge, True)
    horizontal = right_layers + left_layers
    return vertical + jnp.swapaxes(horizontal, 0, 1)
```

```python
import functools

import jax
import jax.numpy as jnp
from jax import lax
from jax.experimental import pallas as pl
from jax.experimental.pallas import tpu as pltpu
from jax.sharding import PartitionSpec as P

DISPARITIES = 128
SUB = 8
PARTS = DISPARITIES // SUB
MESH = pl.DeviceIdType.MESH


def from_behind(block, axis, distance):
    devices = range(lax.axis_size(axis))
    route = [(i - distance, i) for i in devices if i - distance in devices]
    return lax.ppermute(block, axis, route)


def extended_2(value, sides, width):
    for axis, dim in sides:
        count, length = (lax.axis_size(axis), value.shape[dim])
        up = [(i, (i + 1) % count) for i in range(count - 1)]
        down = [(j, i) for i, j in up]
        last = lax.slice_in_dim(value, length - width, length, axis=dim)
        first = lax.slice_in_dim(value, 0, width, axis=dim)
        before = lax.ppermute(last, axis, up)
        after = lax.ppermute(first, axis, down)
        value = jnp.concatenate([before, value, after], axis=dim)
    return value


def lane_order():
    lane = lax.broadcasted_iota(jnp.int32, (SUB, DISPARITIES), 1)
    return (lane % SUB) * PARTS + lane // SUB


def lane_order_back():
    lane = lax.broadcasted_iota(jnp.int32, (SUB, DISPARITIES), 1)
    return (lane % PARTS) * SUB + lane // PARTS


def pieces_of(value):
    return [value[v * SUB : (v + 1) * SUB] for v in range(PARTS)]


def smallest(state):
    level = list(state)
    while len(level) > 1:
        level = [jnp.minimum(level[2 * i], level[2 * i + 1]) for i in range(len(level) // 2)]
    least = level[0]
    for step in (4, 2, 1):
        least = jnp.minimum(least, pltpu.roll(least, step, 0))
    return least


def step_once(state, cost, p1, p2, first_sub, last_sub):
    lifted = [s + p1 for s in state]
    below = jnp.where(first_sub, jnp.inf, pltpu.roll(lifted[-1], 1, 0))
    above = jnp.where(last_sub, jnp.inf, pltpu.roll(lifted[0], SUB - 1, 0))
    near = [below] + lifted + [above]
    jump = smallest(state) + p2
    return [
        cost[v]
        + jnp.minimum(jnp.minimum(state[v], jnp.minimum(near[v], near[v + 2])), jump)
        for v in range(PARTS)
    ]


def walk(slots, out, count, state, charges, at):
    sub = lax.broadcasted_iota(jnp.int32, (SUB, SUB), 0)
    first_sub, last_sub = sub == 0, sub == SUB - 1
    p1 = charges[0].astype(jnp.float32) / 64.0
    p2 = charges[1].astype(jnp.float32) / 64.0

    def body(turn, state):
        state = list(state)
        for k in range(8):
            t = at(turn * 8 + k)
            state = step_once(state, pieces_of(slots[t]), p1, p2, first_sub, last_sub)
            for v in range(PARTS):
                out[t, v * SUB : (v + 1) * SUB, :] = state[v]
        return tuple(state)

    return list(lax.fori_loop(0, count // 8, body, tuple(state)))


def turn_in(source, slots, count):
    order = lane_order()

    def body(turn, _):
        for k in range(8):
            t = turn * 8 + k
            slots[t] = jnp.take_along_axis(source[t], order, axis=1).T
        return 0

    lax.fori_loop(0, count // 8, body, 0)


def vertical_kernel(source, charges, out, slots):
    count = source.shape[0]
    turn_in(source, slots, count)
    zero = [jnp.zeros((SUB, SUB), jnp.float32) for _ in range(PARTS)]
    walk(slots, slots, count, zero, charges, lambda t: t)
    back = lane_order_back()

    def body(turn, least):
        for k in range(8):
            t = turn * 8 + k
            value = slots[t].T
            out[t] = jnp.take_along_axis(value - least, back, axis=1)
            least = jnp.min(value, axis=1, keepdims=True)
        return least

    lax.fori_loop(0, count // 8, body, jnp.zeros((SUB, 1), jnp.float32))


def vertical_call(source, charges):
    count = source.shape[0]
    return pl.pallas_call(
        vertical_kernel,
        out_shape=jax.ShapeDtypeStruct(source.shape, jnp.float32),
        in_specs=[
            pl.BlockSpec(memory_space=pltpu.VMEM),
            pl.BlockSpec(memory_space=pltpu.SMEM),
        ],
        out_specs=pl.BlockSpec(memory_space=pltpu.VMEM),
        scratch_shapes=[pltpu.VMEM((count, DISPARITIES, SUB), jnp.float32)],
        name="vertical_paths",
    )(source, charges)


def horizontal_kernel(
    size, source, charges, out, slots, walked, edge_out, edge_in, send_sem, recv_sem
):
    count = source.shape[0]
    me = lax.axis_index("col")
    barrier = pltpu.get_barrier_semaphore()

    @pl.when(me > 0)
    def _():
        pl.semaphore_signal(barrier, inc=1, device_id={"col": me - 1}, device_id_type=MESH)

    @pl.when(me < size - 1)
    def _():
        pl.semaphore_signal(barrier, inc=1, device_id={"col": me + 1}, device_id_type=MESH)

    neighbours = jnp.where(me > 0, 1, 0) + jnp.where(me < size - 1, 1, 0)
    pl.semaphore_wait(barrier, neighbours)

    turn_in(source, slots, count)
    back = lane_order_back()

    def one_direction(way, first):
        starts = me == (0 if way == 0 else size - 1)
        ends = me == (size - 1 if way == 0 else 0)
        toward = me + 1 if way == 0 else me - 1
        at = (lambda t: t) if way == 0 else (lambda t: count - 1 - t)

        def copy():
            return pltpu.make_async_remote_copy(
                src_ref=edge_out.at[way],
                dst_ref=edge_in.at[way],
                send_sem=send_sem.at[way],
                recv_sem=recv_sem.at[way],
                device_id={"col": toward},
                device_id_type=MESH,
            )

        @pl.when(starts)
        def _():
            edge_in[way] = jnp.zeros((SUB, DISPARITIES), jnp.float32)

        @pl.when(jnp.logical_not(starts))
        def _():
            copy().wait_recv()

        edge = edge_in[way]
        state = walk(slots, walked, count, pieces_of(edge.T), charges, at)
        last = jnp.concatenate(state, axis=0).T

        @pl.when(jnp.logical_not(ends))
        def _():
            edge_out[way] = last - jnp.min(last, axis=1, keepdims=True)
            copy().start()

        def body(turn, least):
            for k in range(8):
                t = at(turn * 8 + k)
                value = walked[t].T
                result = jnp.take_along_axis(value - least, back, axis=1)
                out[t] = result if first else out[t] + result
                least = jnp.min(value, axis=1, keepdims=True)
            return least

        lax.fori_loop(0, count // 8, body, jnp.min(edge, axis=1, keepdims=True))

        @pl.when(jnp.logical_not(ends))
        def _():
            copy().wait_send()

    @pl.when(me < size // 2)
    def _():
        one_direction(0, True)
        one_direction(1, False)

    @pl.when(me >= size // 2)
    def _():
        one_direction(1, True)
        one_direction(0, False)


def horizontal_call(source, charges):
    count = source.shape[0]
    size = lax.axis_size("col")
    return pl.pallas_call(
        functools.partial(horizontal_kernel, size),
        out_shape=jax.ShapeDtypeStruct(source.shape, jnp.float32),
        in_specs=[
            pl.BlockSpec(memory_space=pltpu.VMEM),
            pl.BlockSpec(memory_space=pltpu.SMEM),
        ],
        out_specs=pl.BlockSpec(memory_space=pltpu.VMEM),
        scratch_shapes=[
            pltpu.VMEM((count, DISPARITIES, SUB), jnp.float32),
            pltpu.VMEM((count, DISPARITIES, SUB), jnp.float32),
            pltpu.VMEM((2, SUB, DISPARITIES), jnp.float32),
            pltpu.VMEM((2, SUB, DISPARITIES), jnp.float32),
            pltpu.SemaphoreType.DMA((2,)),
            pltpu.SemaphoreType.DMA((2,)),
        ],
        compiler_params=pltpu.CompilerParams(collective_id=0, has_side_effects=True),
        name="horizontal_paths",
    )(source, charges)


def conv_stack(stereo_neuron_outputs, filter_tap_coefficients, filter_stack_intercepts):
    layers_total = filter_tap_coefficients.shape[0]
    rows_here = stereo_neuron_outputs.shape[1]
    cols_here = stereo_neuron_outputs.shape[3]
    hidden = extended_2(stereo_neuron_outputs, (("row", 1), ("col", 3)), layers_total)
    row_start = lax.axis_index("row") * rows_here
    col_start = lax.axis_index("col") * cols_here
    row_limit = lax.axis_size("row") * rows_here
    col_limit = lax.axis_size("col") * cols_here
    features = None
    for layer_number in range(layers_total):
        margin = layers_total - 1 - layer_number
        out_rows = rows_here + 2 * margin
        out_cols = cols_here + 2 * margin
        summed = None
        for tap_row in range(3):
            for tap_col in range(3):
                window = hidden[:, tap_row : tap_row + out_rows, :, tap_col : tap_col + out_cols]
                term = jnp.einsum(
                    "oc,iycx->iyox",
                    filter_tap_coefficients[layer_number, tap_row, tap_col],
                    window,
                    preferred_element_type=jnp.float32,
                )
                summed = term if summed is None else summed + term
        summed = summed + filter_stack_intercepts[layer_number][None, None, :, None]
        if layer_number < layers_total - 1:
            global_rows = row_start - margin + jnp.arange(out_rows, dtype=jnp.int32)
            global_cols = col_start - margin + jnp.arange(out_cols, dtype=jnp.int32)
            keep_rows = jnp.logical_and(global_rows >= 0, global_rows < row_limit)
            keep_cols = jnp.logical_and(global_cols >= 0, global_cols < col_limit)
            keeper = jnp.logical_and(keep_rows[None, :, None, None], keep_cols[None, None, None, :])
            hidden = jnp.where(keeper, jnp.maximum(summed, 0.0), 0.0).astype(jnp.bfloat16)
        else:
            features = summed
    scale = lax.rsqrt(jnp.sum(features * features, axis=2, keepdims=True) + 1e-06)
    return (features * scale).astype(jnp.bfloat16)


def per_device(
    stereo_neuron_outputs,
    filter_tap_coefficients,
    filter_stack_intercepts,
    reference_picture_present,
    tile_shift_amounts,
    smoothness_charges,
):
    unit = conv_stack(stereo_neuron_outputs, filter_tap_coefficients, filter_stack_intercepts)
    left_unit = unit[0]
    right_normalized_features = unit[1]
    rows_here = left_unit.shape[0]
    cols_here = left_unit.shape[2]
    reach = (3 * cols_here + DISPARITIES - 2) // cols_here
    tile_offset = tile_shift_amounts[0, 0]
    pieces = [
        from_behind(right_normalized_features, "col", distance) for distance in range(reach, 0, -1)
    ]
    extended = jnp.concatenate(pieces + [right_normalized_features], axis=2)
    strip_start = reach * cols_here - tile_offset - (DISPARITIES - 1)
    strip = lax.dynamic_slice_in_dim(extended, strip_start, cols_here + DISPARITIES - 1, 2)
    product = jnp.einsum("ycj,yck->yjk", left_unit, strip, preferred_element_type=jnp.float32)
    padded = jnp.pad(product, ((0, 0), (0, 0), (0, 1)))
    flat = padded.reshape(rows_here, cols_here * (cols_here + DISPARITIES))
    flat = jnp.pad(flat, ((0, 0), (0, cols_here)))
    skewed = flat.reshape(rows_here, cols_here, cols_here + DISPARITIES + 1)[:, :, :DISPARITIES]
    similarity = skewed[:, :, ::-1]
    cost = jnp.where(reference_picture_present[:, :, None] == 1, 1.0 - similarity, 1.0)
    horizontal = horizontal_call(jnp.swapaxes(cost, 0, 1), smoothness_charges)
    strip = lax.all_to_all(
        cost.astype(jnp.bfloat16), "row", split_axis=1, concat_axis=0, tiled=True
    ).astype(jnp.float32)
    width = strip.shape[1]
    both = vertical_call(jnp.concatenate([strip, strip[::-1]], axis=1), smoothness_charges)
    vertical = (both[:, :width] + both[::-1, width:]).astype(jnp.bfloat16)
    vertical = lax.all_to_all(vertical, "row", split_axis=0, concat_axis=1, tiled=True)
    return vertical.astype(jnp.float32) + jnp.swapaxes(horizontal, 0, 1)


def solution(mesh):
    return jax.shard_map(
        per_device,
        mesh=mesh,
        in_specs=(P(None, "row", None, "col"), P(), P(), P("row", "col"), P("row", "col"), P()),
        out_specs=P("row", "col", None),
        check_vma=False,
    )
```

```python
import functools

import jax
import jax.numpy as jnp
from jax import lax
from jax.experimental import pallas as pl
from jax.experimental.pallas import tpu as pltpu
from jax.sharding import PartitionSpec as P

DISPARITIES = 128
SUB = 8
PARTS = DISPARITIES // SUB
MESH = pl.DeviceIdType.MESH


def from_behind(block, axis, distance):
    devices = range(lax.axis_size(axis))
    route = [(i - distance, i) for i in devices if i - distance in devices]
    return lax.ppermute(block, axis, route)


def extended_2(value, sides, width):
    for axis, dim in sides:
        count, length = (lax.axis_size(axis), value.shape[dim])
        up = [(i, (i + 1) % count) for i in range(count - 1)]
        down = [(j, i) for i, j in up]
        last = lax.slice_in_dim(value, length - width, length, axis=dim)
        first = lax.slice_in_dim(value, 0, width, axis=dim)
        before = lax.ppermute(last, axis, up)
        after = lax.ppermute(first, axis, down)
        value = jnp.concatenate([before, value, after], axis=dim)
    return value


def lane_order():
    lane = lax.broadcasted_iota(jnp.int32, (SUB, DISPARITIES), 1)
    return (lane % SUB) * PARTS + lane // SUB


def lane_order_back():
    lane = lax.broadcasted_iota(jnp.int32, (SUB, DISPARITIES), 1)
    return (lane % PARTS) * SUB + lane // PARTS


def pieces_of(value):
    return [value[v * SUB : (v + 1) * SUB] for v in range(PARTS)]


def smallest(state):
    level = list(state)
    while len(level) > 1:
        level = [jnp.minimum(level[2 * i], level[2 * i + 1]) for i in range(len(level) // 2)]
    least = level[0]
    for step in (4, 2, 1):
        least = jnp.minimum(least, pltpu.roll(least, step, 0))
    return least


def step_once(state, cost, p1, p2, first_sub, last_sub):
    lifted = [s + p1 for s in state]
    below = jnp.where(first_sub, jnp.inf, pltpu.roll(lifted[-1], 1, 0))
    above = jnp.where(last_sub, jnp.inf, pltpu.roll(lifted[0], SUB - 1, 0))
    near = [below] + lifted + [above]
    jump = smallest(state) + p2
    return [
        cost[v]
        + jnp.minimum(jnp.minimum(state[v], jnp.minimum(near[v], near[v + 2])), jump)
        for v in range(PARTS)
    ]


def walk(slots, out, count, state, charges, at):
    sub = lax.broadcasted_iota(jnp.int32, (SUB, SUB), 0)
    first_sub, last_sub = sub == 0, sub == SUB - 1
    p1 = charges[0].astype(jnp.float32) / 64.0
    p2 = charges[1].astype(jnp.float32) / 64.0

    def body(turn, state):
        state = list(state)
        for k in range(8):
            t = at(turn * 8 + k)
            state = step_once(state, pieces_of(slots[t]), p1, p2, first_sub, last_sub)
            for v in range(PARTS):
                out[t, v * SUB : (v + 1) * SUB, :] = state[v]
        return tuple(state)

    return list(lax.fori_loop(0, count // 8, body, tuple(state)))


def turn_in(piece, slots, count):
    order = lane_order()

    def body(turn, _):
        for k in range(16):
            t = turn * 16 + k
            slots[t] = jnp.take_along_axis(piece(t), order, axis=1).T
        return 0

    lax.fori_loop(0, count // 16, body, 0)


def half_turn(value):
    return pltpu.roll(value, SUB // 2, 0)


def paths_kernel(
    row_size,
    col_size,
    cost,
    charges,
    out_across,
    out_down,
    slots,
    walked,
    strips,
    edge_out,
    edge_in,
    sent,
    came,
    back_out,
    back_in,
    edge_send,
    edge_recv,
    sent_sem,
    came_sem,
    back_send,
    back_recv,
):
    count = out_across.shape[0]
    height = strips.shape[0]
    row = lax.axis_index("row")
    me = lax.axis_index("col")
    low = lax.broadcasted_iota(jnp.int32, (SUB, DISPARITIES), 0) < SUB // 2
    back = lane_order_back()

    barrier = pltpu.get_barrier_semaphore()

    @pl.when(me > 0)
    def _():
        pl.semaphore_signal(barrier, inc=1, device_id={"col": me - 1}, device_id_type=MESH)

    @pl.when(me < col_size - 1)
    def _():
        pl.semaphore_signal(barrier, inc=1, device_id={"col": me + 1}, device_id_type=MESH)

    def greet(j, _):
        peer = lax.rem(row + j, row_size)
        pl.semaphore_signal(barrier, inc=1, device_id={"row": peer}, device_id_type=MESH)
        return 0

    lax.fori_loop(1, row_size, greet, 0)

    def exchange(source, target, send_sem, recv_sem, what):
        def copy(mine, slot):
            return pltpu.make_async_remote_copy(
                src_ref=source.at[mine],
                dst_ref=target.at[slot],
                send_sem=send_sem.at[mine],
                recv_sem=recv_sem.at[slot],
                device_id={"row": mine},
                device_id_type=MESH,
            )

        def body(j, _):
            peer = lax.rem(row + j, row_size)
            if what == "start":
                copy(peer, row).start()
            elif what == "sent":
                copy(peer, row).wait_send()
            else:
                copy(peer, peer).wait_recv()
            return 0

        lax.fori_loop(1, row_size, body, 0)
        if what == "start":
            target[row] = source[row]

    def cut(tile, _):
        start = pl.multiple_of(tile * SUB, SUB)
        rows = [cost[y, pl.ds(start, SUB), :] for y in range(SUB)]
        even = [jnp.where(low, rows[y], half_turn(rows[y + 1])) for y in range(0, SUB, 2)]
        odd = [jnp.where(low, half_turn(rows[y]), rows[y + 1]) for y in range(0, SUB, 2)]
        sent[2 * tile] = jnp.concatenate(even, axis=0).astype(jnp.bfloat16)
        sent[2 * tile + 1] = jnp.concatenate(odd, axis=0).astype(jnp.bfloat16)
        return 0

    lax.fori_loop(0, row_size // 2, cut, 0)
    neighbours = jnp.where(me > 0, 1, 0) + jnp.where(me < col_size - 1, 1, 0)
    pl.semaphore_wait(barrier, neighbours + row_size - 1)
    exchange(sent, came, sent_sem, came_sem, "start")
    turn_in(lambda x: cost[:, x, :], slots, count)

    def vertical_in():
        exchange(sent, came, sent_sem, came_sem, "came")
        order = lane_order()

        def body(source, _):
            near = came[source].astype(jnp.float32)
            far = came[row_size - 1 - source].astype(jnp.float32)
            for q in range(SUB // 2):
                a = near[q * SUB : (q + 1) * SUB]
                b = far[(3 - q) * SUB : (4 - q) * SUB]
                first = jnp.where(low, a, b)
                second = half_turn(jnp.where(low, b, a))
                t = source * SUB + 2 * q
                strips[t] = jnp.take_along_axis(first, order, axis=1).T
                strips[t + 1] = jnp.take_along_axis(second, order, axis=1).T
            return 0

        lax.fori_loop(0, row_size, body, 0)

    def vertical_walk():
        zero = [jnp.zeros((SUB, SUB), jnp.float32) for _ in range(PARTS)]
        walk(strips, strips, height, zero, charges, lambda t: t)

    def vertical_out():
        def layers(start):
            before = strips[jnp.maximum(start - 1, 0)].T
            least = jnp.min(before, axis=1, keepdims=True)
            least = jnp.where(start == 0, 0.0, least)
            found = []
            for y in range(SUB):
                value = strips[start + y].T
                found.append(value - least)
                least = jnp.min(value, axis=1, keepdims=True)
            return found

        def body(near, _):
            far = row_size - 1 - near
            one = layers(near * SUB)
            other = layers(far * SUB)
            total = [
                jnp.take_along_axis(one[y] + half_turn(other[SUB - 1 - y]), back, axis=1)
                for y in range(SUB)
            ]
            up = [jnp.where(low, total[y], half_turn(total[y + 1])) for y in (0, 2, 4, 6)]
            down = [jnp.where(low, half_turn(total[y + 1]), total[y]) for y in (6, 4, 2, 0)]
            back_out[near] = jnp.concatenate(up, axis=0).astype(jnp.bfloat16)
            back_out[far] = jnp.concatenate(down, axis=0).astype(jnp.bfloat16)
            return 0

        lax.fori_loop(0, row_size // 2, body, 0)
        exchange(back_out, back_in, back_send, back_recv, "start")

    def one_direction(way, first):
        starts = me == (0 if way == 0 else col_size - 1)
        ends = me == (col_size - 1 if way == 0 else 0)
        toward = me + 1 if way == 0 else me - 1
        at = (lambda t: t) if way == 0 else (lambda t: count - 1 - t)

        def copy():
            return pltpu.make_async_remote_copy(
                src_ref=edge_out.at[way],
                dst_ref=edge_in.at[way],
                send_sem=edge_send.at[way],
                recv_sem=edge_recv.at[way],
                device_id={"col": toward},
                device_id_type=MESH,
            )

        @pl.when(starts)
        def _():
            edge_in[way] = jnp.zeros((SUB, DISPARITIES), jnp.float32)

        @pl.when(jnp.logical_not(starts))
        def _():
            copy().wait_recv()

        edge = edge_in[way]
        state = walk(slots, walked, count, pieces_of(edge.T), charges, at)
        last = jnp.concatenate(state, axis=0).T

        @pl.when(jnp.logical_not(ends))
        def _():
            edge_out[way] = last - jnp.min(last, axis=1, keepdims=True)
            copy().start()

        def body(turn, least):
            for k in range(16):
                t = at(turn * 16 + k)
                value = walked[t].T
                result = jnp.take_along_axis(value - least, back, axis=1)
                out_across[t] = result if first else out_across[t] + result
                least = jnp.min(value, axis=1, keepdims=True)
            return least

        lax.fori_loop(0, count // 16, body, jnp.min(edge, axis=1, keepdims=True))

        @pl.when(jnp.logical_not(ends))
        def _():
            copy().wait_send()

    place = jnp.minimum(me, col_size - 1 - me)
    pieces = ((vertical_in, 3), (vertical_walk, 5), (vertical_out, 6))
    for piece, threshold in pieces:
        pl.when(place >= threshold)(piece)

    @pl.when(me < col_size // 2)
    def _():
        one_direction(0, True)

    @pl.when(me >= col_size // 2)
    def _():
        one_direction(1, True)

    for piece, threshold in pieces:
        pl.when(place < threshold)(piece)

    @pl.when(me < col_size // 2)
    def _():
        one_direction(1, False)

    @pl.when(me >= col_size // 2)
    def _():
        one_direction(0, False)

    exchange(back_out, back_in, back_send, back_recv, "came")

    def hand_over(j, _):
        out_down[j] = back_in[j]
        return 0

    lax.fori_loop(0, row_size, hand_over, 0)
    exchange(sent, came, sent_sem, came_sem, "sent")
    exchange(back_out, back_in, back_send, back_recv, "sent")


def paths_call(cost, charges):
    rows, count, _ = cost.shape
    row_size, col_size = lax.axis_size("row"), lax.axis_size("col")
    width = count // row_size
    block = (row_size, rows * width, DISPARITIES)
    vmem = pl.BlockSpec(memory_space=pltpu.VMEM)
    return pl.pallas_call(
        functools.partial(paths_kernel, row_size, col_size),
        out_shape=(
            jax.ShapeDtypeStruct((count, rows, DISPARITIES), jnp.float32),
            jax.ShapeDtypeStruct(block, jnp.bfloat16),
        ),
        in_specs=[vmem, pl.BlockSpec(memory_space=pltpu.SMEM)],
        out_specs=(vmem, vmem),
        scratch_shapes=[
            pltpu.VMEM((count, DISPARITIES, SUB), jnp.float32),
            pltpu.VMEM((count, DISPARITIES, SUB), jnp.float32),
            pltpu.VMEM((rows * row_size, DISPARITIES, SUB), jnp.float32),
            pltpu.VMEM((2, SUB, DISPARITIES), jnp.float32),
            pltpu.VMEM((2, SUB, DISPARITIES), jnp.float32),
            pltpu.VMEM(block, jnp.bfloat16),
            pltpu.VMEM(block, jnp.bfloat16),
            pltpu.VMEM(block, jnp.bfloat16),
            pltpu.VMEM(block, jnp.bfloat16),
            pltpu.SemaphoreType.DMA((2,)),
            pltpu.SemaphoreType.DMA((2,)),
            pltpu.SemaphoreType.DMA((row_size,)),
            pltpu.SemaphoreType.DMA((row_size,)),
            pltpu.SemaphoreType.DMA((row_size,)),
            pltpu.SemaphoreType.DMA((row_size,)),
        ],
        compiler_params=pltpu.CompilerParams(
            collective_id=0, has_side_effects=True, vmem_limit_bytes=60 * 1024 * 1024
        ),
        name="four_paths",
    )(cost, charges)


def conv_stack(stereo_neuron_outputs, filter_tap_coefficients, filter_stack_intercepts):
    layers_total = filter_tap_coefficients.shape[0]
    rows_here = stereo_neuron_outputs.shape[1]
    cols_here = stereo_neuron_outputs.shape[3]
    hidden = extended_2(stereo_neuron_outputs, (("row", 1), ("col", 3)), layers_total)
    row_start = lax.axis_index("row") * rows_here
    col_start = lax.axis_index("col") * cols_here
    row_limit = lax.axis_size("row") * rows_here
    col_limit = lax.axis_size("col") * cols_here
    features = None
    for layer_number in range(layers_total):
        margin = layers_total - 1 - layer_number
        out_rows = rows_here + 2 * margin
        out_cols = cols_here + 2 * margin
        summed = None
        for tap_row in range(3):
            for tap_col in range(3):
                window = hidden[:, tap_row : tap_row + out_rows, :, tap_col : tap_col + out_cols]
                term = jnp.einsum(
                    "oc,iycx->iyox",
                    filter_tap_coefficients[layer_number, tap_row, tap_col],
                    window,
                    preferred_element_type=jnp.float32,
                )
                summed = term if summed is None else summed + term
        summed = summed + filter_stack_intercepts[layer_number][None, None, :, None]
        if layer_number < layers_total - 1:
            global_rows = row_start - margin + jnp.arange(out_rows, dtype=jnp.int32)
            global_cols = col_start - margin + jnp.arange(out_cols, dtype=jnp.int32)
            keep_rows = jnp.logical_and(global_rows >= 0, global_rows < row_limit)
            keep_cols = jnp.logical_and(global_cols >= 0, global_cols < col_limit)
            keeper = jnp.logical_and(keep_rows[None, :, None, None], keep_cols[None, None, None, :])
            hidden = jnp.where(keeper, jnp.maximum(summed, 0.0), 0.0).astype(jnp.bfloat16)
        else:
            features = summed
    scale = lax.rsqrt(jnp.sum(features * features, axis=2, keepdims=True) + 1e-06)
    return (features * scale).astype(jnp.bfloat16)


def per_device(
    stereo_neuron_outputs,
    filter_tap_coefficients,
    filter_stack_intercepts,
    reference_picture_present,
    tile_shift_amounts,
    smoothness_charges,
):
    unit = conv_stack(stereo_neuron_outputs, filter_tap_coefficients, filter_stack_intercepts)
    left_unit = unit[0]
    right_normalized_features = unit[1]
    rows_here = left_unit.shape[0]
    cols_here = left_unit.shape[2]
    reach = (3 * cols_here + DISPARITIES - 2) // cols_here
    tile_offset = tile_shift_amounts[0, 0]
    pieces = [
        from_behind(right_normalized_features, "col", distance) for distance in range(reach, 0, -1)
    ]
    extended = jnp.concatenate(pieces + [right_normalized_features], axis=2)
    strip_start = reach * cols_here - tile_offset - (DISPARITIES - 1)
    strip = lax.dynamic_slice_in_dim(extended, strip_start, cols_here + DISPARITIES - 1, 2)
    product = jnp.einsum("ycj,yck->yjk", left_unit, strip, preferred_element_type=jnp.float32)
    padded = jnp.pad(product, ((0, 0), (0, 0), (0, 1)))
    flat = padded.reshape(rows_here, cols_here * (cols_here + DISPARITIES))
    flat = jnp.pad(flat, ((0, 0), (0, cols_here)))
    skewed = flat.reshape(rows_here, cols_here, cols_here + DISPARITIES + 1)[:, :, :DISPARITIES]
    similarity = skewed[:, :, ::-1]
    cost = jnp.where(reference_picture_present[:, :, None] == 1, 1.0 - similarity, 1.0)
    across, down = paths_call(cost, smoothness_charges)
    down = down.reshape(lax.axis_size("row"), rows_here, -1, DISPARITIES).astype(jnp.float32)
    down = jnp.swapaxes(down, 0, 1).reshape(cost.shape)
    return down + jnp.swapaxes(across, 0, 1)


def solution(mesh):
    return jax.shard_map(
        per_device,
        mesh=mesh,
        in_specs=(P(None, "row", None, "col"), P(), P(), P("row", "col"), P("row", "col"), P()),
        out_specs=P("row", "col", None),
        check_vma=False,
    )
```

```python
import functools

import jax
import jax.numpy as jnp
from jax import lax
from jax.experimental import pallas as pl
from jax.experimental.pallas import tpu as pltpu
from jax.sharding import PartitionSpec as P

DISPARITIES = 128
SUB = 8
PARTS = DISPARITIES // SUB
MESH = pl.DeviceIdType.MESH


def from_behind(block, axis, distance):
    devices = range(lax.axis_size(axis))
    route = [(i - distance, i) for i in devices if i - distance in devices]
    return lax.ppermute(block, axis, route)


def extended_2(value, sides, width):
    for axis, dim in sides:
        count, length = (lax.axis_size(axis), value.shape[dim])
        up = [(i, (i + 1) % count) for i in range(count - 1)]
        down = [(j, i) for i, j in up]
        last = lax.slice_in_dim(value, length - width, length, axis=dim)
        first = lax.slice_in_dim(value, 0, width, axis=dim)
        before = lax.ppermute(last, axis, up)
        after = lax.ppermute(first, axis, down)
        value = jnp.concatenate([before, value, after], axis=dim)
    return value


def order_matrix():
    row = lax.broadcasted_iota(jnp.int32, (DISPARITIES, DISPARITIES), 0)
    lane = lax.broadcasted_iota(jnp.int32, (DISPARITIES, DISPARITIES), 1)
    return jnp.where(lane == (row % SUB) * PARTS + row // SUB, 1.0, 0.0).astype(jnp.bfloat16)


def turned(value, order):
    return lax.dot_general(
        order,
        value.astype(jnp.bfloat16),
        (((1,), (1,)), ((), ())),
        preferred_element_type=jnp.float32,
    )


def ordered(value, order):
    return jnp.dot(value, order, preferred_element_type=jnp.float32)


def pieces_of(value):
    return [value[v * SUB : (v + 1) * SUB] for v in range(PARTS)]


def smallest(state):
    level = list(state)
    while len(level) > 1:
        level = [jnp.minimum(level[2 * i], level[2 * i + 1]) for i in range(len(level) // 2)]
    least = level[0]
    for step in (4, 2, 1):
        least = jnp.minimum(least, pltpu.roll(least, step, 0))
    return least


def step_once(state, cost, p1, p2, first_sub, last_sub):
    lifted = [s + p1 for s in state]
    below = jnp.where(first_sub, jnp.inf, pltpu.roll(lifted[-1], 1, 0))
    above = jnp.where(last_sub, jnp.inf, pltpu.roll(lifted[0], SUB - 1, 0))
    near = [below] + lifted + [above]
    least = smallest(state)
    jump = least + p2
    fresh = [
        cost[v]
        + jnp.minimum(jnp.minimum(state[v], jnp.minimum(near[v], near[v + 2])), jump)
        for v in range(PARTS)
    ]
    return fresh, least


def walk(slots, out, leasts, count, state, charges, at):
    sub = lax.broadcasted_iota(jnp.int32, (SUB, SUB), 0)
    first_sub, last_sub = sub == 0, sub == SUB - 1
    p1 = charges[0].astype(jnp.float32) / 64.0
    p2 = charges[1].astype(jnp.float32) / 64.0

    def body(turn, carry):
        state, least = list(carry[0]), carry[1]
        for k in range(8):
            t = at(turn * 8 + k)
            state, least = step_once(state, pieces_of(slots[t]), p1, p2, first_sub, last_sub)
            leasts[t] = least
            for v in range(PARTS):
                out[t, v * SUB : (v + 1) * SUB, :] = state[v]
        return tuple(state), least

    start = (tuple(state), jnp.zeros((SUB, SUB), jnp.float32))
    return lax.fori_loop(0, count // 8, body, start)


def layer(walked, leasts, t):
    least = leasts[t]
    return jnp.concatenate([piece - least for piece in pieces_of(walked[t])], axis=0).T


def turn_in(piece, slots, count, order):
    def body(turn, _):
        for k in range(16):
            t = turn * 16 + k
            slots[t] = turned(piece(t), order)
        return 0

    lax.fori_loop(0, count // 16, body, 0)


def half_turn(value):
    return pltpu.roll(value, SUB // 2, 0)


def paths_kernel(
    row_size,
    col_size,
    cost,
    charges,
    out_across,
    out_down,
    slots,
    walked,
    strips,
    leasts,
    strip_leasts,
    edge_out,
    edge_in,
    sent,
    came,
    back_out,
    back_in,
    edge_send,
    edge_recv,
    sent_sem,
    came_sem,
    back_send,
    back_recv,
):
    count = out_across.shape[0]
    height = strips.shape[0]
    row = lax.axis_index("row")
    me = lax.axis_index("col")
    low = lax.broadcasted_iota(jnp.int32, (SUB, DISPARITIES), 0) < SUB // 2
    order = order_matrix()

    barrier = pltpu.get_barrier_semaphore()

    @pl.when(me > 0)
    def _():
        pl.semaphore_signal(barrier, inc=1, device_id={"col": me - 1}, device_id_type=MESH)

    @pl.when(me < col_size - 1)
    def _():
        pl.semaphore_signal(barrier, inc=1, device_id={"col": me + 1}, device_id_type=MESH)

    def greet(j, _):
        peer = lax.rem(row + j, row_size)
        pl.semaphore_signal(barrier, inc=1, device_id={"row": peer}, device_id_type=MESH)
        return 0

    lax.fori_loop(1, row_size, greet, 0)

    def exchange(source, target, send_sem, recv_sem, what):
        def copy(mine, slot):
            return pltpu.make_async_remote_copy(
                src_ref=source.at[mine],
                dst_ref=target.at[slot],
                send_sem=send_sem.at[mine],
                recv_sem=recv_sem.at[slot],
                device_id={"row": mine},
                device_id_type=MESH,
            )

        def body(j, _):
            peer = lax.rem(row + j, row_size)
            if what == "start":
                copy(peer, row).start()
            elif what == "sent":
                copy(peer, row).wait_send()
            else:
                copy(peer, peer).wait_recv()
            return 0

        lax.fori_loop(1, row_size, body, 0)
        if what == "start":
            target[row] = source[row]

    def cut(tile, _):
        start = pl.multiple_of(tile * SUB, SUB)
        rows = [cost[y, pl.ds(start, SUB), :] for y in range(SUB)]
        even = [jnp.where(low, rows[y], half_turn(rows[y + 1])) for y in range(0, SUB, 2)]
        odd = [jnp.where(low, half_turn(rows[y]), rows[y + 1]) for y in range(0, SUB, 2)]
        sent[2 * tile] = jnp.concatenate(even, axis=0).astype(jnp.bfloat16)
        sent[2 * tile + 1] = jnp.concatenate(odd, axis=0).astype(jnp.bfloat16)
        return 0

    lax.fori_loop(0, row_size // 2, cut, 0)
    neighbours = jnp.where(me > 0, 1, 0) + jnp.where(me < col_size - 1, 1, 0)
    pl.semaphore_wait(barrier, neighbours + row_size - 1)
    exchange(sent, came, sent_sem, came_sem, "start")
    turn_in(lambda x: cost[:, x, :], slots, count, order)

    def vertical_in():
        exchange(sent, came, sent_sem, came_sem, "came")

        def body(source, _):
            near = came[source].astype(jnp.float32)
            far = came[row_size - 1 - source].astype(jnp.float32)
            for q in range(SUB // 2):
                a = near[q * SUB : (q + 1) * SUB]
                b = far[(3 - q) * SUB : (4 - q) * SUB]
                first = jnp.where(low, a, b)
                second = half_turn(jnp.where(low, b, a))
                t = source * SUB + 2 * q
                strips[t] = turned(first, order)
                strips[t + 1] = turned(second, order)
            return 0

        lax.fori_loop(0, row_size, body, 0)

    def vertical_walk():
        zero = [jnp.zeros((SUB, SUB), jnp.float32) for _ in range(PARTS)]
        walk(strips, strips, strip_leasts, height, zero, charges, lambda t: t)

    def vertical_out():
        def body(near, _):
            far = row_size - 1 - near
            one = [layer(strips, strip_leasts, near * SUB + y) for y in range(SUB)]
            other = [layer(strips, strip_leasts, far * SUB + y) for y in range(SUB)]
            total = [one[y] + half_turn(other[SUB - 1 - y]) for y in range(SUB)]
            up = [jnp.where(low, total[y], half_turn(total[y + 1])) for y in (0, 2, 4, 6)]
            down = [jnp.where(low, half_turn(total[y + 1]), total[y]) for y in (6, 4, 2, 0)]
            both = jnp.concatenate(up + down, axis=0).astype(jnp.bfloat16)
            both = ordered(both, order).astype(jnp.bfloat16)
            half = SUB * SUB // 2
            back_out[near] = both[:half]
            back_out[far] = both[half:]
            return 0

        lax.fori_loop(0, row_size // 2, body, 0)
        exchange(back_out, back_in, back_send, back_recv, "start")

    def one_direction(way, first):
        starts = me == (0 if way == 0 else col_size - 1)
        ends = me == (col_size - 1 if way == 0 else 0)
        toward = me + 1 if way == 0 else me - 1
        at = (lambda t: t) if way == 0 else (lambda t: count - 1 - t)

        def copy():
            return pltpu.make_async_remote_copy(
                src_ref=edge_out.at[way],
                dst_ref=edge_in.at[way],
                send_sem=edge_send.at[way],
                recv_sem=edge_recv.at[way],
                device_id={"col": toward},
                device_id_type=MESH,
            )

        @pl.when(starts)
        def _():
            edge_in[way] = jnp.zeros((DISPARITIES, SUB), jnp.float32)

        @pl.when(jnp.logical_not(starts))
        def _():
            copy().wait_recv()

        state, least = walk(
            slots, walked, leasts, count, pieces_of(edge_in[way]), charges, at
        )

        @pl.when(jnp.logical_not(ends))
        def _():
            edge_out[way] = jnp.concatenate([piece - least for piece in state], axis=0)
            copy().start()

        def body(turn, _):
            start = turn * 16
            results = [layer(walked, leasts, start + k) for k in range(16)]
            if first:
                for k in range(16):
                    out_across[start + k] = results[k]
            else:
                total = [out_across[start + k] + results[k] for k in range(16)]
                total = jnp.concatenate(total, axis=0)
                high = total.astype(jnp.bfloat16)
                rest = (total - high.astype(jnp.float32)).astype(jnp.bfloat16)
                total = ordered(high, order) + ordered(rest, order)
                for k in range(16):
                    out_across[start + k] = total[k * SUB : (k + 1) * SUB]
            return 0

        lax.fori_loop(0, count // 16, body, 0)

        @pl.when(jnp.logical_not(ends))
        def _():
            copy().wait_send()

    place = jnp.minimum(me, col_size - 1 - me)
    pieces = ((vertical_in, 3), (vertical_walk, 5), (vertical_out, 6))
    for piece, threshold in pieces:
        pl.when(place >= threshold)(piece)

    @pl.when(me < col_size // 2)
    def _():
        one_direction(0, True)

    @pl.when(me >= col_size // 2)
    def _():
        one_direction(1, True)

    for piece, threshold in pieces:
        pl.when(place < threshold)(piece)

    @pl.when(me < col_size // 2)
    def _():
        one_direction(1, False)

    @pl.when(me >= col_size // 2)
    def _():
        one_direction(0, False)

    exchange(back_out, back_in, back_send, back_recv, "came")

    def hand_over(j, _):
        out_down[j] = back_in[j]
        return 0

    lax.fori_loop(0, row_size, hand_over, 0)
    exchange(sent, came, sent_sem, came_sem, "sent")
    exchange(back_out, back_in, back_send, back_recv, "sent")


def paths_call(cost, charges):
    rows, count, _ = cost.shape
    row_size, col_size = lax.axis_size("row"), lax.axis_size("col")
    width = count // row_size
    block = (row_size, rows * width, DISPARITIES)
    vmem = pl.BlockSpec(memory_space=pltpu.VMEM)
    return pl.pallas_call(
        functools.partial(paths_kernel, row_size, col_size),
        out_shape=(
            jax.ShapeDtypeStruct((count, rows, DISPARITIES), jnp.float32),
            jax.ShapeDtypeStruct(block, jnp.bfloat16),
        ),
        in_specs=[vmem, pl.BlockSpec(memory_space=pltpu.SMEM)],
        out_specs=(vmem, vmem),
        scratch_shapes=[
            pltpu.VMEM((count, DISPARITIES, SUB), jnp.float32),
            pltpu.VMEM((count, DISPARITIES, SUB), jnp.float32),
            pltpu.VMEM((rows * row_size, DISPARITIES, SUB), jnp.float32),
            pltpu.VMEM((count, SUB, SUB), jnp.float32),
            pltpu.VMEM((rows * row_size, SUB, SUB), jnp.float32),
            pltpu.VMEM((2, DISPARITIES, SUB), jnp.float32),
            pltpu.VMEM((2, DISPARITIES, SUB), jnp.float32),
            pltpu.VMEM(block, jnp.bfloat16),
            pltpu.VMEM(block, jnp.bfloat16),
            pltpu.VMEM(block, jnp.bfloat16),
            pltpu.VMEM(block, jnp.bfloat16),
            pltpu.SemaphoreType.DMA((2,)),
            pltpu.SemaphoreType.DMA((2,)),
            pltpu.SemaphoreType.DMA((row_size,)),
            pltpu.SemaphoreType.DMA((row_size,)),
            pltpu.SemaphoreType.DMA((row_size,)),
            pltpu.SemaphoreType.DMA((row_size,)),
        ],
        compiler_params=pltpu.CompilerParams(
            collective_id=0, has_side_effects=True, vmem_limit_bytes=60 * 1024 * 1024
        ),
        name="four_paths",
    )(cost, charges)


def conv_stack(stereo_neuron_outputs, filter_tap_coefficients, filter_stack_intercepts):
    layers_total = filter_tap_coefficients.shape[0]
    rows_here = stereo_neuron_outputs.shape[1]
    cols_here = stereo_neuron_outputs.shape[3]
    hidden = extended_2(stereo_neuron_outputs, (("row", 1), ("col", 3)), layers_total)
    row_start = lax.axis_index("row") * rows_here
    col_start = lax.axis_index("col") * cols_here
    row_limit = lax.axis_size("row") * rows_here
    col_limit = lax.axis_size("col") * cols_here
    features = None
    for layer_number in range(layers_total):
        margin = layers_total - 1 - layer_number
        out_rows = rows_here + 2 * margin
        out_cols = cols_here + 2 * margin
        summed = None
        for tap_row in range(3):
            for tap_col in range(3):
                window = hidden[:, tap_row : tap_row + out_rows, :, tap_col : tap_col + out_cols]
                term = jnp.einsum(
                    "oc,iycx->iyox",
                    filter_tap_coefficients[layer_number, tap_row, tap_col],
                    window,
                    preferred_element_type=jnp.float32,
                )
                summed = term if summed is None else summed + term
        summed = summed + filter_stack_intercepts[layer_number][None, None, :, None]
        if layer_number < layers_total - 1:
            global_rows = row_start - margin + jnp.arange(out_rows, dtype=jnp.int32)
            global_cols = col_start - margin + jnp.arange(out_cols, dtype=jnp.int32)
            keep_rows = jnp.logical_and(global_rows >= 0, global_rows < row_limit)
            keep_cols = jnp.logical_and(global_cols >= 0, global_cols < col_limit)
            keeper = jnp.logical_and(keep_rows[None, :, None, None], keep_cols[None, None, None, :])
            hidden = jnp.where(keeper, jnp.maximum(summed, 0.0), 0.0).astype(jnp.bfloat16)
        else:
            features = summed
    scale = lax.rsqrt(jnp.sum(features * features, axis=2, keepdims=True) + 1e-06)
    return (features * scale).astype(jnp.bfloat16)


def per_device(
    stereo_neuron_outputs,
    filter_tap_coefficients,
    filter_stack_intercepts,
    reference_picture_present,
    tile_shift_amounts,
    smoothness_charges,
):
    unit = conv_stack(stereo_neuron_outputs, filter_tap_coefficients, filter_stack_intercepts)
    left_unit = unit[0]
    right_normalized_features = unit[1]
    rows_here = left_unit.shape[0]
    cols_here = left_unit.shape[2]
    reach = (3 * cols_here + DISPARITIES - 2) // cols_here
    tile_offset = tile_shift_amounts[0, 0]
    pieces = [
        from_behind(right_normalized_features, "col", distance) for distance in range(reach, 0, -1)
    ]
    extended = jnp.concatenate(pieces + [right_normalized_features], axis=2)
    strip_start = reach * cols_here - tile_offset - (DISPARITIES - 1)
    strip = lax.dynamic_slice_in_dim(extended, strip_start, cols_here + DISPARITIES - 1, 2)
    product = jnp.einsum("ycj,yck->yjk", left_unit, strip, preferred_element_type=jnp.float32)
    padded = jnp.pad(product, ((0, 0), (0, 0), (0, 1)))
    flat = padded.reshape(rows_here, cols_here * (cols_here + DISPARITIES))
    flat = jnp.pad(flat, ((0, 0), (0, cols_here)))
    skewed = flat.reshape(rows_here, cols_here, cols_here + DISPARITIES + 1)[:, :, :DISPARITIES]
    similarity = skewed[:, :, ::-1]
    cost = jnp.where(reference_picture_present[:, :, None] == 1, 1.0 - similarity, 1.0)
    across, down = paths_call(cost, smoothness_charges)
    down = down.reshape(lax.axis_size("row"), rows_here, -1, DISPARITIES).astype(jnp.float32)
    down = jnp.swapaxes(down, 0, 1).reshape(cost.shape)
    return down + jnp.swapaxes(across, 0, 1)


def solution(mesh):
    return jax.shard_map(
        per_device,
        mesh=mesh,
        in_specs=(P(None, "row", None, "col"), P(), P(), P("row", "col"), P("row", "col"), P()),
        out_specs=P("row", "col", None),
        check_vma=False,
    )
```

```python
import functools

import jax
import jax.numpy as jnp
from jax import lax
from jax.experimental import pallas as pl
from jax.experimental.pallas import tpu as pltpu
from jax.sharding import PartitionSpec as P

DISPARITIES = 128
SUB = 8
PARTS = DISPARITIES // SUB
MESH = pl.DeviceIdType.MESH


def order_matrix():
    row = lax.broadcasted_iota(jnp.int32, (DISPARITIES, DISPARITIES), 0)
    lane = lax.broadcasted_iota(jnp.int32, (DISPARITIES, DISPARITIES), 1)
    return jnp.where(lane == (row % SUB) * PARTS + row // SUB, 1.0, 0.0).astype(jnp.bfloat16)


def turned(value, order):
    return lax.dot_general(
        order,
        value.astype(jnp.bfloat16),
        (((1,), (1,)), ((), ())),
        preferred_element_type=jnp.float32,
    )


def ordered(value, order):
    return jnp.dot(value, order, preferred_element_type=jnp.float32)


def pieces_of(value):
    return [value[v * SUB : (v + 1) * SUB] for v in range(PARTS)]


def smallest(state):
    level = list(state)
    while len(level) > 1:
        level = [jnp.minimum(level[2 * i], level[2 * i + 1]) for i in range(len(level) // 2)]
    least = level[0]
    for step in (4, 2, 1):
        least = jnp.minimum(least, pltpu.roll(least, step, 0))
    return least


def step_once(state, cost, p1, p2, first_sub, last_sub):
    lifted = [s + p1 for s in state]
    below = jnp.where(first_sub, jnp.inf, pltpu.roll(lifted[-1], 1, 0))
    above = jnp.where(last_sub, jnp.inf, pltpu.roll(lifted[0], SUB - 1, 0))
    near = [below] + lifted + [above]
    least = smallest(state)
    jump = least + p2
    fresh = [
        cost[v]
        + jnp.minimum(jnp.minimum(state[v], jnp.minimum(near[v], near[v + 2])), jump)
        for v in range(PARTS)
    ]
    return fresh, least


def walk(slots, out, leasts, count, state, charges, at):
    sub = lax.broadcasted_iota(jnp.int32, (SUB, SUB), 0)
    first_sub, last_sub = sub == 0, sub == SUB - 1
    p1 = charges[0].astype(jnp.float32) / 64.0
    p2 = charges[1].astype(jnp.float32) / 64.0

    def body(turn, carry):
        state, least = list(carry[0]), carry[1]
        for k in range(8):
            t = at(turn * 8 + k)
            state, least = step_once(state, pieces_of(slots[t]), p1, p2, first_sub, last_sub)
            leasts[t] = least
            for v in range(PARTS):
                out[t, v * SUB : (v + 1) * SUB, :] = state[v]
        return tuple(state), least

    start = (tuple(state), jnp.zeros((SUB, SUB), jnp.float32))
    return lax.fori_loop(0, count // 8, body, start)


def layer(walked, leasts, t):
    least = leasts[t]
    return jnp.concatenate([piece - least for piece in pieces_of(walked[t])], axis=0).T


def turn_in(piece, slots, count, order):
    def body(turn, _):
        for k in range(16):
            t = turn * 16 + k
            slots[t] = turned(piece(t), order)
        return 0

    lax.fori_loop(0, count // 16, body, 0)


def half_turn(value):
    return pltpu.roll(value, SUB // 2, 0)


def paths_kernel(
    row_size,
    col_size,
    cost,
    charges,
    out_across,
    out_down,
    slots,
    walked,
    strips,
    leasts,
    strip_leasts,
    edge_out,
    edge_in,
    sent,
    came,
    back_out,
    back_in,
    edge_send,
    edge_recv,
    sent_sem,
    came_sem,
    back_send,
    back_recv,
):
    count = out_across.shape[0]
    height = strips.shape[0]
    row = lax.axis_index("row")
    me = lax.axis_index("col")
    low = lax.broadcasted_iota(jnp.int32, (SUB, DISPARITIES), 0) < SUB // 2
    order = order_matrix()

    barrier = pltpu.get_barrier_semaphore()

    @pl.when(me > 0)
    def _():
        pl.semaphore_signal(barrier, inc=1, device_id={"col": me - 1}, device_id_type=MESH)

    @pl.when(me < col_size - 1)
    def _():
        pl.semaphore_signal(barrier, inc=1, device_id={"col": me + 1}, device_id_type=MESH)

    def greet(j, _):
        peer = lax.rem(row + j, row_size)
        pl.semaphore_signal(barrier, inc=1, device_id={"row": peer}, device_id_type=MESH)
        return 0

    lax.fori_loop(1, row_size, greet, 0)

    def exchange(source, target, send_sem, recv_sem, what):
        def copy(mine, slot):
            return pltpu.make_async_remote_copy(
                src_ref=source.at[mine],
                dst_ref=target.at[slot],
                send_sem=send_sem.at[mine],
                recv_sem=recv_sem.at[slot],
                device_id={"row": mine},
                device_id_type=MESH,
            )

        def body(j, _):
            peer = lax.rem(row + j, row_size)
            if what == "start":
                copy(peer, row).start()
            elif what == "sent":
                copy(peer, row).wait_send()
            else:
                copy(peer, peer).wait_recv()
            return 0

        lax.fori_loop(1, row_size, body, 0)
        if what == "start":
            target[row] = source[row]

    def cut(tile, _):
        start = pl.multiple_of(tile * SUB, SUB)
        rows = [cost[y, pl.ds(start, SUB), :] for y in range(SUB)]
        even = [jnp.where(low, rows[y], half_turn(rows[y + 1])) for y in range(0, SUB, 2)]
        odd = [jnp.where(low, half_turn(rows[y]), rows[y + 1]) for y in range(0, SUB, 2)]
        sent[2 * tile] = jnp.concatenate(even, axis=0).astype(jnp.bfloat16)
        sent[2 * tile + 1] = jnp.concatenate(odd, axis=0).astype(jnp.bfloat16)
        return 0

    lax.fori_loop(0, row_size // 2, cut, 0)
    neighbours = jnp.where(me > 0, 1, 0) + jnp.where(me < col_size - 1, 1, 0)
    pl.semaphore_wait(barrier, neighbours + row_size - 1)
    exchange(sent, came, sent_sem, came_sem, "start")
    turn_in(lambda x: cost[:, x, :], slots, count, order)

    def vertical_in():
        exchange(sent, came, sent_sem, came_sem, "came")

        def body(source, _):
            near = came[source].astype(jnp.float32)
            far = came[row_size - 1 - source].astype(jnp.float32)
            for q in range(SUB // 2):
                a = near[q * SUB : (q + 1) * SUB]
                b = far[(3 - q) * SUB : (4 - q) * SUB]
                first = jnp.where(low, a, b)
                second = half_turn(jnp.where(low, b, a))
                t = source * SUB + 2 * q
                strips[t] = turned(first, order)
                strips[t + 1] = turned(second, order)
            return 0

        lax.fori_loop(0, row_size, body, 0)

    def vertical_walk():
        zero = [jnp.zeros((SUB, SUB), jnp.float32) for _ in range(PARTS)]
        walk(strips, strips, strip_leasts, height, zero, charges, lambda t: t)

    def vertical_out():
        def body(near, _):
            far = row_size - 1 - near
            one = [layer(strips, strip_leasts, near * SUB + y) for y in range(SUB)]
            other = [layer(strips, strip_leasts, far * SUB + y) for y in range(SUB)]
            total = [one[y] + half_turn(other[SUB - 1 - y]) for y in range(SUB)]
            up = [jnp.where(low, total[y], half_turn(total[y + 1])) for y in (0, 2, 4, 6)]
            down = [jnp.where(low, half_turn(total[y + 1]), total[y]) for y in (6, 4, 2, 0)]
            both = jnp.concatenate(up + down, axis=0).astype(jnp.bfloat16)
            both = ordered(both, order).astype(jnp.bfloat16)
            half = SUB * SUB // 2
            back_out[near] = both[:half]
            back_out[far] = both[half:]
            return 0

        lax.fori_loop(0, row_size // 2, body, 0)
        exchange(back_out, back_in, back_send, back_recv, "start")

    def one_direction(way, first):
        starts = me == (0 if way == 0 else col_size - 1)
        ends = me == (col_size - 1 if way == 0 else 0)
        toward = me + 1 if way == 0 else me - 1
        at = (lambda t: t) if way == 0 else (lambda t: count - 1 - t)

        def copy():
            return pltpu.make_async_remote_copy(
                src_ref=edge_out.at[way],
                dst_ref=edge_in.at[way],
                send_sem=edge_send.at[way],
                recv_sem=edge_recv.at[way],
                device_id={"col": toward},
                device_id_type=MESH,
            )

        @pl.when(starts)
        def _():
            edge_in[way] = jnp.zeros((DISPARITIES, SUB), jnp.float32)

        @pl.when(jnp.logical_not(starts))
        def _():
            copy().wait_recv()

        state, least = walk(
            slots, walked, leasts, count, pieces_of(edge_in[way]), charges, at
        )

        @pl.when(jnp.logical_not(ends))
        def _():
            edge_out[way] = jnp.concatenate([piece - least for piece in state], axis=0)
            copy().start()

        def body(turn, _):
            start = turn * 16
            results = [layer(walked, leasts, start + k) for k in range(16)]
            if first:
                for k in range(16):
                    out_across[start + k] = results[k]
            else:
                total = [out_across[start + k] + results[k] for k in range(16)]
                total = jnp.concatenate(total, axis=0)
                high = total.astype(jnp.bfloat16)
                rest = (total - high.astype(jnp.float32)).astype(jnp.bfloat16)
                total = ordered(high, order) + ordered(rest, order)
                for k in range(16):
                    out_across[start + k] = total[k * SUB : (k + 1) * SUB]
            return 0

        lax.fori_loop(0, count // 16, body, 0)

        @pl.when(jnp.logical_not(ends))
        def _():
            copy().wait_send()

    place = jnp.minimum(me, col_size - 1 - me)
    pieces = ((vertical_in, 3), (vertical_walk, 5), (vertical_out, 6))
    for piece, threshold in pieces:
        pl.when(place >= threshold)(piece)

    @pl.when(me < col_size // 2)
    def _():
        one_direction(0, True)

    @pl.when(me >= col_size // 2)
    def _():
        one_direction(1, True)

    for piece, threshold in pieces:
        pl.when(place < threshold)(piece)

    @pl.when(me < col_size // 2)
    def _():
        one_direction(1, False)

    @pl.when(me >= col_size // 2)
    def _():
        one_direction(0, False)

    exchange(back_out, back_in, back_send, back_recv, "came")

    def hand_over(j, _):
        out_down[j] = back_in[j]
        return 0

    lax.fori_loop(0, row_size, hand_over, 0)
    exchange(sent, came, sent_sem, came_sem, "sent")
    exchange(back_out, back_in, back_send, back_recv, "sent")


def paths_call(cost, charges):
    rows, count, _ = cost.shape
    row_size, col_size = lax.axis_size("row"), lax.axis_size("col")
    width = count // row_size
    block = (row_size, rows * width, DISPARITIES)
    vmem = pl.BlockSpec(memory_space=pltpu.VMEM)
    return pl.pallas_call(
        functools.partial(paths_kernel, row_size, col_size),
        out_shape=(
            jax.ShapeDtypeStruct((count, rows, DISPARITIES), jnp.float32),
            jax.ShapeDtypeStruct(block, jnp.bfloat16),
        ),
        in_specs=[vmem, pl.BlockSpec(memory_space=pltpu.SMEM)],
        out_specs=(vmem, vmem),
        scratch_shapes=[
            pltpu.VMEM((count, DISPARITIES, SUB), jnp.float32),
            pltpu.VMEM((count, DISPARITIES, SUB), jnp.float32),
            pltpu.VMEM((rows * row_size, DISPARITIES, SUB), jnp.float32),
            pltpu.VMEM((count, SUB, SUB), jnp.float32),
            pltpu.VMEM((rows * row_size, SUB, SUB), jnp.float32),
            pltpu.VMEM((2, DISPARITIES, SUB), jnp.float32),
            pltpu.VMEM((2, DISPARITIES, SUB), jnp.float32),
            pltpu.VMEM(block, jnp.bfloat16),
            pltpu.VMEM(block, jnp.bfloat16),
            pltpu.VMEM(block, jnp.bfloat16),
            pltpu.VMEM(block, jnp.bfloat16),
            pltpu.SemaphoreType.DMA((2,)),
            pltpu.SemaphoreType.DMA((2,)),
            pltpu.SemaphoreType.DMA((row_size,)),
            pltpu.SemaphoreType.DMA((row_size,)),
            pltpu.SemaphoreType.DMA((row_size,)),
            pltpu.SemaphoreType.DMA((row_size,)),
        ],
        compiler_params=pltpu.CompilerParams(
            collective_id=0, has_side_effects=True, vmem_limit_bytes=60 * 1024 * 1024
        ),
        name="four_paths",
    )(cost, charges)


def outer_kernel_sizes(images, halo):
    rows, channels, count = images.shape[1:]
    return rows, channels, count, rows + 2 * halo


def cost_kernel(
    row_size,
    col_size,
    layers_total,
    images,
    taps,
    biases,
    present,
    shift,
    cost,
    above,
    below,
    packed,
    from_left,
    from_right,
    stack_a,
    stack_b,
    left_unit,
    reach_unit,
    rows_send,
    rows_recv,
    cols_send,
    cols_recv,
    unit_send,
    unit_recv,
):
    rows, channels, count, tall = outer_kernel_sizes(images, layers_total)
    far = reach_unit.shape[0] - 1
    deep = 3 * channels
    row, me = lax.axis_index("row"), lax.axis_index("col")
    has_up, has_down = row > 0, row < row_size - 1
    has_left, has_right = me > 0, me < col_size - 1

    barrier = pltpu.get_barrier_semaphore()
    expected = jnp.where(has_up, 1, 0) + jnp.where(has_down, 1, 0)
    for there, step in ((has_up, -1), (has_down, 1)):

        @pl.when(there)
        def _(step=step):
            pl.semaphore_signal(barrier, inc=1, device_id={"row": row + step}, device_id_type=MESH)

    for distance in range(1, far + 1):
        for there, step in ((me >= distance, -distance), (me + distance < col_size, distance)):
            expected = expected + jnp.where(there, 1, 0)

            @pl.when(there)
            def _(step=step):
                pl.semaphore_signal(
                    barrier, inc=1, device_id={"col": me + step}, device_id_type=MESH
                )

    pl.semaphore_wait(barrier, expected)

    def row_copy(step):
        index = 0 if step < 0 else 1
        first = 0 if step < 0 else rows - layers_total
        return pltpu.make_async_remote_copy(
            src_ref=images.at[:, first : first + layers_total],
            dst_ref=below if step < 0 else above,
            send_sem=rows_send.at[index],
            recv_sem=rows_recv.at[index],
            device_id={"row": row + step},
            device_id_type=MESH,
        )

    def col_copy(step):
        index = 0 if step < 0 else 1
        return pltpu.make_async_remote_copy(
            src_ref=packed,
            dst_ref=from_right if step < 0 else from_left,
            send_sem=cols_send.at[index],
            recv_sem=cols_recv.at[index],
            device_id={"col": me + step},
            device_id_type=MESH,
        )

    def unit_copy(distance):
        return pltpu.make_async_remote_copy(
            src_ref=reach_unit.at[0],
            dst_ref=reach_unit.at[distance],
            send_sem=unit_send.at[distance],
            recv_sem=unit_recv.at[distance],
            device_id={"col": me + distance},
            device_id_type=MESH,
        )

    pl.when(has_up)(lambda: row_copy(-1).start())
    pl.when(has_down)(lambda: row_copy(1).start())

    @pl.when(jnp.logical_not(has_up))
    def _():
        above[...] = jnp.zeros_like(above)

    @pl.when(jnp.logical_not(has_down))
    def _():
        below[...] = jnp.zeros_like(below)

    pl.when(has_down)(lambda: row_copy(-1).wait_recv())
    pl.when(has_up)(lambda: row_copy(1).wait_recv())

    def row_of(image, k):
        if k < layers_total:
            return above[image, k]
        if k < layers_total + rows:
            return images[image, k - layers_total]
        return below[image, k - layers_total - rows]

    pick_row = lax.broadcasted_iota(jnp.int32, (count, count), 0)
    pick_lane = lax.broadcasted_iota(jnp.int32, (count, count), 1)

    def one_hot(where):
        return jnp.where(where, 1.0, 0.0).astype(jnp.bfloat16)

    for image in range(2):
        total = None
        for k in range(tall):
            slot = pick_lane - k * SUB
            head = jnp.logical_and(slot >= 0, jnp.logical_and(slot < 3, pick_row == slot))
            tail = jnp.logical_and(
                slot >= 3, jnp.logical_and(slot < 6, pick_row == slot + count - 6)
            )
            pick = one_hot(jnp.logical_or(head, tail))
            term = jnp.dot(row_of(image, k), pick, preferred_element_type=jnp.float32)
            total = term if total is None else total + term
        packed[image] = total.astype(jnp.bfloat16)

    pl.when(has_left)(lambda: col_copy(-1).start())
    pl.when(has_right)(lambda: col_copy(1).start())

    @pl.when(jnp.logical_not(has_left))
    def _():
        from_left[...] = jnp.zeros_like(from_left)

    @pl.when(jnp.logical_not(has_right))
    def _():
        from_right[...] = jnp.zeros_like(from_right)

    for distance in range(1, far + 1):

        @pl.when(me < distance)
        def _(distance=distance):
            reach_unit[distance] = jnp.zeros(reach_unit.shape[1:], reach_unit.dtype)

    pl.when(has_right)(lambda: col_copy(-1).wait_recv())
    pl.when(has_left)(lambda: col_copy(1).wait_recv())

    lanes = lax.broadcasted_iota(jnp.int32, (channels, 2 * count), 1)
    side = jnp.where(lanes < count + count // 2, has_right.astype(jnp.int32), has_left.astype(jnp.int32))
    keep_lane = jnp.where(lanes < count, 1, side)

    def put(stack, k, value):
        base = k * deep if isinstance(k, int) else pl.multiple_of(k * deep, deep)
        for b, turn in enumerate((1, 0, 2 * count - 1)):
            moved = pltpu.roll(value, turn, 1) if turn else value
            stack[pl.ds(base + b * channels, channels), :] = moved.astype(jnp.bfloat16)

    def features(image):
        for k in range(tall):
            slot_left = pick_row - k * SUB - 3 == pick_lane - (count - 3)
            slot_left = jnp.logical_and(slot_left, pick_lane >= count - 3)
            slot_right = jnp.logical_and(pick_row - k * SUB == pick_lane, pick_lane < 3)
            edge = jnp.dot(
                from_left[image], one_hot(slot_left), preferred_element_type=jnp.float32
            ) + jnp.dot(
                from_right[image], one_hot(slot_right), preferred_element_type=jnp.float32
            )
            put(
                stack_a,
                k,
                jnp.concatenate([row_of(image, k).astype(jnp.float32), edge], axis=1),
            )
        source, target = stack_a, stack_b
        for layer_number in range(layers_total):
            margin = layers_total - 1 - layer_number
            bias = biases[layer_number]
            weights = taps[layer_number]
            last = margin == 0

            def body(pair, _):
                for k in range(2):
                    y = pair * 2 + k
                    window = source[pl.ds(pl.multiple_of(y * deep, deep), 3 * deep), :]
                    if last:
                        window = window[:, :count]
                    value = jnp.dot(weights, window, preferred_element_type=jnp.float32) + bias
                    if last:
                        square = jnp.sum(value * value, axis=0, keepdims=True)
                        unit = (value * lax.rsqrt(square + 1e-06)).astype(jnp.bfloat16)
                        start = pl.multiple_of(y * channels, channels)
                        if image == 1:
                            reach_unit[0, pl.ds(start, channels), :] = unit
                        else:
                            left_unit[pl.ds(start, channels), :] = unit
                    else:
                        keep = jnp.logical_and(
                            jnp.logical_or(y >= margin, has_up),
                            jnp.logical_or(y < margin + rows, has_down),
                        )
                        value = jnp.where(
                            keep_lane * keep.astype(jnp.int32) == 1, jnp.maximum(value, 0.0), 0.0
                        )
                        put(target, y, value)
                return 0

            lax.fori_loop(0, (rows + 2 * margin) // 2, body, 0)
            source, target = target, source

    features(1)
    for distance in range(1, far + 1):
        pl.when(me + distance < col_size)(lambda distance=distance: unit_copy(distance).start())
    features(0)
    for distance in range(1, far + 1):
        pl.when(me >= distance)(lambda distance=distance: unit_copy(distance).wait_recv())

    wide = (far + 1) * count
    place = lax.broadcasted_iota(jnp.int32, (wide, 2 * count), 0)
    lane = lax.broadcasted_iota(jnp.int32, (wide, 2 * count), 1)
    choose = one_hot(place + lane == wide - 1 - shift[0, 0])

    def match(y, _):
        start = pl.multiple_of(y * channels, channels)
        reach = jnp.concatenate(
            [reach_unit[distance, pl.ds(start, channels), :] for distance in range(far, -1, -1)],
            axis=1,
        )
        strip = jnp.dot(reach, choose, preferred_element_type=jnp.float32).astype(jnp.bfloat16)
        held = present[pl.ds(y, 1), :] == 1
        left = left_unit[pl.ds(start, channels), :].astype(jnp.float32)
        left = jnp.where(held, left, 0.0).astype(jnp.bfloat16)
        product = lax.dot_general(
            left, strip, (((0,), (0,)), ((), ())), preferred_element_type=jnp.float32
        )
        skewed = pltpu.roll(product, count + 1, 1, stride=1, stride_axis=0)
        cost[y] = 1.0 - skewed[:, :DISPARITIES]
        return 0

    lax.fori_loop(0, rows, match, 0)

    pl.when(has_up)(lambda: row_copy(-1).wait_send())
    pl.when(has_down)(lambda: row_copy(1).wait_send())
    pl.when(has_left)(lambda: col_copy(-1).wait_send())
    pl.when(has_right)(lambda: col_copy(1).wait_send())
    for distance in range(1, far + 1):
        pl.when(me + distance < col_size)(lambda distance=distance: unit_copy(distance).wait_send())


def cost_call(images, taps, biases, present, shift):
    rows, channels, count = images.shape[1:]
    layers_total = taps.shape[0]
    tall = rows + 2 * layers_total
    far = (3 * count + DISPARITIES - 2) // count
    taps = jnp.transpose(taps, (0, 3, 1, 2, 4)).reshape(layers_total, channels, 9 * channels)
    vmem = pl.BlockSpec(memory_space=pltpu.VMEM)
    halo = pltpu.VMEM((2, layers_total, channels, count), jnp.bfloat16)
    edge = pltpu.VMEM((2, channels, count), jnp.bfloat16)
    stack = pltpu.VMEM((tall * 3 * channels, 2 * count), jnp.bfloat16)
    return pl.pallas_call(
        functools.partial(
            cost_kernel, lax.axis_size("row"), lax.axis_size("col"), layers_total
        ),
        out_shape=jax.ShapeDtypeStruct((rows, count, DISPARITIES), jnp.float32),
        in_specs=[vmem, vmem, vmem, vmem, pl.BlockSpec(memory_space=pltpu.SMEM)],
        out_specs=vmem,
        scratch_shapes=[
            halo,
            halo,
            edge,
            edge,
            edge,
            stack,
            stack,
            pltpu.VMEM((rows * channels, count), jnp.bfloat16),
            pltpu.VMEM((far + 1, rows * channels, count), jnp.bfloat16),
            pltpu.SemaphoreType.DMA((2,)),
            pltpu.SemaphoreType.DMA((2,)),
            pltpu.SemaphoreType.DMA((2,)),
            pltpu.SemaphoreType.DMA((2,)),
            pltpu.SemaphoreType.DMA((far + 1,)),
            pltpu.SemaphoreType.DMA((far + 1,)),
        ],
        compiler_params=pltpu.CompilerParams(
            collective_id=1, has_side_effects=True, vmem_limit_bytes=60 * 1024 * 1024
        ),
        name="matching_cost",
    )(images, taps, biases[:, :, None], present, shift)


def per_device(
    stereo_neuron_outputs,
    filter_tap_coefficients,
    filter_stack_intercepts,
    reference_picture_present,
    tile_shift_amounts,
    smoothness_charges,
):
    cost = cost_call(
        stereo_neuron_outputs,
        filter_tap_coefficients,
        filter_stack_intercepts,
        reference_picture_present,
        tile_shift_amounts,
    )
    across, down = paths_call(cost, smoothness_charges)
    down = down.reshape(lax.axis_size("row"), cost.shape[0], -1, DISPARITIES)
    down = jnp.swapaxes(down.astype(jnp.float32), 0, 1).reshape(cost.shape)
    return down + jnp.swapaxes(across, 0, 1)


def solution(mesh):
    return jax.shard_map(
        per_device,
        mesh=mesh,
        in_specs=(P(None, "row", None, "col"), P(), P(), P("row", "col"), P("row", "col"), P()),
        out_specs=P("row", "col", None),
        check_vma=False,
    )
```

```python
import functools

import jax
import jax.numpy as jnp
from jax import lax
from jax.experimental import pallas as pl
from jax.experimental.pallas import tpu as pltpu
from jax.sharding import PartitionSpec as P

DISPARITIES = 128
SUB = 8
PARTS = DISPARITIES // SUB
MESH = pl.DeviceIdType.MESH


def order_matrix():
    row = lax.broadcasted_iota(jnp.int32, (DISPARITIES, DISPARITIES), 0)
    lane = lax.broadcasted_iota(jnp.int32, (DISPARITIES, DISPARITIES), 1)
    return jnp.where(lane == (row % SUB) * PARTS + row // SUB, 1.0, 0.0).astype(jnp.bfloat16)


def turned(value, order):
    return lax.dot_general(
        order,
        value.astype(jnp.bfloat16),
        (((1,), (1,)), ((), ())),
        preferred_element_type=jnp.float32,
    )


def ordered(value, order):
    return jnp.dot(value, order, preferred_element_type=jnp.float32)


def pieces_of(value):
    return [value[v * SUB : (v + 1) * SUB] for v in range(PARTS)]


def smallest(state):
    level = list(state)
    while len(level) > 1:
        level = [jnp.minimum(level[2 * i], level[2 * i + 1]) for i in range(len(level) // 2)]
    least = level[0]
    for step in (4, 2, 1):
        least = jnp.minimum(least, pltpu.roll(least, step, 0))
    return least


def step_once(state, cost, p1, p2, first_sub, last_sub):
    lifted = [s + p1 for s in state]
    below = jnp.where(first_sub, jnp.inf, pltpu.roll(lifted[-1], 1, 0))
    above = jnp.where(last_sub, jnp.inf, pltpu.roll(lifted[0], SUB - 1, 0))
    near = [below] + lifted + [above]
    least = smallest(state)
    jump = least + p2
    fresh = [
        cost[v]
        + jnp.minimum(jnp.minimum(state[v], jnp.minimum(near[v], near[v + 2])), jump)
        for v in range(PARTS)
    ]
    return fresh, least


def walk(slots, out, leasts, count, state, charges, at):
    sub = lax.broadcasted_iota(jnp.int32, (SUB, SUB), 0)
    first_sub, last_sub = sub == 0, sub == SUB - 1
    p1 = charges[0].astype(jnp.float32) / 64.0
    p2 = charges[1].astype(jnp.float32) / 64.0

    def body(turn, carry):
        state, least = list(carry[0]), carry[1]
        for k in range(8):
            t = at(turn * 8 + k)
            state, least = step_once(state, pieces_of(slots[t]), p1, p2, first_sub, last_sub)
            leasts[t] = least
            for v in range(PARTS):
                out[t, v * SUB : (v + 1) * SUB, :] = state[v]
        return tuple(state), least

    start = (tuple(state), jnp.zeros((SUB, SUB), jnp.float32))
    return lax.fori_loop(0, count // 8, body, start)


def layer(walked, leasts, t):
    least = leasts[t]
    return jnp.concatenate([piece - least for piece in pieces_of(walked[t])], axis=0).T


BLOCK = 16
OFFSETS = 2 * BLOCK + 1
TABLE = 5 * SUB + 2 * BLOCK


def row_paths(came, back, charges, way, order, costs, table, turned_table, states):
    tiles = came.shape[0]
    sub = lax.broadcasted_iota(jnp.int32, (SUB, DISPARITIES), 0)
    first_sub, last_sub = sub == 0, sub == SUB - 1
    p1 = charges[0].astype(jnp.float32) / 64.0
    p2 = charges[1].astype(jnp.float32) / 64.0
    middle = DISPARITIES

    def at(n):
        return jnp.where(way == 0, n, BLOCK - 1 - n)

    def take(pair, _):
        start = pl.multiple_of(pair * 2 * SUB, 2 * SUB)
        parts = [came[c, pl.ds(start, 2 * SUB), :].astype(jnp.float32) for c in range(tiles)]
        for half in range(2):
            rows = [part[half * SUB : (half + 1) * SUB] for part in parts]
            value = turned(jnp.concatenate(rows, axis=0), order)
            for v, piece in enumerate(pieces_of(value)):
                t = pair * 2 + half
                lower = jnp.where(first_sub, jnp.inf, pltpu.roll(piece, 1, 0))
                upper = jnp.where(last_sub, jnp.inf, pltpu.roll(piece, SUB - 1, 0))
                costs[t, v * SUB : (v + 1) * SUB, :] = lower
                costs[t, middle + v * SUB : middle + (v + 1) * SUB, :] = piece
                costs[t, 2 * middle + v * SUB : 2 * middle + (v + 1) * SUB, :] = upper
        return 0

    lax.fori_loop(0, BLOCK // 2, take, 0)

    def keep(index, v, value):
        table[index, pl.ds(pl.multiple_of(v * SUB, SUB), SUB), :] = value

    def no_jump(v, _):
        paths = {0: None}
        for n in range(BLOCK):
            t = at(n)
            fresh = {}
            for o in range(-n - 1, n + 2):
                near = [paths[q] for q in (o - 1, o + 1) if q in paths]
                start = pl.multiple_of((PARTS + v + o) * SUB, SUB)
                cost = costs[t, pl.ds(start, SUB), :]
                if n == 0:
                    fresh[o] = cost if o == 0 else cost + p1
                    continue
                best = near[0] if len(near) == 1 else jnp.minimum(near[0], near[1])
                best = best + p1
                if o in paths:
                    best = jnp.minimum(paths[o], best)
                fresh[o] = cost + best
            paths = fresh
            if n < BLOCK - 1:
                level = list(paths.values())
                while len(level) > 1:
                    rest = level[len(level) // 2 * 2 :]
                    level = [
                        jnp.minimum(level[2 * i], level[2 * i + 1]) for i in range(len(level) // 2)
                    ] + rest
                keep(5 * SUB + n + 1, v, level[0])
        for o in range(-BLOCK, BLOCK + 1):
            keep(BLOCK + o, v, paths[o])
        for index in range(OFFSETS, 5 * SUB):
            keep(index, v, jnp.full((SUB, DISPARITIES), jnp.inf, jnp.float32))
        keep(5 * SUB, v, jnp.zeros((SUB, DISPARITIES), jnp.float32))
        return 0

    lax.fori_loop(0, PARTS, no_jump, 0)

    def costs_of(n):
        t = at(n)
        return [costs[t, middle + v * SUB : middle + (v + 1) * SUB, :] for v in range(PARTS)]

    def jumped(first, _):
        def one(n, state):
            return tuple(step_once(list(state), costs_of(n), p1, p2, first_sub, last_sub)[0])

        state = lax.fori_loop(first + 1, BLOCK, one, tuple(costs_of(first)))
        for v in range(PARTS):
            table[5 * SUB + BLOCK + first, v * SUB : (v + 1) * SUB, :] = state[v] + p2
        return 0

    lax.fori_loop(0, BLOCK, jumped, 0)

    def turn(group, _):
        for k in range(4):
            turned_table[group * 4 + k] = table[group * 4 + k].T
        return 0

    lax.fori_loop(0, TABLE // 4, turn, 0)
    lane = lax.broadcasted_iota(jnp.int32, (SUB, DISPARITIES), 1)
    natural = (lane % PARTS) * SUB + lane // PARTS

    def sort(group, _):
        for k in range(8):
            for v in range(PARTS):
                piece = turned_table[group * 8 + k, v * SUB : (v + 1) * SUB, :]
                turned_table[group * 8 + k, v * SUB : (v + 1) * SUB, :] = jnp.take_along_axis(
                    piece, natural, axis=1
                )
        return 0

    lax.fori_loop(0, TABLE // 8, sort, 0)

    def apply(turn_of, state):
        for k in range(SUB):
            n = turn_of * SUB + k
            b = jnp.where(way == 0, n, DISPARITIES - 1 - n)
            states[pl.ds(b, 1), :] = state[:1]
            found = []
            for g in range(5):
                term = state + turned_table[g * SUB : (g + 1) * SUB, b, :]
                amount = (g * SUB - BLOCK) % DISPARITIES
                found.append(pltpu.roll(term, amount, 1, stride=1, stride_axis=0))
            for g in range(2):
                start = 5 * SUB + g * SUB
                least = jnp.min(
                    state + turned_table[start : start + SUB, b, :], axis=1, keepdims=True
                )
                start = start + BLOCK
                found.append(least + turned_table[start : start + SUB, b, :])
            while len(found) > 1:
                rest = found[len(found) // 2 * 2 :]
                found = [
                    jnp.minimum(found[2 * i], found[2 * i + 1]) for i in range(len(found) // 2)
                ] + rest
            state = found[0]
            for step in (4, 2, 1):
                state = jnp.minimum(state, pltpu.roll(state, step, 0))
        return state - jnp.min(state, axis=1, keepdims=True)

    lax.fori_loop(
        0, DISPARITIES // SUB, apply, jnp.zeros((SUB, DISPARITIES), jnp.float32)
    )
    before = states[...]
    before = before - jnp.min(before, axis=1, keepdims=True)
    high = before.astype(jnp.bfloat16)
    rest = before - high.astype(jnp.float32)
    state = pieces_of(turned(high, order) + turned(rest, order))

    def inside(pair, state):
        state = list(state)
        results = []
        for k in range(2):
            state, least = step_once(
                state, costs_of(pair * 2 + k), p1, p2, first_sub, last_sub
            )
            value = jnp.concatenate([piece - least for piece in state], axis=0).T
            results.append(ordered(value.astype(jnp.bfloat16), order))
        low = jnp.where(way == 0, results[0], results[1])
        top = jnp.where(way == 0, results[1], results[0])
        start = jnp.where(way == 0, pair, BLOCK // 2 - 1 - pair) * 2 * SUB
        start = pl.multiple_of(start, 2 * SUB)
        for c in range(tiles):
            rows = slice(c * SUB, (c + 1) * SUB)
            back[c, pl.ds(start, 2 * SUB), :] = jnp.concatenate(
                [low[rows], top[rows]], axis=0
            ).astype(jnp.bfloat16)
        return tuple(state)

    lax.fori_loop(0, BLOCK // 2, inside, tuple(state))


def half_turn(value):
    return pltpu.roll(value, SUB // 2, 0)


def paths_kernel(
    row_size,
    col_size,
    cost,
    charges,
    out_across,
    out_down,
    strips,
    strip_leasts,
    costs,
    table,
    turned_table,
    states,
    row_sent,
    row_came,
    row_back,
    row_return,
    sent,
    came,
    back_out,
    back_in,
    row_send,
    row_recv,
    return_send,
    return_recv,
    sent_sem,
    came_sem,
    back_send,
    back_recv,
):
    rows = cost.shape[0]
    height = strips.shape[0]
    row = lax.axis_index("row")
    me = lax.axis_index("col")
    low = lax.broadcasted_iota(jnp.int32, (SUB, DISPARITIES), 0) < SUB // 2
    order = order_matrix()

    barrier = pltpu.get_barrier_semaphore()
    for axis, mine, size in (("row", row, row_size), ("col", me, col_size)):

        def greet(j, _, axis=axis, mine=mine, size=size):
            peer = lax.rem(mine + j, size)
            pl.semaphore_signal(barrier, inc=1, device_id={axis: peer}, device_id_type=MESH)
            return 0

        lax.fori_loop(1, size, greet, 0)

    def exchange(axis, source, target, sems, what, pick=lambda peer: peer):
        mine, size = (row, row_size) if axis == "row" else (me, col_size)
        send_sem, recv_sem = sems

        def copy(peer, slot):
            return pltpu.make_async_remote_copy(
                src_ref=source.at[pick(peer)],
                dst_ref=target.at[slot],
                send_sem=send_sem.at[peer],
                recv_sem=recv_sem.at[slot],
                device_id={axis: peer},
                device_id_type=MESH,
            )

        def body(j, _):
            peer = lax.rem(mine + j, size)
            if what == "start":
                copy(peer, mine).start()
            elif what == "sent":
                copy(peer, mine).wait_send()
            else:
                copy(peer, peer).wait_recv()
            return 0

        lax.fori_loop(1, size, body, 0)
        if what == "start":
            target[mine] = source[pick(mine)]

    out_rows = ("col", row_sent, row_came, (row_send, row_recv))
    back_rows = ("col", row_back, row_return, (return_send, return_recv))
    out_strips = ("row", sent, came, (sent_sem, came_sem))
    back_strips = ("row", back_out, back_in, (back_send, back_recv))

    def row_of(peer):
        return lax.rem(peer, rows)

    def group(y, _):
        row_sent[y] = ordered(order, cost[y].astype(jnp.bfloat16)).astype(jnp.bfloat16)
        return 0

    lax.fori_loop(0, rows, group, 0)

    def cut(tile, _):
        start = pl.multiple_of(tile * SUB, SUB)
        rows = [cost[y, pl.ds(start, SUB), :] for y in range(SUB)]
        even = [jnp.where(low, rows[y], half_turn(rows[y + 1])) for y in range(0, SUB, 2)]
        odd = [jnp.where(low, half_turn(rows[y]), rows[y + 1]) for y in range(0, SUB, 2)]
        sent[2 * tile] = jnp.concatenate(even, axis=0).astype(jnp.bfloat16)
        sent[2 * tile + 1] = jnp.concatenate(odd, axis=0).astype(jnp.bfloat16)
        return 0

    lax.fori_loop(0, row_size // 2, cut, 0)
    pl.semaphore_wait(barrier, row_size + col_size - 2)
    exchange(*out_rows, "start", row_of)
    exchange(*out_strips, "start")

    def vertical_in():
        exchange(*out_strips, "came")

        def body(source, _):
            near = came[source].astype(jnp.float32)
            far = came[row_size - 1 - source].astype(jnp.float32)
            for q in range(SUB // 2):
                a = near[q * SUB : (q + 1) * SUB]
                b = far[(3 - q) * SUB : (4 - q) * SUB]
                first = jnp.where(low, a, b)
                second = half_turn(jnp.where(low, b, a))
                t = source * SUB + 2 * q
                strips[t] = turned(first, order)
                strips[t + 1] = turned(second, order)
            return 0

        lax.fori_loop(0, row_size, body, 0)

    def vertical_walk():
        zero = [jnp.zeros((SUB, SUB), jnp.float32) for _ in range(PARTS)]
        walk(strips, strips, strip_leasts, height, zero, charges, lambda t: t)

    def vertical_out():
        def body(near, _):
            far = row_size - 1 - near
            one = [layer(strips, strip_leasts, near * SUB + y) for y in range(SUB)]
            other = [layer(strips, strip_leasts, far * SUB + y) for y in range(SUB)]
            total = [one[y] + half_turn(other[SUB - 1 - y]) for y in range(SUB)]
            up = [jnp.where(low, total[y], half_turn(total[y + 1])) for y in (0, 2, 4, 6)]
            down = [jnp.where(low, half_turn(total[y + 1]), total[y]) for y in (6, 4, 2, 0)]
            both = jnp.concatenate(up + down, axis=0).astype(jnp.bfloat16)
            both = ordered(both, order).astype(jnp.bfloat16)
            half = SUB * SUB // 2
            back_out[near] = both[:half]
            back_out[far] = both[half:]
            return 0

        lax.fori_loop(0, row_size // 2, body, 0)
        exchange(*back_strips, "start")

    exchange(*out_rows, "came", row_of)
    way = me // rows
    row_paths(row_came, row_back, charges, way, order, costs, table, turned_table, states)
    exchange(*back_rows, "start")
    vertical_in()
    vertical_walk()
    vertical_out()
    exchange(*back_rows, "came")
    place = lax.broadcasted_iota(jnp.int32, (DISPARITIES, DISPARITIES), 0)
    lane = lax.broadcasted_iota(jnp.int32, (DISPARITIES, DISPARITIES), 1)
    spread = place == (lane % SUB) * PARTS + lane // SUB
    spread = jnp.where(spread, 1.0, 0.0).astype(jnp.bfloat16)

    def gather(y, _):
        out_across[y] = ordered(spread, row_return[y]) + ordered(spread, row_return[y + rows])
        return 0

    lax.fori_loop(0, rows, gather, 0)
    exchange(*back_strips, "came")

    def hand_over(j, _):
        out_down[j] = back_in[j]
        return 0

    lax.fori_loop(0, row_size, hand_over, 0)
    exchange(*out_rows, "sent", row_of)
    exchange(*back_rows, "sent")
    exchange(*out_strips, "sent")
    exchange(*back_strips, "sent")


def paths_call(cost, charges):
    rows, count, _ = cost.shape
    row_size, col_size = lax.axis_size("row"), lax.axis_size("col")
    width = count // row_size
    block = (row_size, rows * width, DISPARITIES)
    vmem = pl.BlockSpec(memory_space=pltpu.VMEM)
    return pl.pallas_call(
        functools.partial(paths_kernel, row_size, col_size),
        out_shape=(
            jax.ShapeDtypeStruct(cost.shape, jnp.float32),
            jax.ShapeDtypeStruct(block, jnp.bfloat16),
        ),
        in_specs=[vmem, pl.BlockSpec(memory_space=pltpu.SMEM)],
        out_specs=(vmem, vmem),
        scratch_shapes=[
            pltpu.VMEM((rows * row_size, DISPARITIES, SUB), jnp.float32),
            pltpu.VMEM((rows * row_size, SUB, SUB), jnp.float32),
            pltpu.VMEM((BLOCK, 3 * DISPARITIES, DISPARITIES), jnp.float32),
            pltpu.VMEM((TABLE, DISPARITIES, DISPARITIES), jnp.float32),
            pltpu.VMEM((TABLE, DISPARITIES, DISPARITIES), jnp.float32),
            pltpu.VMEM((DISPARITIES, DISPARITIES), jnp.float32),
            pltpu.VMEM((rows, count, DISPARITIES), jnp.bfloat16),
            pltpu.VMEM((col_size, count, DISPARITIES), jnp.bfloat16),
            pltpu.VMEM((col_size, count, DISPARITIES), jnp.bfloat16),
            pltpu.VMEM((col_size, count, DISPARITIES), jnp.bfloat16),
            pltpu.VMEM(block, jnp.bfloat16),
            pltpu.VMEM(block, jnp.bfloat16),
            pltpu.VMEM(block, jnp.bfloat16),
            pltpu.VMEM(block, jnp.bfloat16),
            pltpu.SemaphoreType.DMA((col_size,)),
            pltpu.SemaphoreType.DMA((col_size,)),
            pltpu.SemaphoreType.DMA((col_size,)),
            pltpu.SemaphoreType.DMA((col_size,)),
            pltpu.SemaphoreType.DMA((row_size,)),
            pltpu.SemaphoreType.DMA((row_size,)),
            pltpu.SemaphoreType.DMA((row_size,)),
            pltpu.SemaphoreType.DMA((row_size,)),
        ],
        compiler_params=pltpu.CompilerParams(
            collective_id=0, has_side_effects=True, vmem_limit_bytes=60 * 1024 * 1024
        ),
        name="four_paths",
    )(cost, charges)


def outer_kernel_sizes(images, halo):
    rows, channels, count = images.shape[1:]
    return rows, channels, count, rows + 2 * halo


def cost_kernel(
    row_size,
    col_size,
    layers_total,
    images,
    taps,
    biases,
    present,
    shift,
    cost,
    above,
    below,
    packed,
    from_left,
    from_right,
    stack_a,
    stack_b,
    left_unit,
    reach_unit,
    rows_send,
    rows_recv,
    cols_send,
    cols_recv,
    unit_send,
    unit_recv,
):
    rows, channels, count, tall = outer_kernel_sizes(images, layers_total)
    far = reach_unit.shape[0] - 1
    deep = 3 * channels
    row, me = lax.axis_index("row"), lax.axis_index("col")
    has_up, has_down = row > 0, row < row_size - 1
    has_left, has_right = me > 0, me < col_size - 1

    barrier = pltpu.get_barrier_semaphore()
    expected = jnp.where(has_up, 1, 0) + jnp.where(has_down, 1, 0)
    for there, step in ((has_up, -1), (has_down, 1)):

        @pl.when(there)
        def _(step=step):
            pl.semaphore_signal(barrier, inc=1, device_id={"row": row + step}, device_id_type=MESH)

    for distance in range(1, far + 1):
        for there, step in ((me >= distance, -distance), (me + distance < col_size, distance)):
            expected = expected + jnp.where(there, 1, 0)

            @pl.when(there)
            def _(step=step):
                pl.semaphore_signal(
                    barrier, inc=1, device_id={"col": me + step}, device_id_type=MESH
                )

    pl.semaphore_wait(barrier, expected)

    def row_copy(step):
        index = 0 if step < 0 else 1
        first = 0 if step < 0 else rows - layers_total
        return pltpu.make_async_remote_copy(
            src_ref=images.at[:, first : first + layers_total],
            dst_ref=below if step < 0 else above,
            send_sem=rows_send.at[index],
            recv_sem=rows_recv.at[index],
            device_id={"row": row + step},
            device_id_type=MESH,
        )

    def col_copy(step):
        index = 0 if step < 0 else 1
        return pltpu.make_async_remote_copy(
            src_ref=packed,
            dst_ref=from_right if step < 0 else from_left,
            send_sem=cols_send.at[index],
            recv_sem=cols_recv.at[index],
            device_id={"col": me + step},
            device_id_type=MESH,
        )

    def unit_copy(distance):
        return pltpu.make_async_remote_copy(
            src_ref=reach_unit.at[0],
            dst_ref=reach_unit.at[distance],
            send_sem=unit_send.at[distance],
            recv_sem=unit_recv.at[distance],
            device_id={"col": me + distance},
            device_id_type=MESH,
        )

    pl.when(has_up)(lambda: row_copy(-1).start())
    pl.when(has_down)(lambda: row_copy(1).start())

    @pl.when(jnp.logical_not(has_up))
    def _():
        above[...] = jnp.zeros_like(above)

    @pl.when(jnp.logical_not(has_down))
    def _():
        below[...] = jnp.zeros_like(below)

    pl.when(has_down)(lambda: row_copy(-1).wait_recv())
    pl.when(has_up)(lambda: row_copy(1).wait_recv())

    def row_of(image, k):
        if k < layers_total:
            return above[image, k]
        if k < layers_total + rows:
            return images[image, k - layers_total]
        return below[image, k - layers_total - rows]

    pick_row = lax.broadcasted_iota(jnp.int32, (count, count), 0)
    pick_lane = lax.broadcasted_iota(jnp.int32, (count, count), 1)

    def one_hot(where):
        return jnp.where(where, 1.0, 0.0).astype(jnp.bfloat16)

    for image in range(2):
        total = None
        for k in range(tall):
            slot = pick_lane - k * SUB
            head = jnp.logical_and(slot >= 0, jnp.logical_and(slot < 3, pick_row == slot))
            tail = jnp.logical_and(
                slot >= 3, jnp.logical_and(slot < 6, pick_row == slot + count - 6)
            )
            pick = one_hot(jnp.logical_or(head, tail))
            term = jnp.dot(row_of(image, k), pick, preferred_element_type=jnp.float32)
            total = term if total is None else total + term
        packed[image] = total.astype(jnp.bfloat16)

    pl.when(has_left)(lambda: col_copy(-1).start())
    pl.when(has_right)(lambda: col_copy(1).start())

    @pl.when(jnp.logical_not(has_left))
    def _():
        from_left[...] = jnp.zeros_like(from_left)

    @pl.when(jnp.logical_not(has_right))
    def _():
        from_right[...] = jnp.zeros_like(from_right)

    for distance in range(1, far + 1):

        @pl.when(me < distance)
        def _(distance=distance):
            reach_unit[distance] = jnp.zeros(reach_unit.shape[1:], reach_unit.dtype)

    pl.when(has_right)(lambda: col_copy(-1).wait_recv())
    pl.when(has_left)(lambda: col_copy(1).wait_recv())

    lanes = lax.broadcasted_iota(jnp.int32, (channels, 2 * count), 1)
    side = jnp.where(lanes < count + count // 2, has_right.astype(jnp.int32), has_left.astype(jnp.int32))
    keep_lane = jnp.where(lanes < count, 1, side)

    def put(stack, k, value):
        base = k * deep if isinstance(k, int) else pl.multiple_of(k * deep, deep)
        for b, turn in enumerate((1, 0, 2 * count - 1)):
            moved = pltpu.roll(value, turn, 1) if turn else value
            stack[pl.ds(base + b * channels, channels), :] = moved.astype(jnp.bfloat16)

    def features(image):
        for k in range(tall):
            slot_left = pick_row - k * SUB - 3 == pick_lane - (count - 3)
            slot_left = jnp.logical_and(slot_left, pick_lane >= count - 3)
            slot_right = jnp.logical_and(pick_row - k * SUB == pick_lane, pick_lane < 3)
            edge = jnp.dot(
                from_left[image], one_hot(slot_left), preferred_element_type=jnp.float32
            ) + jnp.dot(
                from_right[image], one_hot(slot_right), preferred_element_type=jnp.float32
            )
            put(
                stack_a,
                k,
                jnp.concatenate([row_of(image, k).astype(jnp.float32), edge], axis=1),
            )
        source, target = stack_a, stack_b
        for layer_number in range(layers_total):
            margin = layers_total - 1 - layer_number
            bias = biases[layer_number]
            weights = taps[layer_number]
            last = margin == 0

            def body(pair, _):
                for k in range(2):
                    y = pair * 2 + k
                    window = source[pl.ds(pl.multiple_of(y * deep, deep), 3 * deep), :]
                    if last:
                        window = window[:, :count]
                    value = jnp.dot(weights, window, preferred_element_type=jnp.float32) + bias
                    if last:
                        square = jnp.sum(value * value, axis=0, keepdims=True)
                        unit = (value * lax.rsqrt(square + 1e-06)).astype(jnp.bfloat16)
                        start = pl.multiple_of(y * channels, channels)
                        if image == 1:
                            reach_unit[0, pl.ds(start, channels), :] = unit
                        else:
                            left_unit[pl.ds(start, channels), :] = unit
                    else:
                        keep = jnp.logical_and(
                            jnp.logical_or(y >= margin, has_up),
                            jnp.logical_or(y < margin + rows, has_down),
                        )
                        value = jnp.where(
                            keep_lane * keep.astype(jnp.int32) == 1, jnp.maximum(value, 0.0), 0.0
                        )
                        put(target, y, value)
                return 0

            lax.fori_loop(0, (rows + 2 * margin) // 2, body, 0)
            source, target = target, source

    features(1)
    for distance in range(1, far + 1):
        pl.when(me + distance < col_size)(lambda distance=distance: unit_copy(distance).start())
    features(0)
    for distance in range(1, far + 1):
        pl.when(me >= distance)(lambda distance=distance: unit_copy(distance).wait_recv())

    wide = (far + 1) * count
    place = lax.broadcasted_iota(jnp.int32, (wide, 2 * count), 0)
    lane = lax.broadcasted_iota(jnp.int32, (wide, 2 * count), 1)
    choose = one_hot(place + lane == wide - 1 - shift[0, 0])

    def match(y, _):
        start = pl.multiple_of(y * channels, channels)
        reach = jnp.concatenate(
            [reach_unit[distance, pl.ds(start, channels), :] for distance in range(far, -1, -1)],
            axis=1,
        )
        strip = jnp.dot(reach, choose, preferred_element_type=jnp.float32).astype(jnp.bfloat16)
        held = present[pl.ds(y, 1), :] == 1
        left = left_unit[pl.ds(start, channels), :].astype(jnp.float32)
        left = jnp.where(held, left, 0.0).astype(jnp.bfloat16)
        product = lax.dot_general(
            left, strip, (((0,), (0,)), ((), ())), preferred_element_type=jnp.float32
        )
        skewed = pltpu.roll(product, count + 1, 1, stride=1, stride_axis=0)
        cost[y] = 1.0 - skewed[:, :DISPARITIES]
        return 0

    lax.fori_loop(0, rows, match, 0)

    pl.when(has_up)(lambda: row_copy(-1).wait_send())
    pl.when(has_down)(lambda: row_copy(1).wait_send())
    pl.when(has_left)(lambda: col_copy(-1).wait_send())
    pl.when(has_right)(lambda: col_copy(1).wait_send())
    for distance in range(1, far + 1):
        pl.when(me + distance < col_size)(lambda distance=distance: unit_copy(distance).wait_send())


def cost_call(images, taps, biases, present, shift):
    rows, channels, count = images.shape[1:]
    layers_total = taps.shape[0]
    tall = rows + 2 * layers_total
    far = (3 * count + DISPARITIES - 2) // count
    taps = jnp.transpose(taps, (0, 3, 1, 2, 4)).reshape(layers_total, channels, 9 * channels)
    vmem = pl.BlockSpec(memory_space=pltpu.VMEM)
    halo = pltpu.VMEM((2, layers_total, channels, count), jnp.bfloat16)
    edge = pltpu.VMEM((2, channels, count), jnp.bfloat16)
    stack = pltpu.VMEM((tall * 3 * channels, 2 * count), jnp.bfloat16)
    return pl.pallas_call(
        functools.partial(
            cost_kernel, lax.axis_size("row"), lax.axis_size("col"), layers_total
        ),
        out_shape=jax.ShapeDtypeStruct((rows, count, DISPARITIES), jnp.float32),
        in_specs=[vmem, vmem, vmem, vmem, pl.BlockSpec(memory_space=pltpu.SMEM)],
        out_specs=vmem,
        scratch_shapes=[
            halo,
            halo,
            edge,
            edge,
            edge,
            stack,
            stack,
            pltpu.VMEM((rows * channels, count), jnp.bfloat16),
            pltpu.VMEM((far + 1, rows * channels, count), jnp.bfloat16),
            pltpu.SemaphoreType.DMA((2,)),
            pltpu.SemaphoreType.DMA((2,)),
            pltpu.SemaphoreType.DMA((2,)),
            pltpu.SemaphoreType.DMA((2,)),
            pltpu.SemaphoreType.DMA((far + 1,)),
            pltpu.SemaphoreType.DMA((far + 1,)),
        ],
        compiler_params=pltpu.CompilerParams(
            collective_id=1, has_side_effects=True, vmem_limit_bytes=60 * 1024 * 1024
        ),
        name="matching_cost",
    )(images, taps, biases[:, :, None], present, shift)


def per_device(
    stereo_neuron_outputs,
    filter_tap_coefficients,
    filter_stack_intercepts,
    reference_picture_present,
    tile_shift_amounts,
    smoothness_charges,
):
    cost = cost_call(
        stereo_neuron_outputs,
        filter_tap_coefficients,
        filter_stack_intercepts,
        reference_picture_present,
        tile_shift_amounts,
    )
    across, down = paths_call(cost, smoothness_charges)
    down = down.reshape(lax.axis_size("row"), cost.shape[0], -1, DISPARITIES)
    down = jnp.swapaxes(down.astype(jnp.float32), 0, 1).reshape(cost.shape)
    return down + across


def solution(mesh):
    return jax.shard_map(
        per_device,
        mesh=mesh,
        in_specs=(P(None, "row", None, "col"), P(), P(), P("row", "col"), P("row", "col"), P()),
        out_specs=P("row", "col", None),
        check_vma=False,
    )
```

```python
import functools

import jax
import jax.numpy as jnp
from jax import lax
from jax.experimental import pallas as pl
from jax.experimental.pallas import tpu as pltpu
from jax.sharding import PartitionSpec as P

DISPARITIES = 128
SUB = 8
PARTS = DISPARITIES // SUB
MESH = pl.DeviceIdType.MESH


def order_matrix():
    row = lax.broadcasted_iota(jnp.int32, (DISPARITIES, DISPARITIES), 0)
    lane = lax.broadcasted_iota(jnp.int32, (DISPARITIES, DISPARITIES), 1)
    return jnp.where(lane == (row % SUB) * PARTS + row // SUB, 1.0, 0.0).astype(jnp.bfloat16)


def turned(value, order):
    return lax.dot_general(
        order,
        value.astype(jnp.bfloat16),
        (((1,), (1,)), ((), ())),
        preferred_element_type=jnp.float32,
    )


def ordered(value, order):
    return jnp.dot(value, order, preferred_element_type=jnp.float32)


def pieces_of(value):
    return [value[v * SUB : (v + 1) * SUB] for v in range(PARTS)]


def smallest(state):
    level = list(state)
    while len(level) > 1:
        level = [jnp.minimum(level[2 * i], level[2 * i + 1]) for i in range(len(level) // 2)]
    least = level[0]
    for step in (4, 2, 1):
        least = jnp.minimum(least, pltpu.roll(least, step, 0))
    return least


def step_once(state, cost, p1, p2, first_sub, last_sub):
    lifted = [s + p1 for s in state]
    below = jnp.where(first_sub, jnp.inf, pltpu.roll(lifted[-1], 1, 0))
    above = jnp.where(last_sub, jnp.inf, pltpu.roll(lifted[0], SUB - 1, 0))
    near = [below] + lifted + [above]
    least = smallest(state)
    jump = least + p2
    fresh = [
        cost[v]
        + jnp.minimum(jnp.minimum(state[v], jnp.minimum(near[v], near[v + 2])), jump)
        for v in range(PARTS)
    ]
    return fresh, least


def walk(slots, out, leasts, count, state, charges, at):
    sub = lax.broadcasted_iota(jnp.int32, (SUB, SUB), 0)
    first_sub, last_sub = sub == 0, sub == SUB - 1
    p1 = charges[0].astype(jnp.float32) / 64.0
    p2 = charges[1].astype(jnp.float32) / 64.0

    def body(turn, carry):
        state, least = list(carry[0]), carry[1]
        for k in range(8):
            t = at(turn * 8 + k)
            state, least = step_once(state, pieces_of(slots[t]), p1, p2, first_sub, last_sub)
            leasts[t] = least
            for v in range(PARTS):
                out[t, v * SUB : (v + 1) * SUB, :] = state[v]
        return tuple(state), least

    start = (tuple(state), jnp.zeros((SUB, SUB), jnp.float32))
    return lax.fori_loop(0, count // 8, body, start)


def layer(walked, leasts, t):
    least = leasts[t]
    return jnp.concatenate([piece - least for piece in pieces_of(walked[t])], axis=0).T


BLOCK = 16
OFFSETS = 2 * BLOCK + 1
TABLE = 5 * SUB + 2 * BLOCK


def row_paths(came, back, charges, way, order, costs, table, turned_table, states):
    tiles = came.shape[0]
    sub = lax.broadcasted_iota(jnp.int32, (SUB, DISPARITIES), 0)
    first_sub, last_sub = sub == 0, sub == SUB - 1
    p1 = charges[0].astype(jnp.float32) / 64.0
    p2 = charges[1].astype(jnp.float32) / 64.0
    middle = DISPARITIES

    def at(n):
        return jnp.where(way == 0, n, BLOCK - 1 - n)

    def take(pair, _):
        start = pl.multiple_of(pair * 2 * SUB, 2 * SUB)
        parts = [came[c, pl.ds(start, 2 * SUB), :].astype(jnp.float32) for c in range(tiles)]
        for half in range(2):
            rows = [part[half * SUB : (half + 1) * SUB] for part in parts]
            value = turned(jnp.concatenate(rows, axis=0), order)
            for v, piece in enumerate(pieces_of(value)):
                t = pair * 2 + half
                lower = jnp.where(first_sub, jnp.inf, pltpu.roll(piece, 1, 0))
                upper = jnp.where(last_sub, jnp.inf, pltpu.roll(piece, SUB - 1, 0))
                costs[t, v * SUB : (v + 1) * SUB, :] = lower
                costs[t, middle + v * SUB : middle + (v + 1) * SUB, :] = piece
                costs[t, 2 * middle + v * SUB : 2 * middle + (v + 1) * SUB, :] = upper
        return 0

    lax.fori_loop(0, BLOCK // 2, take, 0)

    def keep(index, v, value):
        table[index, pl.ds(pl.multiple_of(v * SUB, SUB), SUB), :] = value

    def no_jump(v, _):
        paths = {0: None}
        for n in range(BLOCK):
            t = at(n)
            fresh = {}
            for o in range(-n - 1, n + 2):
                near = [paths[q] for q in (o - 1, o + 1) if q in paths]
                start = pl.multiple_of((PARTS + v + o) * SUB, SUB)
                cost = costs[t, pl.ds(start, SUB), :]
                if n == 0:
                    fresh[o] = cost if o == 0 else cost + p1
                    continue
                best = near[0] if len(near) == 1 else jnp.minimum(near[0], near[1])
                best = best + p1
                if o in paths:
                    best = jnp.minimum(paths[o], best)
                fresh[o] = cost + best
            paths = fresh
            if n < BLOCK - 1:
                level = list(paths.values())
                while len(level) > 1:
                    rest = level[len(level) // 2 * 2 :]
                    level = [
                        jnp.minimum(level[2 * i], level[2 * i + 1]) for i in range(len(level) // 2)
                    ] + rest
                keep(5 * SUB + n + 1, v, level[0])
        for o in range(-BLOCK, BLOCK + 1):
            keep(BLOCK + o, v, paths[o])
        for index in range(OFFSETS, 5 * SUB):
            keep(index, v, jnp.full((SUB, DISPARITIES), jnp.inf, jnp.float32))
        keep(5 * SUB, v, jnp.zeros((SUB, DISPARITIES), jnp.float32))
        return 0

    lax.fori_loop(0, PARTS, no_jump, 0)

    def costs_of(n):
        t = at(n)
        return [costs[t, middle + v * SUB : middle + (v + 1) * SUB, :] for v in range(PARTS)]

    def jumped(first, _):
        def one(n, state):
            return tuple(step_once(list(state), costs_of(n), p1, p2, first_sub, last_sub)[0])

        state = lax.fori_loop(first + 1, BLOCK, one, tuple(costs_of(first)))
        for v in range(PARTS):
            table[5 * SUB + BLOCK + first, v * SUB : (v + 1) * SUB, :] = state[v] + p2
        return 0

    lax.fori_loop(0, BLOCK, jumped, 0)

    def turn(group, _):
        for k in range(4):
            turned_table[group * 4 + k] = table[group * 4 + k].T
        return 0

    lax.fori_loop(0, TABLE // 4, turn, 0)
    lane = lax.broadcasted_iota(jnp.int32, (SUB, DISPARITIES), 1)
    natural = (lane % PARTS) * SUB + lane // PARTS

    def sort(group, _):
        for k in range(8):
            for v in range(PARTS):
                piece = turned_table[group * 8 + k, v * SUB : (v + 1) * SUB, :]
                turned_table[group * 8 + k, v * SUB : (v + 1) * SUB, :] = jnp.take_along_axis(
                    piece, natural, axis=1
                )
        return 0

    lax.fori_loop(0, TABLE // 8, sort, 0)

    def apply(turn_of, state):
        for k in range(SUB):
            n = turn_of * SUB + k
            b = jnp.where(way == 0, n, DISPARITIES - 1 - n)
            states[pl.ds(b, 1), :] = state[:1]
            found = []
            for g in range(5):
                term = state + turned_table[g * SUB : (g + 1) * SUB, b, :]
                amount = (g * SUB - BLOCK) % DISPARITIES
                found.append(pltpu.roll(term, amount, 1, stride=1, stride_axis=0))
            for g in range(2):
                start = 5 * SUB + g * SUB
                least = jnp.min(
                    state + turned_table[start : start + SUB, b, :], axis=1, keepdims=True
                )
                start = start + BLOCK
                found.append(least + turned_table[start : start + SUB, b, :])
            while len(found) > 1:
                rest = found[len(found) // 2 * 2 :]
                found = [
                    jnp.minimum(found[2 * i], found[2 * i + 1]) for i in range(len(found) // 2)
                ] + rest
            state = found[0]
            for step in (4, 2, 1):
                state = jnp.minimum(state, pltpu.roll(state, step, 0))
        return state - jnp.min(state, axis=1, keepdims=True)

    lax.fori_loop(
        0, DISPARITIES // SUB, apply, jnp.zeros((SUB, DISPARITIES), jnp.float32)
    )
    before = states[...]
    before = before - jnp.min(before, axis=1, keepdims=True)
    high = before.astype(jnp.bfloat16)
    rest = before - high.astype(jnp.float32)
    state = pieces_of(turned(high, order) + turned(rest, order))

    def inside(pair, state):
        state = list(state)
        results = []
        for k in range(2):
            state, least = step_once(
                state, costs_of(pair * 2 + k), p1, p2, first_sub, last_sub
            )
            value = jnp.concatenate([piece - least for piece in state], axis=0).T
            results.append(ordered(value.astype(jnp.bfloat16), order))
        low = jnp.where(way == 0, results[0], results[1])
        top = jnp.where(way == 0, results[1], results[0])
        start = jnp.where(way == 0, pair, BLOCK // 2 - 1 - pair) * 2 * SUB
        start = pl.multiple_of(start, 2 * SUB)
        for c in range(tiles):
            rows = slice(c * SUB, (c + 1) * SUB)
            back[c, pl.ds(start, 2 * SUB), :] = jnp.concatenate(
                [low[rows], top[rows]], axis=0
            ).astype(jnp.bfloat16)
        return tuple(state)

    lax.fori_loop(0, BLOCK // 2, inside, tuple(state))


def half_turn(value):
    return pltpu.roll(value, SUB // 2, 0)


def paths_kernel(
    row_size,
    col_size,
    cost,
    charges,
    out_across,
    out_down,
    strips,
    strip_leasts,
    costs,
    table,
    turned_table,
    states,
    row_sent,
    row_came,
    row_back,
    swapped,
    summed,
    row_return,
    sent,
    came,
    back_out,
    back_in,
    row_send,
    row_recv,
    pass_send,
    pass_recv,
    swap_send,
    swap_recv,
    return_send,
    return_recv,
    sent_sem,
    came_sem,
    back_send,
    back_recv,
):
    rows = cost.shape[0]
    height = strips.shape[0]
    row = lax.axis_index("row")
    me = lax.axis_index("col")
    low = lax.broadcasted_iota(jnp.int32, (SUB, DISPARITIES), 0) < SUB // 2
    order = order_matrix()

    barrier = pltpu.get_barrier_semaphore()
    for axis, mine, size in (("row", row, row_size), ("col", me, col_size)):

        def greet(j, _, axis=axis, mine=mine, size=size):
            peer = lax.rem(mine + j, size)
            pl.semaphore_signal(barrier, inc=1, device_id={axis: peer}, device_id_type=MESH)
            return 0

        lax.fori_loop(1, size, greet, 0)

    core = lax.rem(me, 2)
    pair, pairs = me // 2, col_size // 2
    partner = me + 1 - 2 * core

    def remote(source, target, send_sem, recv_sem, axis, peer):
        return pltpu.make_async_remote_copy(
            src_ref=source,
            dst_ref=target,
            send_sem=send_sem,
            recv_sem=recv_sem,
            device_id={axis: peer},
            device_id_type=MESH,
        )

    def rows_out(there, slot):
        peer = 2 * there + core
        return remote(
            row_sent.at[there],
            row_came.at[2 * slot + core],
            row_send.at[there],
            row_recv.at[slot],
            "col",
            peer,
        )

    def rows_pass(h, side):
        block = row_came.at[2 * h + side]
        return remote(block, block, pass_send.at[h], pass_recv.at[h], "col", partner)

    def rows_swap(h):
        source = row_back.at[2 * h + 1 - core]
        return remote(source, swapped.at[h], swap_send.at[h], swap_recv.at[h], "col", partner)

    def rows_back(there, slot):
        return remote(
            summed.at[there],
            row_return.at[slot],
            return_send.at[there],
            return_recv.at[slot],
            "col",
            2 * there + core,
        )

    def strips_out(there, slot):
        return remote(
            sent.at[there], came.at[slot], sent_sem.at[there], came_sem.at[slot], "row", there
        )

    def strips_back(there, slot):
        return remote(
            back_out.at[there],
            back_in.at[slot],
            back_send.at[there],
            back_recv.at[slot],
            "row",
            there,
        )

    def each_peer(mine, size, work):
        def body(j, _):
            work(lax.rem(mine + j, size))
            return 0

        lax.fori_loop(1, size, body, 0)

    def each(size, work):
        def body(j, _):
            work(j)
            return 0

        lax.fori_loop(0, size, body, 0)

    def group(y, _):
        row_sent[y] = ordered(order, cost[y].astype(jnp.bfloat16)).astype(jnp.bfloat16)
        return 0

    lax.fori_loop(0, rows, group, 0)

    def cut(tile, _):
        start = pl.multiple_of(tile * SUB, SUB)
        rows = [cost[y, pl.ds(start, SUB), :] for y in range(SUB)]
        even = [jnp.where(low, rows[y], half_turn(rows[y + 1])) for y in range(0, SUB, 2)]
        odd = [jnp.where(low, half_turn(rows[y]), rows[y + 1]) for y in range(0, SUB, 2)]
        sent[2 * tile] = jnp.concatenate(even, axis=0).astype(jnp.bfloat16)
        sent[2 * tile + 1] = jnp.concatenate(odd, axis=0).astype(jnp.bfloat16)
        return 0

    lax.fori_loop(0, row_size // 2, cut, 0)
    pl.semaphore_wait(barrier, row_size + col_size - 2)
    each_peer(pair, pairs, lambda there: rows_out(there, pair).start())
    row_came[me] = row_sent[pair]
    each_peer(row, row_size, lambda there: strips_out(there, row).start())
    came[row] = sent[row]

    def vertical_in():
        each_peer(row, row_size, lambda there: strips_out(there, there).wait_recv())

        def body(source, _):
            near = came[source].astype(jnp.float32)
            far = came[row_size - 1 - source].astype(jnp.float32)
            for q in range(SUB // 2):
                a = near[q * SUB : (q + 1) * SUB]
                b = far[(3 - q) * SUB : (4 - q) * SUB]
                first = jnp.where(low, a, b)
                second = half_turn(jnp.where(low, b, a))
                t = source * SUB + 2 * q
                strips[t] = turned(first, order)
                strips[t + 1] = turned(second, order)
            return 0

        lax.fori_loop(0, row_size, body, 0)

    def vertical_walk():
        zero = [jnp.zeros((SUB, SUB), jnp.float32) for _ in range(PARTS)]
        walk(strips, strips, strip_leasts, height, zero, charges, lambda t: t)

    def vertical_out():
        def send(near):
            for there in (near, row_size - 1 - near):

                @pl.when(there != row)
                def _(there=there):
                    strips_back(there, row).start()

        def body(near, _):
            pl.when(near > 0)(lambda: send(near - 1))
            far = row_size - 1 - near
            one = [layer(strips, strip_leasts, near * SUB + y) for y in range(SUB)]
            other = [layer(strips, strip_leasts, far * SUB + y) for y in range(SUB)]
            total = [one[y] + half_turn(other[SUB - 1 - y]) for y in range(SUB)]
            up = [jnp.where(low, total[y], half_turn(total[y + 1])) for y in (0, 2, 4, 6)]
            down = [jnp.where(low, half_turn(total[y + 1]), total[y]) for y in (6, 4, 2, 0)]
            both = jnp.concatenate(up + down, axis=0).astype(jnp.bfloat16)
            both = ordered(both, order).astype(jnp.bfloat16)
            half = SUB * SUB // 2
            back_out[near] = both[:half]
            back_out[far] = both[half:]
            return 0

        lax.fori_loop(0, row_size // 2, body, 0)
        send(row_size // 2 - 1)
        back_in[row] = back_out[row]

    rows_pass(pair, core).start()

    def forward(j, _):
        there = lax.rem(pair + pairs - j, pairs)
        rows_out(there, there).wait_recv()
        rows_pass(there, core).start()
        return 0

    lax.fori_loop(1, pairs, forward, 0)
    each(pairs, lambda h: rows_pass(h, 1 - core).wait_recv())
    row_paths(row_came, row_back, charges, core, order, costs, table, turned_table, states)
    each(pairs, lambda h: rows_swap(h).start())
    vertical_in()

    def add(h):
        rows_swap(h).wait_recv()
        mine = row_back[2 * h + core].astype(jnp.float32)
        summed[h] = (mine + swapped[h].astype(jnp.float32)).astype(jnp.bfloat16)

    each(pairs, add)
    each_peer(pair, pairs, lambda there: rows_back(there, pair).start())
    row_return[pair] = summed[pair]
    vertical_walk()
    vertical_out()
    each_peer(pair, pairs, lambda there: rows_back(there, there).wait_recv())
    place = lax.broadcasted_iota(jnp.int32, (DISPARITIES, DISPARITIES), 0)
    lane = lax.broadcasted_iota(jnp.int32, (DISPARITIES, DISPARITIES), 1)
    spread = place == (lane % SUB) * PARTS + lane // SUB
    spread = jnp.where(spread, 1.0, 0.0).astype(jnp.bfloat16)

    def gather(y, _):
        out_across[y] = ordered(spread, row_return[y])
        return 0

    lax.fori_loop(0, rows, gather, 0)
    each_peer(row, row_size, lambda there: strips_back(there, there).wait_recv())

    def hand_over(j, _):
        out_down[j] = back_in[j]
        return 0

    lax.fori_loop(0, row_size, hand_over, 0)
    each_peer(pair, pairs, lambda there: rows_out(there, pair).wait_send())
    each(pairs, lambda h: rows_pass(h, core).wait_send())
    each(pairs, lambda h: rows_swap(h).wait_send())
    each_peer(pair, pairs, lambda there: rows_back(there, pair).wait_send())
    each_peer(row, row_size, lambda there: strips_out(there, row).wait_send())
    each_peer(row, row_size, lambda there: strips_back(there, row).wait_send())


def paths_call(cost, charges):
    rows, count, _ = cost.shape
    row_size, col_size = lax.axis_size("row"), lax.axis_size("col")
    width = count // row_size
    block = (row_size, rows * width, DISPARITIES)
    vmem = pl.BlockSpec(memory_space=pltpu.VMEM)
    return pl.pallas_call(
        functools.partial(paths_kernel, row_size, col_size),
        out_shape=(
            jax.ShapeDtypeStruct(cost.shape, jnp.float32),
            jax.ShapeDtypeStruct(block, jnp.bfloat16),
        ),
        in_specs=[vmem, pl.BlockSpec(memory_space=pltpu.SMEM)],
        out_specs=(vmem, vmem),
        scratch_shapes=[
            pltpu.VMEM((rows * row_size, DISPARITIES, SUB), jnp.float32),
            pltpu.VMEM((rows * row_size, SUB, SUB), jnp.float32),
            pltpu.VMEM((BLOCK, 3 * DISPARITIES, DISPARITIES), jnp.float32),
            pltpu.VMEM((TABLE, DISPARITIES, DISPARITIES), jnp.float32),
            pltpu.VMEM((TABLE, DISPARITIES, DISPARITIES), jnp.float32),
            pltpu.VMEM((DISPARITIES, DISPARITIES), jnp.float32),
            pltpu.VMEM((rows, count, DISPARITIES), jnp.bfloat16),
            pltpu.VMEM((col_size, count, DISPARITIES), jnp.bfloat16),
            pltpu.VMEM((col_size, count, DISPARITIES), jnp.bfloat16),
            pltpu.VMEM((rows, count, DISPARITIES), jnp.bfloat16),
            pltpu.VMEM((rows, count, DISPARITIES), jnp.bfloat16),
            pltpu.VMEM((rows, count, DISPARITIES), jnp.bfloat16),
            pltpu.VMEM(block, jnp.bfloat16),
            pltpu.VMEM(block, jnp.bfloat16),
            pltpu.VMEM(block, jnp.bfloat16),
            pltpu.VMEM(block, jnp.bfloat16),
            pltpu.SemaphoreType.DMA((rows,)),
            pltpu.SemaphoreType.DMA((rows,)),
            pltpu.SemaphoreType.DMA((rows,)),
            pltpu.SemaphoreType.DMA((rows,)),
            pltpu.SemaphoreType.DMA((rows,)),
            pltpu.SemaphoreType.DMA((rows,)),
            pltpu.SemaphoreType.DMA((rows,)),
            pltpu.SemaphoreType.DMA((rows,)),
            pltpu.SemaphoreType.DMA((row_size,)),
            pltpu.SemaphoreType.DMA((row_size,)),
            pltpu.SemaphoreType.DMA((row_size,)),
            pltpu.SemaphoreType.DMA((row_size,)),
        ],
        compiler_params=pltpu.CompilerParams(
            collective_id=0, has_side_effects=True, vmem_limit_bytes=60 * 1024 * 1024
        ),
        name="four_paths",
    )(cost, charges)


def outer_kernel_sizes(images, halo):
    rows, channels, count = images.shape[1:]
    return rows, channels, count, rows + 2 * halo


def cost_kernel(
    row_size,
    col_size,
    layers_total,
    images,
    taps,
    biases,
    present,
    shift,
    cost,
    above,
    below,
    packed,
    from_left,
    from_right,
    stack_a,
    stack_b,
    left_unit,
    reach_unit,
    rows_send,
    rows_recv,
    cols_send,
    cols_recv,
    unit_send,
    unit_recv,
):
    rows, channels, count, tall = outer_kernel_sizes(images, layers_total)
    far = reach_unit.shape[0] - 1
    deep = 3 * channels
    row, me = lax.axis_index("row"), lax.axis_index("col")
    has_up, has_down = row > 0, row < row_size - 1
    has_left, has_right = me > 0, me < col_size - 1

    barrier = pltpu.get_barrier_semaphore()
    expected = jnp.where(has_up, 1, 0) + jnp.where(has_down, 1, 0)
    for there, step in ((has_up, -1), (has_down, 1)):

        @pl.when(there)
        def _(step=step):
            pl.semaphore_signal(barrier, inc=1, device_id={"row": row + step}, device_id_type=MESH)

    for distance in range(1, far + 1):
        for there, step in ((me >= distance, -distance), (me + distance < col_size, distance)):
            expected = expected + jnp.where(there, 1, 0)

            @pl.when(there)
            def _(step=step):
                pl.semaphore_signal(
                    barrier, inc=1, device_id={"col": me + step}, device_id_type=MESH
                )

    pl.semaphore_wait(barrier, expected)

    def row_copy(step):
        index = 0 if step < 0 else 1
        first = 0 if step < 0 else rows - layers_total
        return pltpu.make_async_remote_copy(
            src_ref=images.at[:, first : first + layers_total],
            dst_ref=below if step < 0 else above,
            send_sem=rows_send.at[index],
            recv_sem=rows_recv.at[index],
            device_id={"row": row + step},
            device_id_type=MESH,
        )

    def col_copy(step):
        index = 0 if step < 0 else 1
        return pltpu.make_async_remote_copy(
            src_ref=packed,
            dst_ref=from_right if step < 0 else from_left,
            send_sem=cols_send.at[index],
            recv_sem=cols_recv.at[index],
            device_id={"col": me + step},
            device_id_type=MESH,
        )

    def unit_copy(distance):
        return pltpu.make_async_remote_copy(
            src_ref=reach_unit.at[0],
            dst_ref=reach_unit.at[distance],
            send_sem=unit_send.at[distance],
            recv_sem=unit_recv.at[distance],
            device_id={"col": me + distance},
            device_id_type=MESH,
        )

    pl.when(has_up)(lambda: row_copy(-1).start())
    pl.when(has_down)(lambda: row_copy(1).start())

    @pl.when(jnp.logical_not(has_up))
    def _():
        above[...] = jnp.zeros_like(above)

    @pl.when(jnp.logical_not(has_down))
    def _():
        below[...] = jnp.zeros_like(below)

    pl.when(has_down)(lambda: row_copy(-1).wait_recv())
    pl.when(has_up)(lambda: row_copy(1).wait_recv())

    def row_of(image, k):
        if k < layers_total:
            return above[image, k]
        if k < layers_total + rows:
            return images[image, k - layers_total]
        return below[image, k - layers_total - rows]

    pick_row = lax.broadcasted_iota(jnp.int32, (count, count), 0)
    pick_lane = lax.broadcasted_iota(jnp.int32, (count, count), 1)

    def one_hot(where):
        return jnp.where(where, 1.0, 0.0).astype(jnp.bfloat16)

    for image in range(2):
        total = None
        for k in range(tall):
            slot = pick_lane - k * SUB
            head = jnp.logical_and(slot >= 0, jnp.logical_and(slot < 3, pick_row == slot))
            tail = jnp.logical_and(
                slot >= 3, jnp.logical_and(slot < 6, pick_row == slot + count - 6)
            )
            pick = one_hot(jnp.logical_or(head, tail))
            term = jnp.dot(row_of(image, k), pick, preferred_element_type=jnp.float32)
            total = term if total is None else total + term
        packed[image] = total.astype(jnp.bfloat16)

    pl.when(has_left)(lambda: col_copy(-1).start())
    pl.when(has_right)(lambda: col_copy(1).start())

    @pl.when(jnp.logical_not(has_left))
    def _():
        from_left[...] = jnp.zeros_like(from_left)

    @pl.when(jnp.logical_not(has_right))
    def _():
        from_right[...] = jnp.zeros_like(from_right)

    for distance in range(1, far + 1):

        @pl.when(me < distance)
        def _(distance=distance):
            reach_unit[distance] = jnp.zeros(reach_unit.shape[1:], reach_unit.dtype)

    pl.when(has_right)(lambda: col_copy(-1).wait_recv())
    pl.when(has_left)(lambda: col_copy(1).wait_recv())

    lanes = lax.broadcasted_iota(jnp.int32, (channels, 2 * count), 1)
    side = jnp.where(lanes < count + count // 2, has_right.astype(jnp.int32), has_left.astype(jnp.int32))
    keep_lane = jnp.where(lanes < count, 1, side)

    def put(stack, k, value):
        base = k * deep if isinstance(k, int) else pl.multiple_of(k * deep, deep)
        for b, turn in enumerate((1, 0, 2 * count - 1)):
            moved = pltpu.roll(value, turn, 1) if turn else value
            stack[pl.ds(base + b * channels, channels), :] = moved.astype(jnp.bfloat16)

    def features(image):
        for k in range(tall):
            slot_left = pick_row - k * SUB - 3 == pick_lane - (count - 3)
            slot_left = jnp.logical_and(slot_left, pick_lane >= count - 3)
            slot_right = jnp.logical_and(pick_row - k * SUB == pick_lane, pick_lane < 3)
            edge = jnp.dot(
                from_left[image], one_hot(slot_left), preferred_element_type=jnp.float32
            ) + jnp.dot(
                from_right[image], one_hot(slot_right), preferred_element_type=jnp.float32
            )
            put(
                stack_a,
                k,
                jnp.concatenate([row_of(image, k).astype(jnp.float32), edge], axis=1),
            )
        source, target = stack_a, stack_b
        for layer_number in range(layers_total):
            margin = layers_total - 1 - layer_number
            bias = biases[layer_number]
            weights = taps[layer_number]
            last = margin == 0

            def body(pair, _):
                for k in range(2):
                    y = pair * 2 + k
                    window = source[pl.ds(pl.multiple_of(y * deep, deep), 3 * deep), :]
                    if last:
                        window = window[:, :count]
                    value = jnp.dot(weights, window, preferred_element_type=jnp.float32) + bias
                    if last:
                        square = jnp.sum(value * value, axis=0, keepdims=True)
                        unit = (value * lax.rsqrt(square + 1e-06)).astype(jnp.bfloat16)
                        start = pl.multiple_of(y * channels, channels)
                        if image == 1:
                            reach_unit[0, pl.ds(start, channels), :] = unit
                        else:
                            left_unit[pl.ds(start, channels), :] = unit
                    else:
                        keep = jnp.logical_and(
                            jnp.logical_or(y >= margin, has_up),
                            jnp.logical_or(y < margin + rows, has_down),
                        )
                        value = jnp.where(
                            keep_lane * keep.astype(jnp.int32) == 1, jnp.maximum(value, 0.0), 0.0
                        )
                        put(target, y, value)
                return 0

            lax.fori_loop(0, (rows + 2 * margin) // 2, body, 0)
            source, target = target, source

    features(1)
    for distance in range(1, far + 1):
        pl.when(me + distance < col_size)(lambda distance=distance: unit_copy(distance).start())
    features(0)
    for distance in range(1, far + 1):
        pl.when(me >= distance)(lambda distance=distance: unit_copy(distance).wait_recv())

    wide = (far + 1) * count
    place = lax.broadcasted_iota(jnp.int32, (wide, 2 * count), 0)
    lane = lax.broadcasted_iota(jnp.int32, (wide, 2 * count), 1)
    choose = one_hot(place + lane == wide - 1 - shift[0, 0])

    def match(y, _):
        start = pl.multiple_of(y * channels, channels)
        reach = jnp.concatenate(
            [reach_unit[distance, pl.ds(start, channels), :] for distance in range(far, -1, -1)],
            axis=1,
        )
        strip = jnp.dot(reach, choose, preferred_element_type=jnp.float32).astype(jnp.bfloat16)
        held = present[pl.ds(y, 1), :] == 1
        left = left_unit[pl.ds(start, channels), :].astype(jnp.float32)
        left = jnp.where(held, left, 0.0).astype(jnp.bfloat16)
        product = lax.dot_general(
            left, strip, (((0,), (0,)), ((), ())), preferred_element_type=jnp.float32
        )
        skewed = pltpu.roll(product, count + 1, 1, stride=1, stride_axis=0)
        cost[y] = 1.0 - skewed[:, :DISPARITIES]
        return 0

    lax.fori_loop(0, rows, match, 0)

    pl.when(has_up)(lambda: row_copy(-1).wait_send())
    pl.when(has_down)(lambda: row_copy(1).wait_send())
    pl.when(has_left)(lambda: col_copy(-1).wait_send())
    pl.when(has_right)(lambda: col_copy(1).wait_send())
    for distance in range(1, far + 1):
        pl.when(me + distance < col_size)(lambda distance=distance: unit_copy(distance).wait_send())


def cost_call(images, taps, biases, present, shift):
    rows, channels, count = images.shape[1:]
    layers_total = taps.shape[0]
    tall = rows + 2 * layers_total
    far = (3 * count + DISPARITIES - 2) // count
    taps = jnp.transpose(taps, (0, 3, 1, 2, 4)).reshape(layers_total, channels, 9 * channels)
    vmem = pl.BlockSpec(memory_space=pltpu.VMEM)
    halo = pltpu.VMEM((2, layers_total, channels, count), jnp.bfloat16)
    edge = pltpu.VMEM((2, channels, count), jnp.bfloat16)
    stack = pltpu.VMEM((tall * 3 * channels, 2 * count), jnp.bfloat16)
    return pl.pallas_call(
        functools.partial(
            cost_kernel, lax.axis_size("row"), lax.axis_size("col"), layers_total
        ),
        out_shape=jax.ShapeDtypeStruct((rows, count, DISPARITIES), jnp.float32),
        in_specs=[vmem, vmem, vmem, vmem, pl.BlockSpec(memory_space=pltpu.SMEM)],
        out_specs=vmem,
        scratch_shapes=[
            halo,
            halo,
            edge,
            edge,
            edge,
            stack,
            stack,
            pltpu.VMEM((rows * channels, count), jnp.bfloat16),
            pltpu.VMEM((far + 1, rows * channels, count), jnp.bfloat16),
            pltpu.SemaphoreType.DMA((2,)),
            pltpu.SemaphoreType.DMA((2,)),
            pltpu.SemaphoreType.DMA((2,)),
            pltpu.SemaphoreType.DMA((2,)),
            pltpu.SemaphoreType.DMA((far + 1,)),
            pltpu.SemaphoreType.DMA((far + 1,)),
        ],
        compiler_params=pltpu.CompilerParams(
            collective_id=1, has_side_effects=True, vmem_limit_bytes=60 * 1024 * 1024
        ),
        name="matching_cost",
    )(images, taps, biases[:, :, None], present, shift)


def per_device(
    stereo_neuron_outputs,
    filter_tap_coefficients,
    filter_stack_intercepts,
    reference_picture_present,
    tile_shift_amounts,
    smoothness_charges,
):
    cost = cost_call(
        stereo_neuron_outputs,
        filter_tap_coefficients,
        filter_stack_intercepts,
        reference_picture_present,
        tile_shift_amounts,
    )
    across, down = paths_call(cost, smoothness_charges)
    down = down.reshape(lax.axis_size("row"), cost.shape[0], -1, DISPARITIES)
    down = jnp.swapaxes(down.astype(jnp.float32), 0, 1).reshape(cost.shape)
    return down + across


def solution(mesh):
    return jax.shard_map(
        per_device,
        mesh=mesh,
        in_specs=(P(None, "row", None, "col"), P(), P(), P("row", "col"), P("row", "col"), P()),
        out_specs=P("row", "col", None),
        check_vma=False,
    )
```

```python
import functools

import jax
import jax.numpy as jnp
from jax import lax
from jax.experimental import pallas as pl
from jax.experimental.pallas import tpu as pltpu
from jax.sharding import PartitionSpec as P

DISPARITIES = 128
SUB = 8
PARTS = DISPARITIES // SUB
MESH = pl.DeviceIdType.MESH


def order_matrix():
    row = lax.broadcasted_iota(jnp.int32, (DISPARITIES, DISPARITIES), 0)
    lane = lax.broadcasted_iota(jnp.int32, (DISPARITIES, DISPARITIES), 1)
    return jnp.where(lane == (row % SUB) * PARTS + row // SUB, 1.0, 0.0).astype(jnp.bfloat16)


def turned(value, order):
    return lax.dot_general(
        order,
        value.astype(jnp.bfloat16),
        (((1,), (1,)), ((), ())),
        preferred_element_type=jnp.float32,
    )


def ordered(value, order):
    return jnp.dot(value, order, preferred_element_type=jnp.float32)


def pieces_of(value):
    return [value[v * SUB : (v + 1) * SUB] for v in range(PARTS)]


def smallest(state):
    level = list(state)
    while len(level) > 1:
        level = [jnp.minimum(level[2 * i], level[2 * i + 1]) for i in range(len(level) // 2)]
    least = level[0]
    for step in (4, 2, 1):
        least = jnp.minimum(least, pltpu.roll(least, step, 0))
    return least


def step_once(state, cost, p1, p2, first_sub, last_sub):
    lifted = [s + p1 for s in state]
    below = jnp.where(first_sub, jnp.inf, pltpu.roll(lifted[-1], 1, 0))
    above = jnp.where(last_sub, jnp.inf, pltpu.roll(lifted[0], SUB - 1, 0))
    near = [below] + lifted + [above]
    least = smallest(state)
    jump = least + p2
    fresh = [
        cost[v]
        + jnp.minimum(jnp.minimum(state[v], jnp.minimum(near[v], near[v + 2])), jump)
        for v in range(PARTS)
    ]
    return fresh, least


def walk(slots, out, leasts, count, state, charges, at):
    sub = lax.broadcasted_iota(jnp.int32, (SUB, SUB), 0)
    first_sub, last_sub = sub == 0, sub == SUB - 1
    p1 = charges[0].astype(jnp.float32) / 64.0
    p2 = charges[1].astype(jnp.float32) / 64.0

    def body(turn, carry):
        state, least = list(carry[0]), carry[1]
        for k in range(8):
            t = at(turn * 8 + k)
            state, least = step_once(state, pieces_of(slots[t]), p1, p2, first_sub, last_sub)
            leasts[t] = least
            for v in range(PARTS):
                out[t, v * SUB : (v + 1) * SUB, :] = state[v]
        return tuple(state), least

    start = (tuple(state), jnp.zeros((SUB, SUB), jnp.float32))
    return lax.fori_loop(0, count // 8, body, start)


def layer(walked, leasts, t):
    least = leasts[t]
    return jnp.concatenate([piece - least for piece in pieces_of(walked[t])], axis=0).T


BLOCK = 16
OFFSETS = 2 * BLOCK + 1
TABLE = 5 * SUB + 2 * BLOCK


def row_paths(came, back, charges, way, order, costs, table, turned_table, states):
    tiles = came.shape[0]
    sub = lax.broadcasted_iota(jnp.int32, (SUB, DISPARITIES), 0)
    first_sub, last_sub = sub == 0, sub == SUB - 1
    p1 = charges[0].astype(jnp.float32) / 64.0
    p2 = charges[1].astype(jnp.float32) / 64.0
    middle = DISPARITIES

    def at(n):
        return jnp.where(way == 0, n, BLOCK - 1 - n)

    def take(pair, _):
        start = pl.multiple_of(pair * 2 * SUB, 2 * SUB)
        parts = [came[c, pl.ds(start, 2 * SUB), :].astype(jnp.float32) for c in range(tiles)]
        for half in range(2):
            rows = [part[half * SUB : (half + 1) * SUB] for part in parts]
            value = turned(jnp.concatenate(rows, axis=0), order)
            for v, piece in enumerate(pieces_of(value)):
                t = pair * 2 + half
                lower = jnp.where(first_sub, jnp.inf, pltpu.roll(piece, 1, 0))
                upper = jnp.where(last_sub, jnp.inf, pltpu.roll(piece, SUB - 1, 0))
                costs[t, v * SUB : (v + 1) * SUB, :] = lower
                costs[t, middle + v * SUB : middle + (v + 1) * SUB, :] = piece
                costs[t, 2 * middle + v * SUB : 2 * middle + (v + 1) * SUB, :] = upper
        return 0

    lax.fori_loop(0, BLOCK // 2, take, 0)

    def keep(index, v, value):
        table[index, pl.ds(pl.multiple_of(v * SUB, SUB), SUB), :] = value

    def no_jump(v, _):
        paths = {0: None}
        for n in range(BLOCK):
            t = at(n)
            fresh = {}
            for o in range(-n - 1, n + 2):
                near = [paths[q] for q in (o - 1, o + 1) if q in paths]
                start = pl.multiple_of((PARTS + v + o) * SUB, SUB)
                cost = costs[t, pl.ds(start, SUB), :]
                if n == 0:
                    fresh[o] = cost if o == 0 else cost + p1
                    continue
                best = near[0] if len(near) == 1 else jnp.minimum(near[0], near[1])
                best = best + p1
                if o in paths:
                    best = jnp.minimum(paths[o], best)
                fresh[o] = cost + best
            paths = fresh
            if n < BLOCK - 1:
                level = list(paths.values())
                while len(level) > 1:
                    rest = level[len(level) // 2 * 2 :]
                    level = [
                        jnp.minimum(level[2 * i], level[2 * i + 1]) for i in range(len(level) // 2)
                    ] + rest
                keep(5 * SUB + n + 1, v, level[0])
        for o in range(-BLOCK, BLOCK + 1):
            keep(BLOCK + o, v, paths[o])
        for index in range(OFFSETS, 5 * SUB):
            keep(index, v, jnp.full((SUB, DISPARITIES), jnp.inf, jnp.float32))
        keep(5 * SUB, v, jnp.zeros((SUB, DISPARITIES), jnp.float32))
        return 0

    lax.fori_loop(0, PARTS, no_jump, 0)

    def costs_of(n):
        t = at(n)
        return [costs[t, middle + v * SUB : middle + (v + 1) * SUB, :] for v in range(PARTS)]

    def jumped(first, _):
        def one(n, state):
            return tuple(step_once(list(state), costs_of(n), p1, p2, first_sub, last_sub)[0])

        state = lax.fori_loop(first + 1, BLOCK, one, tuple(costs_of(first)))
        for v in range(PARTS):
            table[5 * SUB + BLOCK + first, v * SUB : (v + 1) * SUB, :] = state[v] + p2
        return 0

    lax.fori_loop(0, BLOCK, jumped, 0)

    def turn(group, _):
        for k in range(4):
            turned_table[group * 4 + k] = table[group * 4 + k].T
        return 0

    lax.fori_loop(0, TABLE // 4, turn, 0)
    lane = lax.broadcasted_iota(jnp.int32, (SUB, DISPARITIES), 1)
    natural = (lane % PARTS) * SUB + lane // PARTS

    def sort(group, _):
        for k in range(8):
            for v in range(PARTS):
                piece = turned_table[group * 8 + k, v * SUB : (v + 1) * SUB, :]
                turned_table[group * 8 + k, v * SUB : (v + 1) * SUB, :] = jnp.take_along_axis(
                    piece, natural, axis=1
                )
        return 0

    lax.fori_loop(0, TABLE // 8, sort, 0)

    def apply(turn_of, state):
        for k in range(SUB):
            n = turn_of * SUB + k
            b = jnp.where(way == 0, n, DISPARITIES - 1 - n)
            states[pl.ds(b, 1), :] = state[:1]
            found = []
            for g in range(2):
                start = 5 * SUB + g * SUB
                least = jnp.min(
                    state + turned_table[start : start + SUB, b, :], axis=1, keepdims=True
                )
                start = start + BLOCK
                found.append(least + turned_table[start : start + SUB, b, :])
            for g in range(5):
                term = state + turned_table[g * SUB : (g + 1) * SUB, b, :]
                amount = (g * SUB - BLOCK) % DISPARITIES
                found.append(pltpu.roll(term, amount, 1, stride=1, stride_axis=0))
            found = found[2:] + found[:2]
            while len(found) > 1:
                rest = found[len(found) // 2 * 2 :]
                found = [
                    jnp.minimum(found[2 * i], found[2 * i + 1]) for i in range(len(found) // 2)
                ] + rest
            state = found[0]
            for step in (4, 2, 1):
                state = jnp.minimum(state, pltpu.roll(state, step, 0))
        return state - jnp.min(state, axis=1, keepdims=True)

    lax.fori_loop(
        0, DISPARITIES // SUB, apply, jnp.zeros((SUB, DISPARITIES), jnp.float32)
    )
    before = states[...]
    before = before - jnp.min(before, axis=1, keepdims=True)
    high = before.astype(jnp.bfloat16)
    rest = before - high.astype(jnp.float32)
    state = pieces_of(turned(high, order) + turned(rest, order))

    def inside(pair, state):
        state = list(state)
        results = []
        for k in range(2):
            state, least = step_once(
                state, costs_of(pair * 2 + k), p1, p2, first_sub, last_sub
            )
            value = jnp.concatenate([piece - least for piece in state], axis=0).T
            results.append(ordered(value.astype(jnp.bfloat16), order))
        low = jnp.where(way == 0, results[0], results[1])
        top = jnp.where(way == 0, results[1], results[0])
        start = jnp.where(way == 0, pair, BLOCK // 2 - 1 - pair) * 2 * SUB
        start = pl.multiple_of(start, 2 * SUB)
        for c in range(tiles):
            rows = slice(c * SUB, (c + 1) * SUB)
            back[c, pl.ds(start, 2 * SUB), :] = jnp.concatenate(
                [low[rows], top[rows]], axis=0
            ).astype(jnp.bfloat16)
        return tuple(state)

    lax.fori_loop(0, BLOCK // 2, inside, tuple(state))


def half_turn(value):
    return pltpu.roll(value, SUB // 2, 0)


def paths_kernel(
    row_size,
    col_size,
    cost,
    charges,
    out,
    strips,
    strip_leasts,
    costs,
    table,
    turned_table,
    states,
    row_sent,
    row_came,
    row_back,
    swapped,
    summed,
    row_return,
    sent,
    came,
    back_out,
    back_in,
    row_send,
    row_recv,
    pass_send,
    pass_recv,
    swap_send,
    swap_recv,
    return_send,
    return_recv,
    sent_sem,
    came_sem,
    back_send,
    back_recv,
):
    rows = cost.shape[0]
    height = strips.shape[0]
    row = lax.axis_index("row")
    me = lax.axis_index("col")
    low = lax.broadcasted_iota(jnp.int32, (SUB, DISPARITIES), 0) < SUB // 2
    order = order_matrix()

    barrier = pltpu.get_barrier_semaphore()
    for axis, mine, size in (("row", row, row_size), ("col", me, col_size)):

        def greet(j, _, axis=axis, mine=mine, size=size):
            peer = lax.rem(mine + j, size)
            pl.semaphore_signal(barrier, inc=1, device_id={axis: peer}, device_id_type=MESH)
            return 0

        lax.fori_loop(1, size, greet, 0)

    core = lax.rem(me, 2)
    pair, pairs = me // 2, col_size // 2
    partner = me + 1 - 2 * core

    def remote(source, target, send_sem, recv_sem, axis, peer):
        return pltpu.make_async_remote_copy(
            src_ref=source,
            dst_ref=target,
            send_sem=send_sem,
            recv_sem=recv_sem,
            device_id={axis: peer},
            device_id_type=MESH,
        )

    def rows_out(there, slot):
        peer = 2 * there + core
        return remote(
            row_sent.at[there],
            row_came.at[2 * slot + core],
            row_send.at[there],
            row_recv.at[slot],
            "col",
            peer,
        )

    def rows_pass(h, side):
        block = row_came.at[2 * h + side]
        return remote(block, block, pass_send.at[h], pass_recv.at[h], "col", partner)

    def rows_swap(h):
        source = row_back.at[2 * h + 1 - core]
        return remote(source, swapped.at[h], swap_send.at[h], swap_recv.at[h], "col", partner)

    def rows_back(there, slot):
        return remote(
            summed.at[there],
            row_return.at[slot],
            return_send.at[there],
            return_recv.at[slot],
            "col",
            2 * there + core,
        )

    def strips_out(there, slot):
        return remote(
            sent.at[there], came.at[slot], sent_sem.at[there], came_sem.at[slot], "row", there
        )

    def strips_back(there, slot):
        return remote(
            back_out.at[there],
            back_in.at[slot],
            back_send.at[there],
            back_recv.at[slot],
            "row",
            there,
        )

    def each_peer(mine, size, work):
        def body(j, _):
            work(lax.rem(mine + j, size))
            return 0

        lax.fori_loop(1, size, body, 0)

    def each(size, work):
        def body(j, _):
            work(j)
            return 0

        lax.fori_loop(0, size, body, 0)

    def group(y, _):
        row_sent[y] = ordered(order, cost[y].astype(jnp.bfloat16)).astype(jnp.bfloat16)
        return 0

    lax.fori_loop(0, rows, group, 0)

    def cut(tile, _):
        start = pl.multiple_of(tile * SUB, SUB)
        rows = [cost[y, pl.ds(start, SUB), :] for y in range(SUB)]
        even = [jnp.where(low, rows[y], half_turn(rows[y + 1])) for y in range(0, SUB, 2)]
        odd = [jnp.where(low, half_turn(rows[y]), rows[y + 1]) for y in range(0, SUB, 2)]
        sent[2 * tile] = jnp.concatenate(even, axis=0).astype(jnp.bfloat16)
        sent[2 * tile + 1] = jnp.concatenate(odd, axis=0).astype(jnp.bfloat16)
        return 0

    lax.fori_loop(0, row_size // 2, cut, 0)
    pl.semaphore_wait(barrier, row_size + col_size - 2)
    each_peer(pair, pairs, lambda there: rows_out(there, pair).start())
    row_came[me] = row_sent[pair]

    def vertical_in():
        each_peer(row, row_size, lambda there: strips_out(there, there).wait_recv())

        def body(source, _):
            near = came[source].astype(jnp.float32)
            far = came[row_size - 1 - source].astype(jnp.float32)
            for q in range(SUB // 2):
                a = near[q * SUB : (q + 1) * SUB]
                b = far[(3 - q) * SUB : (4 - q) * SUB]
                first = jnp.where(low, a, b)
                second = half_turn(jnp.where(low, b, a))
                t = source * SUB + 2 * q
                strips[t] = turned(first, order)
                strips[t + 1] = turned(second, order)
            return 0

        lax.fori_loop(0, row_size, body, 0)

    def vertical_walk():
        zero = [jnp.zeros((SUB, SUB), jnp.float32) for _ in range(PARTS)]
        walk(strips, strips, strip_leasts, height, zero, charges, lambda t: t)

    def vertical_out():
        def send(near):
            for there in (near, row_size - 1 - near):

                @pl.when(there != row)
                def _(there=there):
                    strips_back(there, row).start()

        def body(near, _):
            pl.when(near > 0)(lambda: send(near - 1))
            far = row_size - 1 - near
            one = [layer(strips, strip_leasts, near * SUB + y) for y in range(SUB)]
            other = [layer(strips, strip_leasts, far * SUB + y) for y in range(SUB)]
            total = [one[y] + half_turn(other[SUB - 1 - y]) for y in range(SUB)]
            up = [jnp.where(low, total[y], half_turn(total[y + 1])) for y in (0, 2, 4, 6)]
            down = [jnp.where(low, half_turn(total[y + 1]), total[y]) for y in (6, 4, 2, 0)]
            both = jnp.concatenate(up + down, axis=0).astype(jnp.bfloat16)
            both = ordered(both, order).astype(jnp.bfloat16)
            half = SUB * SUB // 2
            back_out[near] = both[:half]
            back_out[far] = both[half:]
            return 0

        lax.fori_loop(0, row_size // 2, body, 0)
        send(row_size // 2 - 1)
        back_in[row] = back_out[row]

    rows_pass(pair, core).start()

    def forward(j, _):
        there = lax.rem(pair + pairs - j, pairs)
        rows_out(there, there).wait_recv()
        rows_pass(there, core).start()
        return 0

    lax.fori_loop(1, pairs, forward, 0)
    each_peer(row, row_size, lambda there: strips_out(there, row).start())
    came[row] = sent[row]
    each(pairs, lambda h: rows_pass(h, 1 - core).wait_recv())
    row_paths(row_came, row_back, charges, core, order, costs, table, turned_table, states)
    each(pairs, lambda h: rows_swap(h).start())
    vertical_in()

    def add(h):
        rows_swap(h).wait_recv()
        mine = row_back[2 * h + core].astype(jnp.float32)
        summed[h] = (mine + swapped[h].astype(jnp.float32)).astype(jnp.bfloat16)

    each(pairs, add)
    each_peer(pair, pairs, lambda there: rows_back(there, pair).start())
    row_return[pair] = summed[pair]
    vertical_walk()
    vertical_out()
    each_peer(pair, pairs, lambda there: rows_back(there, there).wait_recv())
    place = lax.broadcasted_iota(jnp.int32, (DISPARITIES, DISPARITIES), 0)
    lane = lax.broadcasted_iota(jnp.int32, (DISPARITIES, DISPARITIES), 1)
    spread = place == (lane % SUB) * PARTS + lane // SUB
    spread = jnp.where(spread, 1.0, 0.0).astype(jnp.bfloat16)

    def gather(y, _):
        out[y] = ordered(spread, row_return[y])
        return 0

    lax.fori_loop(0, rows, gather, 0)
    each_peer(row, row_size, lambda there: strips_back(there, there).wait_recv())

    def hand_over(tile, _):
        start = pl.multiple_of(tile * SUB, SUB)
        near = back_in[2 * tile].astype(jnp.float32)
        far = back_in[2 * tile + 1].astype(jnp.float32)
        for y in range(0, SUB, 2):
            a = near[y // 2 * SUB : (y // 2 + 1) * SUB]
            b = far[y // 2 * SUB : (y // 2 + 1) * SUB]
            here = pl.ds(start, SUB)
            out[y, here, :] = out[y, here, :] + jnp.where(low, a, half_turn(b))
            out[y + 1, here, :] = out[y + 1, here, :] + jnp.where(low, half_turn(a), b)
        return 0

    lax.fori_loop(0, row_size // 2, hand_over, 0)
    each_peer(pair, pairs, lambda there: rows_out(there, pair).wait_send())
    each(pairs, lambda h: rows_pass(h, core).wait_send())
    each(pairs, lambda h: rows_swap(h).wait_send())
    each_peer(pair, pairs, lambda there: rows_back(there, pair).wait_send())
    each_peer(row, row_size, lambda there: strips_out(there, row).wait_send())
    each_peer(row, row_size, lambda there: strips_back(there, row).wait_send())


def paths_call(cost, charges):
    rows, count, _ = cost.shape
    row_size, col_size = lax.axis_size("row"), lax.axis_size("col")
    width = count // row_size
    block = (row_size, rows * width, DISPARITIES)
    vmem = pl.BlockSpec(memory_space=pltpu.VMEM)
    return pl.pallas_call(
        functools.partial(paths_kernel, row_size, col_size),
        out_shape=jax.ShapeDtypeStruct(cost.shape, jnp.float32),
        in_specs=[vmem, pl.BlockSpec(memory_space=pltpu.SMEM)],
        out_specs=vmem,
        scratch_shapes=[
            pltpu.VMEM((rows * row_size, DISPARITIES, SUB), jnp.float32),
            pltpu.VMEM((rows * row_size, SUB, SUB), jnp.float32),
            pltpu.VMEM((BLOCK, 3 * DISPARITIES, DISPARITIES), jnp.float32),
            pltpu.VMEM((TABLE, DISPARITIES, DISPARITIES), jnp.float32),
            pltpu.VMEM((TABLE, DISPARITIES, DISPARITIES), jnp.float32),
            pltpu.VMEM((DISPARITIES, DISPARITIES), jnp.float32),
            pltpu.VMEM((rows, count, DISPARITIES), jnp.bfloat16),
            pltpu.VMEM((col_size, count, DISPARITIES), jnp.bfloat16),
            pltpu.VMEM((col_size, count, DISPARITIES), jnp.bfloat16),
            pltpu.VMEM((rows, count, DISPARITIES), jnp.bfloat16),
            pltpu.VMEM((rows, count, DISPARITIES), jnp.bfloat16),
            pltpu.VMEM((rows, count, DISPARITIES), jnp.bfloat16),
            pltpu.VMEM(block, jnp.bfloat16),
            pltpu.VMEM(block, jnp.bfloat16),
            pltpu.VMEM(block, jnp.bfloat16),
            pltpu.VMEM(block, jnp.bfloat16),
            pltpu.SemaphoreType.DMA((rows,)),
            pltpu.SemaphoreType.DMA((rows,)),
            pltpu.SemaphoreType.DMA((rows,)),
            pltpu.SemaphoreType.DMA((rows,)),
            pltpu.SemaphoreType.DMA((rows,)),
            pltpu.SemaphoreType.DMA((rows,)),
            pltpu.SemaphoreType.DMA((rows,)),
            pltpu.SemaphoreType.DMA((rows,)),
            pltpu.SemaphoreType.DMA((row_size,)),
            pltpu.SemaphoreType.DMA((row_size,)),
            pltpu.SemaphoreType.DMA((row_size,)),
            pltpu.SemaphoreType.DMA((row_size,)),
        ],
        compiler_params=pltpu.CompilerParams(
            collective_id=0, has_side_effects=True, vmem_limit_bytes=60 * 1024 * 1024
        ),
        name="four_paths",
    )(cost, charges)


def outer_kernel_sizes(images, halo):
    rows, channels, count = images.shape[1:]
    return rows, channels, count, rows + 2 * halo


def cost_kernel(
    row_size,
    col_size,
    layers_total,
    images,
    taps,
    biases,
    present,
    shift,
    cost,
    stacked_taps,
    above,
    below,
    packed,
    from_left,
    from_right,
    stack_a,
    stack_b,
    left_unit,
    reach_unit,
    rows_send,
    rows_recv,
    cols_send,
    cols_recv,
    unit_send,
    unit_recv,
):
    rows, channels, count, tall = outer_kernel_sizes(images, layers_total)
    far = reach_unit.shape[0] - 1
    deep = 3 * channels
    row, me = lax.axis_index("row"), lax.axis_index("col")
    has_up, has_down = row > 0, row < row_size - 1
    has_left, has_right = me > 0, me < col_size - 1

    barrier = pltpu.get_barrier_semaphore()
    expected = jnp.where(has_up, 1, 0) + jnp.where(has_down, 1, 0)
    for there, step in ((has_up, -1), (has_down, 1)):

        @pl.when(there)
        def _(step=step):
            pl.semaphore_signal(barrier, inc=1, device_id={"row": row + step}, device_id_type=MESH)

    for distance in range(1, far + 1):
        for there, step in ((me >= distance, -distance), (me + distance < col_size, distance)):
            expected = expected + jnp.where(there, 1, 0)

            @pl.when(there)
            def _(step=step):
                pl.semaphore_signal(
                    barrier, inc=1, device_id={"col": me + step}, device_id_type=MESH
                )

    pl.semaphore_wait(barrier, expected)

    def row_copy(step):
        index = 0 if step < 0 else 1
        first = 0 if step < 0 else rows - layers_total
        return pltpu.make_async_remote_copy(
            src_ref=images.at[:, first : first + layers_total],
            dst_ref=below if step < 0 else above,
            send_sem=rows_send.at[index],
            recv_sem=rows_recv.at[index],
            device_id={"row": row + step},
            device_id_type=MESH,
        )

    def col_copy(step):
        index = 0 if step < 0 else 1
        return pltpu.make_async_remote_copy(
            src_ref=packed,
            dst_ref=from_right if step < 0 else from_left,
            send_sem=cols_send.at[index],
            recv_sem=cols_recv.at[index],
            device_id={"col": me + step},
            device_id_type=MESH,
        )

    def unit_copy(distance):
        return pltpu.make_async_remote_copy(
            src_ref=reach_unit.at[0],
            dst_ref=reach_unit.at[distance],
            send_sem=unit_send.at[distance],
            recv_sem=unit_recv.at[distance],
            device_id={"col": me + distance},
            device_id_type=MESH,
        )

    pl.when(has_up)(lambda: row_copy(-1).start())
    pl.when(has_down)(lambda: row_copy(1).start())

    @pl.when(jnp.logical_not(has_up))
    def _():
        above[...] = jnp.zeros_like(above)

    @pl.when(jnp.logical_not(has_down))
    def _():
        below[...] = jnp.zeros_like(below)

    for layer_number in range(layers_total):
        for a in range(3):
            for b in range(3):
                first = (3 * a + b) * channels
                stacked_taps[layer_number, :, first : first + channels] = taps[layer_number, a, b]

    pl.when(has_down)(lambda: row_copy(-1).wait_recv())
    pl.when(has_up)(lambda: row_copy(1).wait_recv())

    def row_of(image, k):
        if k < layers_total:
            return above[image, k]
        if k < layers_total + rows:
            return images[image, k - layers_total]
        return below[image, k - layers_total - rows]

    pick_row = lax.broadcasted_iota(jnp.int32, (count, count), 0)
    pick_lane = lax.broadcasted_iota(jnp.int32, (count, count), 1)

    def one_hot(where):
        return jnp.where(where, 1.0, 0.0).astype(jnp.bfloat16)

    for image in range(2):
        total = None
        for k in range(tall):
            slot = pick_lane - k * SUB
            head = jnp.logical_and(slot >= 0, jnp.logical_and(slot < 3, pick_row == slot))
            tail = jnp.logical_and(
                slot >= 3, jnp.logical_and(slot < 6, pick_row == slot + count - 6)
            )
            pick = one_hot(jnp.logical_or(head, tail))
            term = jnp.dot(row_of(image, k), pick, preferred_element_type=jnp.float32)
            total = term if total is None else total + term
        packed[image] = total.astype(jnp.bfloat16)

    pl.when(has_left)(lambda: col_copy(-1).start())
    pl.when(has_right)(lambda: col_copy(1).start())

    @pl.when(jnp.logical_not(has_left))
    def _():
        from_left[...] = jnp.zeros_like(from_left)

    @pl.when(jnp.logical_not(has_right))
    def _():
        from_right[...] = jnp.zeros_like(from_right)

    for distance in range(1, far + 1):

        @pl.when(me < distance)
        def _(distance=distance):
            reach_unit[distance] = jnp.zeros(reach_unit.shape[1:], reach_unit.dtype)

    pl.when(has_right)(lambda: col_copy(-1).wait_recv())
    pl.when(has_left)(lambda: col_copy(1).wait_recv())

    lanes = lax.broadcasted_iota(jnp.int32, (channels, 2 * count), 1)
    side = jnp.where(lanes < count + count // 2, has_right.astype(jnp.int32), has_left.astype(jnp.int32))
    keep_lane = jnp.where(lanes < count, 1, side)

    eye = lax.broadcasted_iota(jnp.int32, (channels, channels), 0)
    eye = eye == lax.broadcasted_iota(jnp.int32, (channels, channels), 1)

    def put(stack, k, value):
        base = k * deep if isinstance(k, int) else pl.multiple_of(k * deep, deep)
        for b, turn in enumerate((1, 0, 2 * count - 1)):
            moved = pltpu.roll(value, turn, 1) if turn else value
            stack[pl.ds(base + b * channels, channels), :] = moved.astype(jnp.bfloat16)

    def features(image):
        for k in range(tall):
            slot_left = pick_row - k * SUB - 3 == pick_lane - (count - 3)
            slot_left = jnp.logical_and(slot_left, pick_lane >= count - 3)
            slot_right = jnp.logical_and(pick_row - k * SUB == pick_lane, pick_lane < 3)
            edge = jnp.dot(
                from_left[image], one_hot(slot_left), preferred_element_type=jnp.float32
            ) + jnp.dot(
                from_right[image], one_hot(slot_right), preferred_element_type=jnp.float32
            )
            put(
                stack_a,
                k,
                jnp.concatenate([row_of(image, k).astype(jnp.float32), edge], axis=1),
            )
        source, target = stack_a, stack_b
        for layer_number in range(layers_total):
            margin = layers_total - 1 - layer_number
            bias = jnp.broadcast_to(biases[layer_number : layer_number + 1, :], eye.shape)
            bias = jnp.sum(jnp.where(eye, bias, 0.0), axis=1, keepdims=True)
            weights = stacked_taps[layer_number]
            last = margin == 0

            def body(pair, _):
                for k in range(2):
                    y = pair * 2 + k
                    window = source[pl.ds(pl.multiple_of(y * deep, deep), 3 * deep), :]
                    if last:
                        window = window[:, :count]
                    value = jnp.dot(weights, window, preferred_element_type=jnp.float32) + bias
                    if last:
                        square = jnp.sum(value * value, axis=0, keepdims=True)
                        unit = (value * lax.rsqrt(square + 1e-06)).astype(jnp.bfloat16)
                        start = pl.multiple_of(y * channels, channels)
                        if image == 1:
                            reach_unit[0, pl.ds(start, channels), :] = unit
                        else:
                            left_unit[pl.ds(start, channels), :] = unit
                    else:
                        keep = jnp.logical_and(
                            jnp.logical_or(y >= margin, has_up),
                            jnp.logical_or(y < margin + rows, has_down),
                        )
                        value = jnp.where(
                            keep_lane * keep.astype(jnp.int32) == 1, jnp.maximum(value, 0.0), 0.0
                        )
                        put(target, y, value)
                return 0

            lax.fori_loop(0, (rows + 2 * margin) // 2, body, 0)
            source, target = target, source

    features(1)
    for distance in range(1, far + 1):
        pl.when(me + distance < col_size)(lambda distance=distance: unit_copy(distance).start())
    features(0)
    for distance in range(1, far + 1):
        pl.when(me >= distance)(lambda distance=distance: unit_copy(distance).wait_recv())

    wide = (far + 1) * count
    place = lax.broadcasted_iota(jnp.int32, (wide, 2 * count), 0)
    lane = lax.broadcasted_iota(jnp.int32, (wide, 2 * count), 1)
    choose = one_hot(place + lane == wide - 1 - shift[0, 0])

    def match(y, _):
        start = pl.multiple_of(y * channels, channels)
        reach = jnp.concatenate(
            [reach_unit[distance, pl.ds(start, channels), :] for distance in range(far, -1, -1)],
            axis=1,
        )
        strip = jnp.dot(reach, choose, preferred_element_type=jnp.float32).astype(jnp.bfloat16)
        held = present[pl.ds(y, 1), :] == 1
        left = left_unit[pl.ds(start, channels), :].astype(jnp.float32)
        left = jnp.where(held, left, 0.0).astype(jnp.bfloat16)
        product = lax.dot_general(
            left, strip, (((0,), (0,)), ((), ())), preferred_element_type=jnp.float32
        )
        skewed = pltpu.roll(product, count + 1, 1, stride=1, stride_axis=0)
        cost[y] = 1.0 - skewed[:, :DISPARITIES]
        return 0

    lax.fori_loop(0, rows, match, 0)

    pl.when(has_up)(lambda: row_copy(-1).wait_send())
    pl.when(has_down)(lambda: row_copy(1).wait_send())
    pl.when(has_left)(lambda: col_copy(-1).wait_send())
    pl.when(has_right)(lambda: col_copy(1).wait_send())
    for distance in range(1, far + 1):
        pl.when(me + distance < col_size)(lambda distance=distance: unit_copy(distance).wait_send())


def cost_call(images, taps, biases, present, shift):
    rows, channels, count = images.shape[1:]
    layers_total = taps.shape[0]
    tall = rows + 2 * layers_total
    far = (3 * count + DISPARITIES - 2) // count
    vmem = pl.BlockSpec(memory_space=pltpu.VMEM)
    halo = pltpu.VMEM((2, layers_total, channels, count), jnp.bfloat16)
    edge = pltpu.VMEM((2, channels, count), jnp.bfloat16)
    stack = pltpu.VMEM((tall * 3 * channels, 2 * count), jnp.bfloat16)
    return pl.pallas_call(
        functools.partial(
            cost_kernel, lax.axis_size("row"), lax.axis_size("col"), layers_total
        ),
        out_shape=jax.ShapeDtypeStruct((rows, count, DISPARITIES), jnp.float32),
        in_specs=[vmem, vmem, vmem, vmem, pl.BlockSpec(memory_space=pltpu.SMEM)],
        out_specs=vmem,
        scratch_shapes=[
            pltpu.VMEM((layers_total, channels, 9 * channels), jnp.bfloat16),
            halo,
            halo,
            edge,
            edge,
            edge,
            stack,
            stack,
            pltpu.VMEM((rows * channels, count), jnp.bfloat16),
            pltpu.VMEM((far + 1, rows * channels, count), jnp.bfloat16),
            pltpu.SemaphoreType.DMA((2,)),
            pltpu.SemaphoreType.DMA((2,)),
            pltpu.SemaphoreType.DMA((2,)),
            pltpu.SemaphoreType.DMA((2,)),
            pltpu.SemaphoreType.DMA((far + 1,)),
            pltpu.SemaphoreType.DMA((far + 1,)),
        ],
        compiler_params=pltpu.CompilerParams(
            collective_id=1, has_side_effects=True, vmem_limit_bytes=60 * 1024 * 1024
        ),
        name="matching_cost",
    )(images, taps, biases, present, shift)


def per_device(
    stereo_neuron_outputs,
    filter_tap_coefficients,
    filter_stack_intercepts,
    reference_picture_present,
    tile_shift_amounts,
    smoothness_charges,
):
    cost = cost_call(
        stereo_neuron_outputs,
        filter_tap_coefficients,
        filter_stack_intercepts,
        reference_picture_present,
        tile_shift_amounts,
    )
    return paths_call(cost, smoothness_charges)


def solution(mesh):
    return jax.shard_map(
        per_device,
        mesh=mesh,
        in_specs=(P(None, "row", None, "col"), P(), P(), P("row", "col"), P("row", "col"), P()),
        out_specs=P("row", "col", None),
        check_vma=False,
    )
```

```python
import functools

import jax
import jax.numpy as jnp
from jax import lax
from jax.experimental import pallas as pl
from jax.experimental.pallas import tpu as pltpu
from jax.sharding import PartitionSpec as P

DISPARITIES = 128
SUB = 8
PARTS = DISPARITIES // SUB
MESH = pl.DeviceIdType.MESH


def order_matrix():
    row = lax.broadcasted_iota(jnp.int32, (DISPARITIES, DISPARITIES), 0)
    lane = lax.broadcasted_iota(jnp.int32, (DISPARITIES, DISPARITIES), 1)
    return jnp.where(lane == (row % SUB) * PARTS + row // SUB, 1.0, 0.0).astype(jnp.bfloat16)


def turned(value, order):
    return lax.dot_general(
        order,
        value.astype(jnp.bfloat16),
        (((1,), (1,)), ((), ())),
        preferred_element_type=jnp.float32,
    )


def ordered(value, order):
    return jnp.dot(value, order, preferred_element_type=jnp.float32)


def pieces_of(value):
    return [value[v * SUB : (v + 1) * SUB] for v in range(PARTS)]


def smallest(state):
    level = list(state)
    while len(level) > 1:
        level = [jnp.minimum(level[2 * i], level[2 * i + 1]) for i in range(len(level) // 2)]
    least = level[0]
    for step in (4, 2, 1):
        least = jnp.minimum(least, pltpu.roll(least, step, 0))
    return least


def step_once(state, cost, p1, p2, first_sub, last_sub):
    lifted = [s + p1 for s in state]
    below = jnp.where(first_sub, jnp.inf, pltpu.roll(lifted[-1], 1, 0))
    above = jnp.where(last_sub, jnp.inf, pltpu.roll(lifted[0], SUB - 1, 0))
    near = [below] + lifted + [above]
    least = smallest(state)
    jump = least + p2
    fresh = [
        cost[v]
        + jnp.minimum(jnp.minimum(state[v], jnp.minimum(near[v], near[v + 2])), jump)
        for v in range(PARTS)
    ]
    return fresh, least


def walk(slots, out, leasts, count, state, charges, at):
    sub = lax.broadcasted_iota(jnp.int32, (SUB, SUB), 0)
    first_sub, last_sub = sub == 0, sub == SUB - 1
    p1 = charges[0].astype(jnp.float32) / 64.0
    p2 = charges[1].astype(jnp.float32) / 64.0

    def body(turn, carry):
        state, least = list(carry[0]), carry[1]
        for k in range(8):
            t = at(turn * 8 + k)
            state, least = step_once(state, pieces_of(slots[t]), p1, p2, first_sub, last_sub)
            leasts[t] = least
            for v in range(PARTS):
                out[t, v * SUB : (v + 1) * SUB, :] = state[v]
        return tuple(state), least

    start = (tuple(state), jnp.zeros((SUB, SUB), jnp.float32))
    return lax.fori_loop(0, count // 8, body, start)


def layer(walked, leasts, t):
    least = leasts[t]
    return jnp.concatenate([piece - least for piece in pieces_of(walked[t])], axis=0).T


BLOCK = 16
OFFSETS = 2 * BLOCK + 1
TABLE = 5 * SUB + 2 * BLOCK


def row_paths(came, back, charges, way, order, costs, table, turned_table, states):
    tiles = came.shape[0]
    sub = lax.broadcasted_iota(jnp.int32, (SUB, DISPARITIES), 0)
    first_sub, last_sub = sub == 0, sub == SUB - 1
    p1 = charges[0].astype(jnp.float32) / 64.0
    p2 = charges[1].astype(jnp.float32) / 64.0
    middle = DISPARITIES

    def at(n):
        return jnp.where(way == 0, n, BLOCK - 1 - n)

    def take(pair, _):
        start = pl.multiple_of(pair * 2 * SUB, 2 * SUB)
        parts = [came[c, pl.ds(start, 2 * SUB), :].astype(jnp.float32) for c in range(tiles)]
        for half in range(2):
            rows = [part[half * SUB : (half + 1) * SUB] for part in parts]
            value = turned(jnp.concatenate(rows, axis=0), order)
            for v, piece in enumerate(pieces_of(value)):
                t = pair * 2 + half
                lower = jnp.where(first_sub, jnp.inf, pltpu.roll(piece, 1, 0))
                upper = jnp.where(last_sub, jnp.inf, pltpu.roll(piece, SUB - 1, 0))
                costs[t, v * SUB : (v + 1) * SUB, :] = lower
                costs[t, middle + v * SUB : middle + (v + 1) * SUB, :] = piece
                costs[t, 2 * middle + v * SUB : 2 * middle + (v + 1) * SUB, :] = upper
        return 0

    lax.fori_loop(0, BLOCK // 2, take, 0)

    def keep(index, v, value):
        table[index, pl.ds(pl.multiple_of(v * SUB, SUB), SUB), :] = value

    def no_jump(v, _):
        paths = {0: None}
        for n in range(BLOCK):
            t = at(n)
            fresh = {}
            for o in range(-n - 1, n + 2):
                near = [paths[q] for q in (o - 1, o + 1) if q in paths]
                start = pl.multiple_of((PARTS + v + o) * SUB, SUB)
                cost = costs[t, pl.ds(start, SUB), :]
                if n == 0:
                    fresh[o] = cost if o == 0 else cost + p1
                    continue
                best = near[0] if len(near) == 1 else jnp.minimum(near[0], near[1])
                best = best + p1
                if o in paths:
                    best = jnp.minimum(paths[o], best)
                fresh[o] = cost + best
            paths = fresh
            if n < BLOCK - 1:
                level = list(paths.values())
                while len(level) > 1:
                    rest = level[len(level) // 2 * 2 :]
                    level = [
                        jnp.minimum(level[2 * i], level[2 * i + 1]) for i in range(len(level) // 2)
                    ] + rest
                keep(5 * SUB + n + 1, v, level[0])
        for o in range(-BLOCK, BLOCK + 1):
            keep(BLOCK + o, v, paths[o])
        for index in range(OFFSETS, 5 * SUB):
            keep(index, v, jnp.full((SUB, DISPARITIES), jnp.inf, jnp.float32))
        keep(5 * SUB, v, jnp.zeros((SUB, DISPARITIES), jnp.float32))
        return 0

    lax.fori_loop(0, PARTS, no_jump, 0)

    def costs_of(n):
        t = at(n)
        return [costs[t, middle + v * SUB : middle + (v + 1) * SUB, :] for v in range(PARTS)]

    def jumped(first, _):
        def one(n, state):
            return tuple(step_once(list(state), costs_of(n), p1, p2, first_sub, last_sub)[0])

        state = lax.fori_loop(first + 1, BLOCK, one, tuple(costs_of(first)))
        for v in range(PARTS):
            table[5 * SUB + BLOCK + first, v * SUB : (v + 1) * SUB, :] = state[v] + p2
        return 0

    lax.fori_loop(0, BLOCK, jumped, 0)

    def turn(group, _):
        for k in range(4):
            turned_table[group * 4 + k] = table[group * 4 + k].T
        return 0

    lax.fori_loop(0, TABLE // 4, turn, 0)
    lane = lax.broadcasted_iota(jnp.int32, (SUB, DISPARITIES), 1)
    natural = (lane % PARTS) * SUB + lane // PARTS

    def sort(group, _):
        for k in range(8):
            for v in range(PARTS):
                piece = turned_table[group * 8 + k, v * SUB : (v + 1) * SUB, :]
                turned_table[group * 8 + k, v * SUB : (v + 1) * SUB, :] = jnp.take_along_axis(
                    piece, natural, axis=1
                )
        return 0

    lax.fori_loop(0, TABLE // 8, sort, 0)

    def apply(turn_of, state):
        for k in range(SUB):
            n = turn_of * SUB + k
            b = jnp.where(way == 0, n, DISPARITIES - 1 - n)
            states[pl.ds(b, 1), :] = state[:1]
            found = []
            for g in range(2):
                start = 5 * SUB + g * SUB
                least = jnp.min(
                    state + turned_table[start : start + SUB, b, :], axis=1, keepdims=True
                )
                start = start + BLOCK
                found.append(least + turned_table[start : start + SUB, b, :])
            for g in range(5):
                term = state + turned_table[g * SUB : (g + 1) * SUB, b, :]
                amount = (g * SUB - BLOCK) % DISPARITIES
                found.append(pltpu.roll(term, amount, 1, stride=1, stride_axis=0))
            found = found[2:] + found[:2]
            while len(found) > 1:
                rest = found[len(found) // 2 * 2 :]
                found = [
                    jnp.minimum(found[2 * i], found[2 * i + 1]) for i in range(len(found) // 2)
                ] + rest
            state = found[0]
            for step in (4, 2, 1):
                state = jnp.minimum(state, pltpu.roll(state, step, 0))
        return state - jnp.min(state, axis=1, keepdims=True)

    lax.fori_loop(
        0, DISPARITIES // SUB, apply, jnp.zeros((SUB, DISPARITIES), jnp.float32)
    )
    before = states[...]
    before = before - jnp.min(before, axis=1, keepdims=True)
    high = before.astype(jnp.bfloat16)
    rest = before - high.astype(jnp.float32)
    state = pieces_of(turned(high, order) + turned(rest, order))

    def inside(pair, state):
        state = list(state)
        results = []
        for k in range(2):
            state, least = step_once(
                state, costs_of(pair * 2 + k), p1, p2, first_sub, last_sub
            )
            value = jnp.concatenate([piece - least for piece in state], axis=0).T
            results.append(ordered(value.astype(jnp.bfloat16), order))
        low = jnp.where(way == 0, results[0], results[1])
        top = jnp.where(way == 0, results[1], results[0])
        start = jnp.where(way == 0, pair, BLOCK // 2 - 1 - pair) * 2 * SUB
        start = pl.multiple_of(start, 2 * SUB)
        for c in range(tiles):
            rows = slice(c * SUB, (c + 1) * SUB)
            back[c, pl.ds(start, 2 * SUB), :] = jnp.concatenate(
                [low[rows], top[rows]], axis=0
            ).astype(jnp.bfloat16)
        return tuple(state)

    lax.fori_loop(0, BLOCK // 2, inside, tuple(state))


def half_turn(value):
    return pltpu.roll(value, SUB // 2, 0)


def paths_kernel(
    row_size,
    col_size,
    cost,
    charges,
    out,
    strips,
    strip_leasts,
    costs,
    table,
    turned_table,
    states,
    row_sent,
    row_came,
    row_back,
    swapped,
    summed,
    row_return,
    sent,
    came,
    back_out,
    back_in,
    row_send,
    row_recv,
    pass_send,
    pass_recv,
    swap_send,
    swap_recv,
    return_send,
    return_recv,
    sent_sem,
    came_sem,
    back_send,
    back_recv,
):
    rows = cost.shape[0]
    height = strips.shape[0]
    row = lax.axis_index("row")
    me = lax.axis_index("col")
    low = lax.broadcasted_iota(jnp.int32, (SUB, DISPARITIES), 0) < SUB // 2
    order = order_matrix()

    barrier = pltpu.get_barrier_semaphore()
    for axis, mine, size in (("row", row, row_size), ("col", me, col_size)):

        def greet(j, _, axis=axis, mine=mine, size=size):
            peer = lax.rem(mine + j, size)
            pl.semaphore_signal(barrier, inc=1, device_id={axis: peer}, device_id_type=MESH)
            return 0

        lax.fori_loop(1, size, greet, 0)

    core = lax.rem(me, 2)
    pair, pairs = me // 2, col_size // 2
    partner = me + 1 - 2 * core

    def remote(source, target, send_sem, recv_sem, axis, peer):
        return pltpu.make_async_remote_copy(
            src_ref=source,
            dst_ref=target,
            send_sem=send_sem,
            recv_sem=recv_sem,
            device_id={axis: peer},
            device_id_type=MESH,
        )

    def rows_out(there, slot):
        peer = 2 * there + core
        return remote(
            row_sent.at[there],
            row_came.at[2 * slot + core],
            row_send.at[there],
            row_recv.at[slot],
            "col",
            peer,
        )

    def rows_pass(h, side):
        block = row_came.at[2 * h + side]
        return remote(block, block, pass_send.at[h], pass_recv.at[h], "col", partner)

    def rows_swap(h):
        source = row_back.at[2 * h + 1 - core]
        return remote(source, swapped.at[h], swap_send.at[h], swap_recv.at[h], "col", partner)

    def rows_back(there, slot):
        return remote(
            summed.at[there],
            row_return.at[slot],
            return_send.at[there],
            return_recv.at[slot],
            "col",
            2 * there + core,
        )

    def strips_out(there, slot):
        return remote(
            sent.at[there], came.at[slot], sent_sem.at[there], came_sem.at[slot], "row", there
        )

    def strips_back(there, slot):
        return remote(
            back_out.at[there],
            back_in.at[slot],
            back_send.at[there],
            back_recv.at[slot],
            "row",
            there,
        )

    def each_peer(mine, size, work):
        def body(j, _):
            work(lax.rem(mine + j, size))
            return 0

        lax.fori_loop(1, size, body, 0)

    def each(size, work):
        def body(j, _):
            work(j)
            return 0

        lax.fori_loop(0, size, body, 0)

    def group(y, _):
        row_sent[y] = ordered(order, cost[y].astype(jnp.bfloat16)).astype(jnp.bfloat16)
        return 0

    lax.fori_loop(0, rows, group, 0)

    def cut(tile, _):
        start = pl.multiple_of(tile * SUB, SUB)
        rows = [cost[y, pl.ds(start, SUB), :] for y in range(SUB)]
        even = [jnp.where(low, rows[y], half_turn(rows[y + 1])) for y in range(0, SUB, 2)]
        odd = [jnp.where(low, half_turn(rows[y]), rows[y + 1]) for y in range(0, SUB, 2)]
        sent[2 * tile] = jnp.concatenate(even, axis=0).astype(jnp.bfloat16)
        sent[2 * tile + 1] = jnp.concatenate(odd, axis=0).astype(jnp.bfloat16)
        return 0

    pl.semaphore_wait(barrier, row_size + col_size - 2)
    each_peer(pair, pairs, lambda there: rows_out(there, pair).start())
    row_came[me] = row_sent[pair]

    def vertical_in():
        each_peer(row, row_size, lambda there: strips_out(there, there).wait_recv())

        def body(turn, _):
            for k in range(2):
                source = turn * 2 + k
                near = came[source].astype(jnp.float32)
                far = came[row_size - 1 - source].astype(jnp.float32)
                for q in range(SUB // 2):
                    a = near[q * SUB : (q + 1) * SUB]
                    b = far[(3 - q) * SUB : (4 - q) * SUB]
                    first = jnp.where(low, a, b)
                    second = half_turn(jnp.where(low, b, a))
                    t = source * SUB + 2 * q
                    strips[t] = turned(first, order)
                    strips[t + 1] = turned(second, order)
            return 0

        lax.fori_loop(0, row_size // 2, body, 0)

    def vertical_walk():
        zero = [jnp.zeros((SUB, SUB), jnp.float32) for _ in range(PARTS)]
        walk(strips, strips, strip_leasts, height, zero, charges, lambda t: t)

    def vertical_out():
        def send(near):
            for there in (near, row_size - 1 - near):

                @pl.when(there != row)
                def _(there=there):
                    strips_back(there, row).start()

        def body(near, _):
            pl.when(near > 0)(lambda: send(near - 1))
            far = row_size - 1 - near
            one = [layer(strips, strip_leasts, near * SUB + y) for y in range(SUB)]
            other = [layer(strips, strip_leasts, far * SUB + y) for y in range(SUB)]
            total = [one[y] + half_turn(other[SUB - 1 - y]) for y in range(SUB)]
            up = [jnp.where(low, total[y], half_turn(total[y + 1])) for y in (0, 2, 4, 6)]
            down = [jnp.where(low, half_turn(total[y + 1]), total[y]) for y in (6, 4, 2, 0)]
            both = jnp.concatenate(up + down, axis=0).astype(jnp.bfloat16)
            both = ordered(both, order).astype(jnp.bfloat16)
            half = SUB * SUB // 2
            back_out[near] = both[:half]
            back_out[far] = both[half:]
            return 0

        lax.fori_loop(0, row_size // 2, body, 0)
        send(row_size // 2 - 1)
        back_in[row] = back_out[row]

    rows_pass(pair, core).start()
    lax.fori_loop(0, row_size // 2, cut, 0)

    def forward(j, _):
        there = lax.rem(pair + pairs - j, pairs)
        rows_out(there, there).wait_recv()
        rows_pass(there, core).start()
        return 0

    lax.fori_loop(1, pairs, forward, 0)
    each_peer(row, row_size, lambda there: strips_out(there, row).start())
    came[row] = sent[row]
    each(pairs, lambda h: rows_pass(h, 1 - core).wait_recv())
    row_paths(row_came, row_back, charges, core, order, costs, table, turned_table, states)
    each(pairs, lambda h: rows_swap(h).start())
    vertical_in()

    def add(h):
        rows_swap(h).wait_recv()
        mine = row_back[2 * h + core].astype(jnp.float32)
        summed[h] = (mine + swapped[h].astype(jnp.float32)).astype(jnp.bfloat16)

    each(pairs, add)
    each_peer(pair, pairs, lambda there: rows_back(there, pair).start())
    row_return[pair] = summed[pair]
    vertical_walk()
    vertical_out()
    each_peer(pair, pairs, lambda there: rows_back(there, there).wait_recv())
    place = lax.broadcasted_iota(jnp.int32, (DISPARITIES, DISPARITIES), 0)
    lane = lax.broadcasted_iota(jnp.int32, (DISPARITIES, DISPARITIES), 1)
    spread = place == (lane % SUB) * PARTS + lane // SUB
    spread = jnp.where(spread, 1.0, 0.0).astype(jnp.bfloat16)

    def gather(y, _):
        out[y] = ordered(spread, row_return[y])
        return 0

    lax.fori_loop(0, rows, gather, 0)
    each_peer(row, row_size, lambda there: strips_back(there, there).wait_recv())

    def hand_over(tile, _):
        start = pl.multiple_of(tile * SUB, SUB)
        near = back_in[2 * tile].astype(jnp.float32)
        far = back_in[2 * tile + 1].astype(jnp.float32)
        for y in range(0, SUB, 2):
            a = near[y // 2 * SUB : (y // 2 + 1) * SUB]
            b = far[y // 2 * SUB : (y // 2 + 1) * SUB]
            here = pl.ds(start, SUB)
            out[y, here, :] = out[y, here, :] + jnp.where(low, a, half_turn(b))
            out[y + 1, here, :] = out[y + 1, here, :] + jnp.where(low, half_turn(a), b)
        return 0

    lax.fori_loop(0, row_size // 2, hand_over, 0)
    each_peer(pair, pairs, lambda there: rows_out(there, pair).wait_send())
    each(pairs, lambda h: rows_pass(h, core).wait_send())
    each(pairs, lambda h: rows_swap(h).wait_send())
    each_peer(pair, pairs, lambda there: rows_back(there, pair).wait_send())
    each_peer(row, row_size, lambda there: strips_out(there, row).wait_send())
    each_peer(row, row_size, lambda there: strips_back(there, row).wait_send())


def paths_call(cost, charges):
    rows, count, _ = cost.shape
    row_size, col_size = lax.axis_size("row"), lax.axis_size("col")
    width = count // row_size
    block = (row_size, rows * width, DISPARITIES)
    vmem = pl.BlockSpec(memory_space=pltpu.VMEM)
    return pl.pallas_call(
        functools.partial(paths_kernel, row_size, col_size),
        out_shape=jax.ShapeDtypeStruct(cost.shape, jnp.float32),
        in_specs=[vmem, pl.BlockSpec(memory_space=pltpu.SMEM)],
        out_specs=vmem,
        scratch_shapes=[
            pltpu.VMEM((rows * row_size, DISPARITIES, SUB), jnp.float32),
            pltpu.VMEM((rows * row_size, SUB, SUB), jnp.float32),
            pltpu.VMEM((BLOCK, 3 * DISPARITIES, DISPARITIES), jnp.float32),
            pltpu.VMEM((TABLE, DISPARITIES, DISPARITIES), jnp.float32),
            pltpu.VMEM((TABLE, DISPARITIES, DISPARITIES), jnp.float32),
            pltpu.VMEM((DISPARITIES, DISPARITIES), jnp.float32),
            pltpu.VMEM((rows, count, DISPARITIES), jnp.bfloat16),
            pltpu.VMEM((col_size, count, DISPARITIES), jnp.bfloat16),
            pltpu.VMEM((col_size, count, DISPARITIES), jnp.bfloat16),
            pltpu.VMEM((rows, count, DISPARITIES), jnp.bfloat16),
            pltpu.VMEM((rows, count, DISPARITIES), jnp.bfloat16),
            pltpu.VMEM((rows, count, DISPARITIES), jnp.bfloat16),
            pltpu.VMEM(block, jnp.bfloat16),
            pltpu.VMEM(block, jnp.bfloat16),
            pltpu.VMEM(block, jnp.bfloat16),
            pltpu.VMEM(block, jnp.bfloat16),
            pltpu.SemaphoreType.DMA((rows,)),
            pltpu.SemaphoreType.DMA((rows,)),
            pltpu.SemaphoreType.DMA((rows,)),
            pltpu.SemaphoreType.DMA((rows,)),
            pltpu.SemaphoreType.DMA((rows,)),
            pltpu.SemaphoreType.DMA((rows,)),
            pltpu.SemaphoreType.DMA((rows,)),
            pltpu.SemaphoreType.DMA((rows,)),
            pltpu.SemaphoreType.DMA((row_size,)),
            pltpu.SemaphoreType.DMA((row_size,)),
            pltpu.SemaphoreType.DMA((row_size,)),
            pltpu.SemaphoreType.DMA((row_size,)),
        ],
        compiler_params=pltpu.CompilerParams(
            collective_id=0, has_side_effects=True, vmem_limit_bytes=60 * 1024 * 1024
        ),
        name="four_paths",
    )(cost, charges)


def outer_kernel_sizes(images, halo):
    rows, channels, count = images.shape[1:]
    return rows, channels, count, rows + 2 * halo


def cost_kernel(
    row_size,
    col_size,
    layers_total,
    images,
    taps,
    biases,
    present,
    shift,
    cost,
    stacked_taps,
    above,
    below,
    packed,
    from_left,
    from_right,
    stack_a,
    stack_b,
    left_unit,
    reach_unit,
    rows_send,
    rows_recv,
    cols_send,
    cols_recv,
    unit_send,
    unit_recv,
):
    rows, channels, count, tall = outer_kernel_sizes(images, layers_total)
    far = reach_unit.shape[0] - 1
    deep = 3 * channels
    row, me = lax.axis_index("row"), lax.axis_index("col")
    has_up, has_down = row > 0, row < row_size - 1
    has_left, has_right = me > 0, me < col_size - 1

    barrier = pltpu.get_barrier_semaphore()
    expected = jnp.where(has_up, 1, 0) + jnp.where(has_down, 1, 0)
    for there, step in ((has_up, -1), (has_down, 1)):

        @pl.when(there)
        def _(step=step):
            pl.semaphore_signal(barrier, inc=1, device_id={"row": row + step}, device_id_type=MESH)

    for distance in range(1, far + 1):
        for there, step in ((me >= distance, -distance), (me + distance < col_size, distance)):
            expected = expected + jnp.where(there, 1, 0)

            @pl.when(there)
            def _(step=step):
                pl.semaphore_signal(
                    barrier, inc=1, device_id={"col": me + step}, device_id_type=MESH
                )

    pl.semaphore_wait(barrier, expected)

    def row_copy(step):
        index = 0 if step < 0 else 1
        first = 0 if step < 0 else rows - layers_total
        return pltpu.make_async_remote_copy(
            src_ref=images.at[:, first : first + layers_total],
            dst_ref=below if step < 0 else above,
            send_sem=rows_send.at[index],
            recv_sem=rows_recv.at[index],
            device_id={"row": row + step},
            device_id_type=MESH,
        )

    def col_copy(step):
        index = 0 if step < 0 else 1
        return pltpu.make_async_remote_copy(
            src_ref=packed,
            dst_ref=from_right if step < 0 else from_left,
            send_sem=cols_send.at[index],
            recv_sem=cols_recv.at[index],
            device_id={"col": me + step},
            device_id_type=MESH,
        )

    def unit_copy(distance):
        return pltpu.make_async_remote_copy(
            src_ref=reach_unit.at[0],
            dst_ref=reach_unit.at[distance],
            send_sem=unit_send.at[distance],
            recv_sem=unit_recv.at[distance],
            device_id={"col": me + distance},
            device_id_type=MESH,
        )

    pl.when(has_up)(lambda: row_copy(-1).start())
    pl.when(has_down)(lambda: row_copy(1).start())

    @pl.when(jnp.logical_not(has_up))
    def _():
        above[...] = jnp.zeros_like(above)

    @pl.when(jnp.logical_not(has_down))
    def _():
        below[...] = jnp.zeros_like(below)

    for layer_number in range(layers_total):
        for a in range(3):
            for b in range(3):
                first = (3 * a + b) * channels
                stacked_taps[layer_number, :, first : first + channels] = taps[layer_number, a, b]

    pl.when(has_down)(lambda: row_copy(-1).wait_recv())
    pl.when(has_up)(lambda: row_copy(1).wait_recv())

    def row_of(image, k):
        if k < layers_total:
            return above[image, k]
        if k < layers_total + rows:
            return images[image, k - layers_total]
        return below[image, k - layers_total - rows]

    pick_row = lax.broadcasted_iota(jnp.int32, (count, count), 0)
    pick_lane = lax.broadcasted_iota(jnp.int32, (count, count), 1)

    def one_hot(where):
        return jnp.where(where, 1.0, 0.0).astype(jnp.bfloat16)

    for image in range(2):
        total = None
        for k in range(tall):
            slot = pick_lane - k * SUB
            head = jnp.logical_and(slot >= 0, jnp.logical_and(slot < 3, pick_row == slot))
            tail = jnp.logical_and(
                slot >= 3, jnp.logical_and(slot < 6, pick_row == slot + count - 6)
            )
            pick = one_hot(jnp.logical_or(head, tail))
            term = jnp.dot(row_of(image, k), pick, preferred_element_type=jnp.float32)
            total = term if total is None else total + term
        packed[image] = total.astype(jnp.bfloat16)

    pl.when(has_left)(lambda: col_copy(-1).start())
    pl.when(has_right)(lambda: col_copy(1).start())

    @pl.when(jnp.logical_not(has_left))
    def _():
        from_left[...] = jnp.zeros_like(from_left)

    @pl.when(jnp.logical_not(has_right))
    def _():
        from_right[...] = jnp.zeros_like(from_right)

    for distance in range(1, far + 1):

        @pl.when(me < distance)
        def _(distance=distance):
            reach_unit[distance] = jnp.zeros(reach_unit.shape[1:], reach_unit.dtype)

    pl.when(has_right)(lambda: col_copy(-1).wait_recv())
    pl.when(has_left)(lambda: col_copy(1).wait_recv())

    lanes = lax.broadcasted_iota(jnp.int32, (channels, 2 * count), 1)
    side = jnp.where(lanes < count + count // 2, has_right.astype(jnp.int32), has_left.astype(jnp.int32))
    keep_lane = jnp.where(lanes < count, 1, side)

    eye = lax.broadcasted_iota(jnp.int32, (channels, channels), 0)
    eye = eye == lax.broadcasted_iota(jnp.int32, (channels, channels), 1)

    def put(stack, k, value):
        base = k * deep if isinstance(k, int) else pl.multiple_of(k * deep, deep)
        for b, turn in enumerate((1, 0, 2 * count - 1)):
            moved = pltpu.roll(value, turn, 1) if turn else value
            stack[pl.ds(base + b * channels, channels), :] = moved.astype(jnp.bfloat16)

    def features(image):
        for k in range(tall):
            slot_left = pick_row - k * SUB - 3 == pick_lane - (count - 3)
            slot_left = jnp.logical_and(slot_left, pick_lane >= count - 3)
            slot_right = jnp.logical_and(pick_row - k * SUB == pick_lane, pick_lane < 3)
            edge = jnp.dot(
                from_left[image], one_hot(slot_left), preferred_element_type=jnp.float32
            ) + jnp.dot(
                from_right[image], one_hot(slot_right), preferred_element_type=jnp.float32
            )
            put(
                stack_a,
                k,
                jnp.concatenate([row_of(image, k).astype(jnp.float32), edge], axis=1),
            )
        source, target = stack_a, stack_b
        for layer_number in range(layers_total):
            margin = layers_total - 1 - layer_number
            bias = jnp.broadcast_to(biases[layer_number : layer_number + 1, :], eye.shape)
            bias = jnp.sum(jnp.where(eye, bias, 0.0), axis=1, keepdims=True)
            weights = stacked_taps[layer_number]
            last = margin == 0

            def body(pair, _):
                for k in range(2):
                    y = pair * 2 + k
                    window = source[pl.ds(pl.multiple_of(y * deep, deep), 3 * deep), :]
                    if last:
                        window = window[:, :count]
                    value = jnp.dot(weights, window, preferred_element_type=jnp.float32) + bias
                    if last:
                        square = jnp.sum(value * value, axis=0, keepdims=True)
                        unit = (value * lax.rsqrt(square + 1e-06)).astype(jnp.bfloat16)
                        start = pl.multiple_of(y * channels, channels)
                        if image == 1:
                            reach_unit[0, pl.ds(start, channels), :] = unit
                        else:
                            left_unit[pl.ds(start, channels), :] = unit
                    else:
                        keep = jnp.logical_and(
                            jnp.logical_or(y >= margin, has_up),
                            jnp.logical_or(y < margin + rows, has_down),
                        )
                        value = jnp.where(
                            keep_lane * keep.astype(jnp.int32) == 1, jnp.maximum(value, 0.0), 0.0
                        )
                        put(target, y, value)
                return 0

            lax.fori_loop(0, (rows + 2 * margin) // 2, body, 0)
            source, target = target, source

    features(1)
    for distance in range(1, far + 1):
        pl.when(me + distance < col_size)(lambda distance=distance: unit_copy(distance).start())
    features(0)
    for distance in range(1, far + 1):
        pl.when(me >= distance)(lambda distance=distance: unit_copy(distance).wait_recv())

    wide = (far + 1) * count
    place = lax.broadcasted_iota(jnp.int32, (wide, 2 * count), 0)
    lane = lax.broadcasted_iota(jnp.int32, (wide, 2 * count), 1)
    choose = one_hot(place + lane == wide - 1 - shift[0, 0])

    def match(y, _):
        start = pl.multiple_of(y * channels, channels)
        reach = jnp.concatenate(
            [reach_unit[distance, pl.ds(start, channels), :] for distance in range(far, -1, -1)],
            axis=1,
        )
        strip = jnp.dot(reach, choose, preferred_element_type=jnp.float32).astype(jnp.bfloat16)
        held = present[pl.ds(y, 1), :] == 1
        left = left_unit[pl.ds(start, channels), :].astype(jnp.float32)
        left = jnp.where(held, left, 0.0).astype(jnp.bfloat16)
        product = lax.dot_general(
            left, strip, (((0,), (0,)), ((), ())), preferred_element_type=jnp.float32
        )
        skewed = pltpu.roll(product, count + 1, 1, stride=1, stride_axis=0)
        cost[y] = 1.0 - skewed[:, :DISPARITIES]
        return 0

    lax.fori_loop(0, rows, match, 0)

    pl.when(has_up)(lambda: row_copy(-1).wait_send())
    pl.when(has_down)(lambda: row_copy(1).wait_send())
    pl.when(has_left)(lambda: col_copy(-1).wait_send())
    pl.when(has_right)(lambda: col_copy(1).wait_send())
    for distance in range(1, far + 1):
        pl.when(me + distance < col_size)(lambda distance=distance: unit_copy(distance).wait_send())


def cost_call(images, taps, biases, present, shift):
    rows, channels, count = images.shape[1:]
    layers_total = taps.shape[0]
    tall = rows + 2 * layers_total
    far = (3 * count + DISPARITIES - 2) // count
    vmem = pl.BlockSpec(memory_space=pltpu.VMEM)
    halo = pltpu.VMEM((2, layers_total, channels, count), jnp.bfloat16)
    edge = pltpu.VMEM((2, channels, count), jnp.bfloat16)
    stack = pltpu.VMEM((tall * 3 * channels, 2 * count), jnp.bfloat16)
    return pl.pallas_call(
        functools.partial(
            cost_kernel, lax.axis_size("row"), lax.axis_size("col"), layers_total
        ),
        out_shape=jax.ShapeDtypeStruct((rows, count, DISPARITIES), jnp.float32),
        in_specs=[vmem, vmem, vmem, vmem, pl.BlockSpec(memory_space=pltpu.SMEM)],
        out_specs=vmem,
        scratch_shapes=[
            pltpu.VMEM((layers_total, channels, 9 * channels), jnp.bfloat16),
            halo,
            halo,
            edge,
            edge,
            edge,
            stack,
            stack,
            pltpu.VMEM((rows * channels, count), jnp.bfloat16),
            pltpu.VMEM((far + 1, rows * channels, count), jnp.bfloat16),
            pltpu.SemaphoreType.DMA((2,)),
            pltpu.SemaphoreType.DMA((2,)),
            pltpu.SemaphoreType.DMA((2,)),
            pltpu.SemaphoreType.DMA((2,)),
            pltpu.SemaphoreType.DMA((far + 1,)),
            pltpu.SemaphoreType.DMA((far + 1,)),
        ],
        compiler_params=pltpu.CompilerParams(
            collective_id=1, has_side_effects=True, vmem_limit_bytes=60 * 1024 * 1024
        ),
        name="matching_cost",
    )(images, taps, biases, present, shift)


def per_device(
    stereo_neuron_outputs,
    filter_tap_coefficients,
    filter_stack_intercepts,
    reference_picture_present,
    tile_shift_amounts,
    smoothness_charges,
):
    cost = cost_call(
        stereo_neuron_outputs,
        filter_tap_coefficients,
        filter_stack_intercepts,
        reference_picture_present,
        tile_shift_amounts,
    )
    return paths_call(cost, smoothness_charges)


def solution(mesh):
    return jax.shard_map(
        per_device,
        mesh=mesh,
        in_specs=(P(None, "row", None, "col"), P(), P(), P("row", "col"), P("row", "col"), P()),
        out_specs=P("row", "col", None),
        check_vma=False,
    )
```
